768 devices in a mesh: sect: 3 (over z_hi), lon: 32 (over x, z_lo, core), lat: 8 (over y).
Axes of the slice: x: 4, y: 8, z: 12 (z_hi: 3, z_lo: 4; z = z_hi * 4 + z_lo), core: 2. Of those that a mesh axis runs over, the one named last changes fastest.
Arguments:
- fields: float32 [3, 6, 16, 64, 4096], P('sect', None, None, 'lat', 'lon'), may hold values from -3 to 3, as said below
- levels: int32 [64, 4096], P('lat', 'lon'), may hold values from 0 to 16, as said below
Outputs:
- new_fields: float32 [3, 6, 16, 64, 4096], P('sect', None, None, 'lat', 'lon')
The draws below stay inside these ranges and needn't reach their ends.
Inputs may be any that keep to these rules, and one draw needn't show every extreme that they name: `fields`: section 0: velocities of magnitude below 0.95, temperature and salinity, lateral viscosity between 0.02 and 0.2, background diffusivity between 0.05 and 2. Later sections: tracers. In each device's block of 8 x 128 columns at most 768 columns have levels above 0, and some block has exactly 768; the value 16 occurs in every draw.
All inputs are finite; a program needn't handle non-finite values.
Results may differ from the reference program's by a relative error of at most 0.00002.
Values sent between devices are 32-bit elements; how exact they have to be, the bound alone decides.
A program may use at most 32 MiB of HBM per device.

```python
import math
import jax
import jax.numpy as jnp
from jax import lax

CLON = 128
CLAT = 8
LEV = 16
NSUB = 2
NF = 6
NLON = 4096
NLAT = 64
WET_DEV = 768
N_SECT = 3
N_LON = 32
N_LAT = 8


def draw_fields(key, part):
    keys = jax.random.split(key, 8)
    shape = (LEV, NLAT, NLON)
    zonal_vel = jax.random.uniform(keys[0], shape, jnp.float32, -0.8, 0.8)
    merid_vel = jax.random.uniform(keys[1], shape, jnp.float32, -0.8, 0.8)
    temper = jnp.clip(jax.random.normal(keys[3], shape, jnp.float32), -3.0, 3.0)
    saline = jnp.clip(jax.random.normal(keys[4], shape, jnp.float32), -3.0, 3.0)
    viscosity = jnp.exp(jax.random.uniform(keys[5], shape, jnp.float32, math.log(0.02), math.log(0.2)))
    background = jnp.exp(jax.random.uniform(keys[6], shape, jnp.float32, math.log(0.05), math.log(2.0)))
    dyn_slot = jnp.stack([zonal_vel, merid_vel, temper, saline, viscosity, background])
    tracer_shape = (N_SECT - 1, NF, LEV, NLAT, NLON)
    tracers = jax.random.uniform(keys[7], tracer_shape, jnp.float32, 0.5, 2.0)
    return jnp.concatenate([dyn_slot[None], tracers], axis=0).astype(jnp.float32)


def draw_levels(key, part):
    key_first, key_second, key_forced, key_ranks, key_depth = jax.random.split(key, 5)
    blocks = N_LAT * N_LON
    block_cols = CLAT * CLON
    first = jax.random.randint(key_first, (blocks,), 0, WET_DEV + 1)
    second = jax.random.randint(key_second, (blocks,), 0, WET_DEV + 1)
    forced_id = jax.random.randint(key_forced, (), 0, blocks)
    block_ids = jnp.arange(blocks, dtype=jnp.int32)
    counts_wet = jnp.where(block_ids == forced_id, WET_DEV, jnp.minimum(first, second))

    def shuffled(sub_key):
        return jax.random.permutation(sub_key, block_cols)
    ranks = jax.vmap(shuffled)(jax.random.split(key_ranks, blocks)).astype(jnp.int32)
    depth = jax.random.randint(key_depth, (blocks, block_cols), 1, LEV + 1)
    deep_mark = (ranks == 0) & (block_ids == forced_id)[:, None]
    depth = jnp.where(deep_mark, LEV, depth)
    levels_flat = jnp.where(ranks < counts_wet[:, None], depth, 0)
    levels_grid = levels_flat.reshape(N_LAT, N_LON, CLAT, CLON).transpose(0, 2, 1, 3)
    return levels_grid.reshape(NLAT, NLON).astype(jnp.int32)


def shard_levels(key, extent, cuts, smallest, high):
    def one(dim, shards_of):
        heights = jax.random.uniform(jax.random.fold_in(jax.random.fold_in(key, 6), dim), (shards_of,), jnp.float32, smallest / len(cuts), high / len(cuts))
        return jnp.repeat(jnp.exp(heights), extent[dim] // shards_of).reshape((-1,) + (1,) * (len(extent) - dim - 1))

    factor_of = one(*cuts[0])
    for cut in cuts[1:]:
        factor_of = factor_of * one(*cut)
    return factor_of


def setup_inputs(seed: int = 0) -> dict:
    splits = jax.random.split(jax.random.key(seed), 3)
    fields = draw_fields(jax.random.fold_in(splits[2], 71), 0)
    levels = draw_levels(jax.random.fold_in(splits[2], 71), 0)
    return {"fields": fields, "levels": levels}


TIME_STEP = 1.0
CORIOLIS = 0.3
THERMAL = 0.2
HALINE = 0.15
GRAVITY_SCALE = 0.05
MIX_BOOST = 4.0
RICHARDSON = 1.0


def centre(extended):
    return extended[..., 1:-1, 1:-1]


def to_east(extended):
    return extended[..., 1:-1, 2:]


def to_west(extended):
    return extended[..., 1:-1, :-2]


def to_north(extended):
    return extended[..., 2:, 1:-1]


def to_south(extended):
    return extended[..., :-2, 1:-1]


def extend(quantity, rim_width):
    spec = [(0, 0)] * (quantity.ndim - 2) + [(rim_width, rim_width), (0, 0)]
    padded = jnp.pad(quantity, spec)
    return jnp.concatenate([padded[..., -rim_width:], padded, padded[..., :rim_width]], axis=-1)


def physics(extended, background):
    zonal_vel, merid_vel, temper, saline, viscosity, wetness = extended
    wet_mid = centre(wetness)
    mask_east = wet_mid * to_east(wetness)
    mask_west = to_west(wetness) * wet_mid
    mask_north = wet_mid * to_north(wetness)
    mask_south = to_south(wetness) * wet_mid
    flow_east = centre(zonal_vel) * mask_east
    flow_west = to_west(zonal_vel) * mask_west
    flow_north = centre(merid_vel) * mask_north
    flow_south = to_south(merid_vel) * mask_south
    divergence = (flow_east - flow_west) + (flow_north - flow_south)
    column_sum = jnp.cumsum(divergence[::-1], axis=0)[::-1]
    vertical = jnp.concatenate([jnp.zeros_like(column_sum[:1]), -column_sum[1:]], axis=0)
    visc_mid = centre(viscosity)
    coef_east = 0.5 * (visc_mid + to_east(viscosity)) * mask_east
    coef_west = 0.5 * (to_west(viscosity) + visc_mid) * mask_west
    coef_north = 0.5 * (visc_mid + to_north(viscosity)) * mask_north
    coef_south = 0.5 * (to_south(viscosity) + visc_mid) * mask_south

    def diffuse(quantity):
        middle = centre(quantity)
        return (coef_east * (to_east(quantity) - middle) - coef_west * (middle - to_west(quantity))
                + coef_north * (to_north(quantity) - middle) - coef_south * (middle - to_south(quantity)))

    density = HALINE * saline - THERMAL * temper
    pressure = GRAVITY_SCALE * jnp.cumsum(density * wetness, axis=0)
    press_mid = centre(pressure)
    zonal_new = (centre(zonal_vel) + TIME_STEP * (diffuse(zonal_vel) + CORIOLIS * centre(merid_vel)
                 - (to_east(pressure) - press_mid))) * mask_east
    merid_new = (centre(merid_vel) + TIME_STEP * (diffuse(merid_vel) - CORIOLIS * centre(zonal_vel)
                 - (to_north(pressure) - press_mid))) * mask_north
    temper_new = centre(temper) + TIME_STEP * diffuse(temper)
    saline_new = centre(saline) + TIME_STEP * diffuse(saline)
    temp_jump = THERMAL * (temper_new[:-1] - temper_new[1:])
    mixing = background[1:] * (1.0 + MIX_BOOST / (1.0 + RICHARDSON * temp_jump * temp_jump)) * wet_mid[1:]
    diffusivity = jnp.concatenate([jnp.zeros_like(mixing[:1]), mixing], axis=0)
    return (zonal_new, merid_new, temper_new, saline_new, vertical, diffusivity), (flow_east, flow_north, vertical, diffusivity)


def advect(tracer_ext, east_ext, north_ext, step_size):
    east_mid = centre(east_ext)
    east_side = to_west(east_ext)
    north_mid = centre(north_ext)
    north_side = to_south(north_ext)
    middle = centre(tracer_ext)
    flux_east = jnp.maximum(east_mid, 0.0) * middle + jnp.minimum(east_mid, 0.0) * to_east(tracer_ext)
    flux_west = jnp.maximum(east_side, 0.0) * to_west(tracer_ext) + jnp.minimum(east_side, 0.0) * middle
    flux_north = jnp.maximum(north_mid, 0.0) * middle + jnp.minimum(north_mid, 0.0) * to_north(tracer_ext)
    flux_south = jnp.maximum(north_side, 0.0) * to_south(tracer_ext) + jnp.minimum(north_side, 0.0) * middle
    return middle - step_size * ((flux_east - flux_west) + (flux_north - flux_south))


def vertical_factor(vertical, diffusivity):
    up_part = jnp.maximum(vertical, 0.0) + diffusivity
    down_part = jnp.minimum(vertical, 0.0) - diffusivity
    zero_row = jnp.zeros_like(up_part[:1])
    up_next = jnp.concatenate([up_part[1:], zero_row], axis=0)
    down_next = jnp.concatenate([down_part[1:], zero_row], axis=0)
    lower_band = TIME_STEP * down_part
    diagonal = 1.0 + TIME_STEP * (up_part - down_next)
    upper_band = -TIME_STEP * up_next
    ratios = []
    inverses = []
    for index_k in range(vertical.shape[0]):
        pivot_value = diagonal[index_k]
        if index_k > 0:
            pivot_value = pivot_value - lower_band[index_k] * ratios[-1]
        inverse = 1.0 / pivot_value
        ratios.append(upper_band[index_k] * inverse)
        inverses.append(inverse)
    return lower_band, ratios, inverses


def thomas_solve(lower_band, ratios, inverses, rhs):
    level_count = rhs.shape[-2]
    forward = [rhs[..., 0, :] * inverses[0]]
    for index_k in range(1, level_count):
        forward.append((rhs[..., index_k, :] - lower_band[index_k] * forward[-1]) * inverses[index_k])
    result = [forward[-1]]
    for index_k in range(level_count - 2, -1, -1):
        result.append(forward[index_k] - ratios[index_k] * result[-1])
    return jnp.stack(result[::-1], axis=-2)


def reference(fields, levels):
    depth_ids = lax.broadcasted_iota(jnp.int32, (LEV, NLAT, NLON), 0)
    wetness = (depth_ids < levels[None]).astype(jnp.float32)
    dyn_slot = fields[0]
    extended = extend(jnp.concatenate([dyn_slot[:5], wetness[None]], axis=0), 1)
    outputs, flow_parts = physics(extended, dyn_slot[5])
    flow_east, flow_north, vertical, diffusivity = flow_parts
    east_ext = extend(flow_east, 1)
    north_ext = extend(flow_north, 1)
    all_cols = NLAT * NLON
    lower_band, ratios, inverses = vertical_factor(vertical.reshape(LEV, all_cols), diffusivity.reshape(LEV, all_cols))

    def one_tracer(tracer):
        current = tracer
        for substep in range(NSUB):
            current = advect(extend(current, 1), east_ext, north_ext, TIME_STEP / NSUB)
        settled = thomas_solve(lower_band, ratios, inverses, current.reshape(LEV, all_cols))
        return settled.reshape(LEV, NLAT, NLON) * wetness

    tracers = fields[1:].reshape((N_SECT - 1) * NF, LEV, NLAT, NLON)
    advanced = lax.map(one_tracer, tracers).reshape(N_SECT - 1, NF, LEV, NLAT, NLON)
    return jnp.concatenate([jnp.stack(outputs)[None], advanced], axis=0)
```

```python
import functools

import jax
import jax.numpy as jnp
from jax import lax
from jax.experimental import pallas as pl
from jax.experimental.pallas import tpu as pltpu
from jax.sharding import PartitionSpec as P

MESH = pl.DeviceIdType.MESH
F32 = jnp.float32
K = 16
NF = 6
NT = NF * K
SUB = 0.5
N_ROW = NT + 8

(R_COL_W, R_COL_E, R_NEAR_S, R_NEAR_N, R_FAR_S, R_FAR_N, R_CORNER_S, R_CORNER_N) = range(8)
N_HALO = 8
(Z_ZON, Z_MER, Z_ROW_S, Z_FAR_S, Z_ROW_N, Z_COL, Z_DIFF) = range(7)
N_Z = 7


def tile(t):
    return pl.ds(pl.multiple_of(t * 8, 8), 8)


def lroll(x, amount):
    return pltpu.roll(x, amount, 1)


def sroll(x, amount):
    return pltpu.roll(x, amount, 0)


def face(level, limit, speed):
    return jnp.where(level < limit, speed, 0.0)


def coefficients(fe, fw, fn, fs):
    ce = -SUB * jnp.minimum(fe, 0.0)
    cw = SUB * jnp.maximum(fw, 0.0)
    cn = -SUB * jnp.minimum(fn, 0.0)
    cs = SUB * jnp.maximum(fs, 0.0)
    out = (jnp.maximum(fe, 0.0) - jnp.minimum(fw, 0.0)) + (jnp.maximum(fn, 0.0) - jnp.minimum(fs, 0.0))
    return 1.0 - SUB * out, ce, cw, cn, cs


def combine(c, q, qe, qw, qn, qs):
    c0, ce, cw, cn, cs = c
    return (c0 * q + (ce * qe + cw * qw)) + (cn * qn + cs * qs)


def kernel(n_sect, n_lon, n_lat, x_hbm, lev_ref, out,
           x, cols, cols_w, cols_e, rows_out, rows, near, far, corner_s, corner_n,
           zm, flow_rows, flow_cols, flow_cols_out, diff, rhs, div, ratio, ring_cols, ring_rows,
           in_sem, send_sem, recv_sem, zsend_sem, zrecv_sem):
    sect = lax.axis_index("sect")
    lon = lax.axis_index("lon")
    lat = lax.axis_index("lat")
    east = lax.rem(lon + 1, n_lon)
    west = lax.rem(lon + n_lon - 1, n_lon)
    has_s = lat > 0
    has_n = lat < n_lat - 1

    barrier = pltpu.get_barrier_semaphore()
    for step in range(1, n_sect):
        pl.semaphore_signal(barrier, inc=1, device_id={"sect": lax.rem(sect + step, n_sect)}, device_id_type=MESH)
    for side in (east, west):
        pl.semaphore_signal(barrier, inc=1, device_id={"lon": side}, device_id_type=MESH)

    @pl.when(has_s)
    def _():
        pl.semaphore_signal(barrier, inc=1, device_id={"lat": lat - 1}, device_id_type=MESH)

    @pl.when(has_n)
    def _():
        pl.semaphore_signal(barrier, inc=1, device_id={"lat": lat + 1}, device_id_type=MESH)

    load = pltpu.make_async_copy(x_hbm, x, in_sem)
    load.start()

    lane = lax.broadcasted_iota(jnp.int32, (8, 128), 1)
    row = lax.broadcasted_iota(jnp.int32, (8, 128), 0)
    even = (lane & 1) == 0
    pair = 63 - (lane >> 1)
    pair_b = 63 - (jnp.where(even, (lane + 126) >> 1, (lane + 1) >> 1) & 63)
    first_lane, last_lane = lane == 0, lane == 127
    first_row, last_row = row == 0, row == 7
    lev = lev_ref[...].astype(F32)
    zero = jnp.zeros((8, 128), F32)

    def bcast(value):
        return jnp.broadcast_to(value, (8, 128))

    @pl.when(jnp.logical_not(has_s))
    def _():
        rows[0] = jnp.zeros((N_ROW, 128), F32)
        rows[2] = jnp.zeros((N_ROW, 128), F32)
        corner_s[...] = jnp.zeros((16, 128), F32)

    @pl.when(jnp.logical_not(has_n))
    def _():
        rows[1] = jnp.zeros((N_ROW, 128), F32)
        rows[3] = jnp.zeros((N_ROW, 128), F32)
        corner_n[...] = jnp.zeros((16, 128), F32)

    load.wait()

    def pack(acc, value, turn, p):
        a, b = acc
        turned = lroll(value, turn)
        return jnp.where(pair == p, turned, a), jnp.where(pair_b == p, turned, b)

    def pack_level(k, carry):
        a0, a1, b0, b1 = carry
        for f in range(NF):
            p = (f % 4) * K + k
            value = x[tile(f * K + k), :]
            if f < 4:
                a0, b0 = pack((a0, b0), value, 127 - 2 * p, p)
            else:
                a1, b1 = pack((a1, b1), value, 127 - 2 * p, p)
        return a0, a1, b0, b1

    a0, a1, b0, b1 = lax.fori_loop(0, K, pack_level, (zero,) * 4)
    a1, b1 = pack((a1, b1), lev, 63, 32)
    for i, value in enumerate((a0, a1, b0, b1)):
        cols[i * 8:i * 8 + 8, :] = value

    def pack_rows(u, carry):
        for i, r in enumerate((7, 0, 6, 1)):
            rows_out[i, tile(u), :] = x[pl.ds(u * 64 + r, 8, stride=8), :]
        return carry

    lax.fori_loop(0, NT // 8, pack_rows, 0)
    for i, r in enumerate((7, 0, 6, 1)):
        rows_out[i, NT:NT + 8, :] = bcast(lev[r:r + 1, :])

    pl.semaphore_wait(barrier, n_sect + 1 + has_s.astype(jnp.int32) + has_n.astype(jnp.int32))

    def remote(src, dst, send, recv, to):
        return pltpu.make_async_remote_copy(src_ref=src, dst_ref=dst, send_sem=send, recv_sem=recv, device_id=to,
                                            device_id_type=MESH)

    def halo(src, dst, slot, to):
        return remote(src, dst, send_sem.at[slot], recv_sem.at[slot], to)

    south, north = {"lat": lat - 1}, {"lat": lat + 1}
    from_w = halo(cols, cols_w, R_COL_W, {"lon": east})
    from_e = halo(cols, cols_e, R_COL_E, {"lon": west})
    near_s = halo(rows_out.at[0], rows.at[0], R_NEAR_S, north)
    near_n = halo(rows_out.at[1], rows.at[1], R_NEAR_N, south)
    far_s = halo(rows_out.at[2], rows.at[2], R_FAR_S, north)
    far_n = halo(rows_out.at[3], rows.at[3], R_FAR_N, south)
    edge_s = halo(near, corner_s, R_CORNER_S, north)
    edge_n = halo(near, corner_n, R_CORNER_N, south)

    def across(slot, peer):
        to = {"sect": peer}
        src, dst = (
            (x_hbm.at[0:K * 8], zm.at[0:K * 8]),
            (x_hbm.at[K * 8:2 * K * 8], zm.at[K * 8:2 * K * 8]),
            (rows.at[0, 0:2 * K], flow_rows.at[0:2 * K]),
            (rows.at[2, K:2 * K], flow_rows.at[2 * K:3 * K]),
            (rows.at[1, 0:2 * K], flow_rows.at[3 * K:5 * K]),
            (flow_cols_out, flow_cols),
            (diff, diff),
        )[slot]
        return remote(src, dst, zsend_sem.at[peer - 1, slot], zrecv_sem.at[slot], to)

    def to_tracers(*slots):
        for slot in slots:
            for peer in range(1, n_sect):
                across(slot, peer).start()

    from_w.start()
    from_e.start()

    @pl.when(has_n)
    def _():
        near_s.start()

    @pl.when(has_s)
    def _():
        near_n.start()

    @pl.when(sect == 0)
    def _():
        to_tracers(Z_ZON, Z_MER)

    @pl.when(has_n)
    def _():
        far_s.start()

    @pl.when(has_s)
    def _():
        far_n.start()

    from_w.wait_recv()
    from_e.wait_recv()
    for v in range(2):
        a, b = slice(v * 8, v * 8 + 8), slice(16 + v * 8, 24 + v * 8)
        near[a, :] = jnp.where(even, lroll(cols_e[a, :], 127), lroll(cols_w[a, :], 1))
        far[a, :] = jnp.where(even, lroll(cols_e[b, :], 126), lroll(cols_w[b, :], 2))

    @pl.when(has_n)
    def _():
        edge_s.start()

    @pl.when(has_s)
    def _():
        edge_n.start()

    @pl.when(has_s)
    def _():
        near_s.wait_recv()

    @pl.when(has_n)
    def _():
        near_n.wait_recv()

    def neighbours(q, f, k, columns, south_ref, north_ref):
        v = (f // 4) * 8
        p = (f % 4) * K + k
        side = lroll(columns[v:v + 8, :], 2 * p + 1)
        return (
            jnp.where(last_lane, side, lroll(q, 127)),
            jnp.where(first_lane, side, lroll(q, 1)),
            jnp.where(last_row, bcast(north_ref[pl.ds(f * K + k, 1), :]), sroll(q, 7)),
            jnp.where(first_row, bcast(south_ref[pl.ds(f * K + k, 1), :]), sroll(q, 1)),
        )

    side = lroll(near[8:16, :], 65)
    lev_e = jnp.where(last_lane, side, lroll(lev, 127))
    lev_w = jnp.where(first_lane, side, lroll(lev, 1))
    lev_n = jnp.where(last_row, rows[1, NT:NT + 8, :], sroll(lev, 7))
    lev_s = jnp.where(first_row, rows[0, NT:NT + 8, :], sroll(lev, 1))
    lim_e, lim_w = jnp.minimum(lev, lev_e), jnp.minimum(lev, lev_w)
    lim_n, lim_s = jnp.minimum(lev, lev_n), jnp.minimum(lev, lev_s)

    @pl.when(sect == 0)
    def _():
        def around(f, k):
            q = x[tile(f * K + k), :]
            return q, neighbours(q, f, k, near, rows.at[0], rows.at[1])

        def conductances(k, level):
            v, (ve, vw, vn, vs) = around(4, k)
            return (face(level, lim_e, 0.5 * (v + ve)), face(level, lim_w, 0.5 * (vw + v)),
                    face(level, lim_n, 0.5 * (v + vn)), face(level, lim_s, 0.5 * (vs + v)))

        def diffuse(c, q, sides):
            ce, cw, cn, cs = c
            qe, qw, qn, qs = sides
            return ce * (qe - q) - cw * (q - qw) + cn * (qn - q) - cs * (q - qs)

        def warm(k, above):
            level = lax.convert_element_type(k, F32)
            c = conductances(k, level)
            t, sides = around(2, k)
            new = t + diffuse(c, t, sides)
            out[tile(2 * K + k), :] = new
            jump = 0.2 * (above - new)
            wet = jnp.where((level < lev) & (k > 0), x[tile(5 * K + k), :], 0.0)
            mixing = wet * (1.0 + 4.0 / (1.0 + jump * jump))
            out[tile(5 * K + k), :] = mixing
            diff[tile(k), :] = mixing
            return new

        lax.fori_loop(0, K, warm, zero)

        @pl.when(has_s)
        def _():
            far_s.wait_recv()
            edge_s.wait_recv()

        @pl.when(has_n)
        def _():
            far_n.wait_recv()
            edge_n.wait_recv()

        for i, value in enumerate((cols[0:8, :], near[0:8, :], far[0:8, :], corner_s[0:8, :], corner_n[0:8, :])):
            flow_cols_out[i * 8:i * 8 + 8, :] = value
        to_tracers(Z_ROW_S, Z_FAR_S, Z_ROW_N, Z_COL, Z_DIFF)

        def move(k, sums):
            level = lax.convert_element_type(k, F32)
            c = conductances(k, level)
            z, zs = around(0, k)
            m, ms = around(1, k)
            t, ts = around(2, k)
            s, ss = around(3, k)
            out[tile(3 * K + k), :] = s + diffuse(c, s, ss)
            here, at_e, at_n = sums

            def add(total, limit, sal, tem):
                return total + jnp.where(level < limit, 0.15 * sal - 0.2 * tem, 0.0)

            here = add(here, lev, s, t)
            at_e = add(at_e, lev_e, ss[0], ts[0])
            at_n = add(at_n, lev_n, ss[2], ts[2])
            new_z = z + (diffuse(c, z, zs) + 0.3 * m - 0.05 * (at_e - here))
            new_m = m + (diffuse(c, m, ms) - 0.3 * z - 0.05 * (at_n - here))
            out[tile(k), :] = face(level, lim_e, new_z)
            out[tile(K + k), :] = face(level, lim_n, new_m)
            div[tile(k), :] = (face(level, lim_e, z) - face(level, lim_w, zs[1])) + (
                face(level, lim_n, m) - face(level, lim_s, ms[3]))
            return here, at_e, at_n

        lax.fori_loop(0, K, move, (zero,) * 3)

        def rise(i, total):
            k = K - 1 - i
            total = total + div[tile(k), :]
            out[tile(4 * K + k), :] = jnp.where(k > 0, -total, 0.0)
            return total

        lax.fori_loop(0, K, rise, zero)

    @pl.when(sect != 0)
    def _():
        @pl.when(has_s)
        def _():
            far_s.wait_recv()
            edge_s.wait_recv()

        @pl.when(has_n)
        def _():
            far_n.wait_recv()
            edge_n.wait_recv()

        for slot in (Z_ROW_S, Z_FAR_S, Z_ROW_N, Z_COL, Z_ZON, Z_MER):
            across(slot, 1).wait_recv()

        p1_lev = jnp.where(even, bcast(near[8:16, 62:63]), bcast(near[8:16, 63:64]))
        p2_lev = jnp.where(even, bcast(far[8:16, 62:63]), bcast(far[8:16, 63:64]))
        p0_lev = jnp.where(even, bcast(cols[8:16, 62:63]), bcast(cols[8:16, 63:64]))
        cs_lev = jnp.where(even, bcast(corner_s[8:16, 62:63]), bcast(corner_s[8:16, 63:64]))
        cn_lev = jnp.where(even, bcast(corner_n[8:16, 62:63]), bcast(corner_n[8:16, 63:64]))

        def up_one(value, beyond):
            return jnp.where(last_row, sroll(beyond, 7), sroll(value, 7))

        def down_one(value, beyond):
            return jnp.where(first_row, sroll(beyond, 1), sroll(value, 1))

        def repeat(value, offset):
            if offset:
                value = lroll(value, offset)
            value = jnp.where(lane >= 96, value, 0.0)
            value = value + lroll(value, 32)
            return value + lroll(value, 64)

        p0_z, p1_z, p2_z = (repeat(flow_cols[i * 8:i * 8 + 8, :], 0) for i in range(3))
        p1_m, cs_m, cn_m = (repeat(flow_cols[i * 8:i * 8 + 8, :], 32) for i in (1, 3, 4))
        k_lane = (pair & (K - 1)).astype(F32)
        lim = functools.partial(jnp.minimum, p1_lev)
        c = coefficients(
            face(k_lane, lim(jnp.where(even, p2_lev, p0_lev)), p1_z),
            face(k_lane, lim(jnp.where(even, p0_lev, p2_lev)), jnp.where(even, p0_z, p2_z)),
            face(k_lane, lim(up_one(p1_lev, cn_lev)), p1_m),
            face(k_lane, lim(down_one(p1_lev, cs_lev)), down_one(p1_m, cs_m)),
        )
        for v in range(2):
            a = slice(v * 8, v * 8 + 8)
            p0, p1, p2 = cols[a, :], near[a, :], far[a, :]
            ring_cols[a, :] = combine(c, p1, jnp.where(even, p2, p0), jnp.where(even, p0, p2),
                                      up_one(p1, corner_n[a, :]), down_one(p1, corner_s[a, :]))

        def corner_of(value, at, p):
            return pltpu.roll(bcast(value[at:at + 1, :]), 2 * p + 1, 1, stride=2, stride_axis=0)

        def turn(value, corner):
            return jnp.where(last_lane, corner, lroll(value, 127)), jnp.where(first_lane, corner, lroll(value, 1))

        for north_side in range(2):
            at = 0 if north_side else 7
            corner = corner_n if north_side else corner_s
            corner_z = flow_cols[32:40, :] if north_side else flow_cols[24:32, :]
            base = 3 * K if north_side else 0
            r_lev = rows[north_side, NT:NT + 8, :]
            r_in = rows_out[1 - north_side, NT:NT + 8, :]
            r_out = rows[2 + north_side, NT:NT + 8, :]
            r_e, r_w = turn(r_lev, lroll(bcast(corner[8 + at:9 + at, :]), 65))
            for octet in range(2):
                k_row = (row + 8 * octet).astype(F32)
                z = flow_rows[base + octet * 8:base + octet * 8 + 8, :]
                m = flow_rows[base + K + octet * 8:base + K + octet * 8 + 8, :]
                _, zw = turn(z, corner_of(corner_z, at, octet * 8))
                lim_in, lim_out = jnp.minimum(r_lev, r_in), jnp.minimum(r_lev, r_out)
                if north_side:
                    inner = zm[pl.ds(K * 8 + octet * 64 + 7, 8, stride=8), :]
                    fn, fs = face(k_row, lim_out, m), face(k_row, lim_in, inner)
                else:
                    outer = flow_rows[2 * K + octet * 8:2 * K + octet * 8 + 8, :]
                    fn, fs = face(k_row, lim_in, m), face(k_row, lim_out, outer)
                c = coefficients(face(k_row, jnp.minimum(r_lev, r_e), z), face(k_row, jnp.minimum(r_lev, r_w), zw), fn, fs)
                for f in range(NF):
                    v, p, u = f // 4, (f % 4) * K + octet * 8, (f * K + octet * 8)
                    a = slice(u, u + 8)
                    q, inner, outer = rows[north_side, a, :], rows_out[1 - north_side, a, :], rows[2 + north_side, a, :]
                    qe, qw = turn(q, corner_of(corner[v * 8:v * 8 + 8, :], at, p))
                    qn, qs = (outer, inner) if north_side else (inner, outer)
                    ring_rows[north_side, a, :] = combine(c, q, qe, qw, qn, qs)

        def advance(k, carry):
            level = lax.convert_element_type(k, F32)
            z, m = zm[tile(k), :], zm[tile(K + k), :]
            side = lroll(flow_cols[8:16, :], 2 * k + 1)
            zw = jnp.where(first_lane, side, lroll(z, 1))
            ms = jnp.where(first_row, bcast(flow_rows[pl.ds(K + k, 1), :]), sroll(m, 1))
            fe, fw, fn, fs = face(level, lim_e, z), face(level, lim_w, zw), face(level, lim_n, m), face(level, lim_s, ms)
            div[tile(k), :] = (fe - fw) + (fn - fs)
            c = coefficients(fe, fw, fn, fs)
            for f in range(NF):
                q = x[tile(f * K + k), :]
                q = combine(c, q, *neighbours(q, f, k, near, rows.at[0], rows.at[1]))
                q = combine(c, q, *neighbours(q, f, k, ring_cols, ring_rows.at[0], ring_rows.at[1]))
                rhs[tile(f * K + k), :] = q
            return carry

        lax.fori_loop(0, K, advance, 0)
        across(Z_DIFF, 1).wait_recv()

        def eliminate(i, carry):
            total, up_below, down_below, ratio_below, below = carry
            k = K - 1 - i
            total = total + div[tile(k), :]
            kappa = diff[tile(k), :]
            vertical = jnp.where(k > 0, -total, 0.0)
            up = jnp.maximum(vertical, 0.0) + kappa
            down = jnp.minimum(vertical, 0.0) - kappa
            inverse = 1.0 / ((1.0 + (up - down_below)) + up_below * ratio_below)
            here = down * inverse
            ratio[tile(k), :] = here
            values = []
            for f in range(NF):
                value = (rhs[tile(f * K + k), :] + up_below * below[f]) * inverse
                rhs[tile(f * K + k), :] = value
                values.append(value)
            return total, up, down, here, tuple(values)

        lax.fori_loop(0, K, eliminate, (zero,) * 4 + ((zero,) * NF,))

        def settle(k, above):
            level = lax.convert_element_type(k, F32)
            here = ratio[tile(k), :]
            values = []
            for f in range(NF):
                value = rhs[tile(f * K + k), :] - here * above[f]
                out[tile(f * K + k), :] = face(level, lev, value)
                values.append(value)
            return tuple(values)

        lax.fori_loop(0, K, settle, (zero,) * NF)

    from_w.wait_send()
    from_e.wait_send()

    @pl.when(has_n)
    def _():
        for copy in (near_s, far_s, edge_s):
            copy.wait_send()

    @pl.when(has_s)
    def _():
        for copy in (near_n, far_n, edge_n):
            copy.wait_send()

    @pl.when(sect == 0)
    def _():
        for slot in range(N_Z):
            for peer in range(1, n_sect):
                across(slot, peer).wait_send()


def solution(mesh):
    n_sect, n_lon, n_lat = (mesh.shape[a] for a in ("sect", "lon", "lat"))

    def on_device(fields, levels):
        vmem = pltpu.VMEM
        result = pl.pallas_call(
            functools.partial(kernel, n_sect, n_lon, n_lat),
            out_shape=jax.ShapeDtypeStruct((NT * 8, 128), F32),
            in_specs=[pl.BlockSpec(memory_space=pl.ANY), pl.BlockSpec(memory_space=pltpu.VMEM)],
            out_specs=pl.BlockSpec(memory_space=pltpu.VMEM),
            scratch_shapes=[
                vmem((NT * 8, 128), F32),
                vmem((32, 128), F32),
                vmem((32, 128), F32),
                vmem((32, 128), F32),
                vmem((4, N_ROW, 128), F32),
                vmem((4, N_ROW, 128), F32),
                vmem((16, 128), F32),
                vmem((16, 128), F32),
                vmem((16, 128), F32),
                vmem((16, 128), F32),
                vmem((2 * K * 8, 128), F32),
                vmem((5 * K, 128), F32),
                vmem((40, 128), F32),
                vmem((40, 128), F32),
                vmem((K * 8, 128), F32),
                vmem((NT * 8, 128), F32),
                vmem((K * 8, 128), F32),
                vmem((K * 8, 128), F32),
                vmem((16, 128), F32),
                vmem((2, NT, 128), F32),
                pltpu.SemaphoreType.DMA,
                pltpu.SemaphoreType.DMA((N_HALO,)),
                pltpu.SemaphoreType.DMA((N_HALO,)),
                pltpu.SemaphoreType.DMA((n_sect - 1, N_Z)),
                pltpu.SemaphoreType.DMA((N_Z,)),
            ],
            compiler_params=pltpu.CompilerParams(collective_id=0, has_side_effects=True),
        )(fields.reshape(NT * 8, 128), levels)
        return result.reshape(1, NF, K, 8, 128)

    return jax.shard_map(
        on_device,
        mesh=mesh,
        in_specs=(P("sect", None, None, "lat", "lon"), P("lat", "lon")),
        out_specs=P("sect", None, None, "lat", "lon"),
        check_vma=False,
    )
```

```python
import functools

import jax
import jax.numpy as jnp
from jax import lax
from jax.experimental import pallas as pl
from jax.experimental.pallas import tpu as pltpu
from jax.sharding import PartitionSpec as P

MESH = pl.DeviceIdType.MESH
F32 = jnp.float32
K = 16
NF = 6
NT = NF * K
SUB = 0.5
N_ROW = NT + 8

(R_COL_W, R_COL_E, R_NEAR_S, R_NEAR_N, R_FAR_S, R_FAR_N, R_CORNER_S, R_CORNER_N, R_FLOW_S, R_FLOW_N) = (*range(8), 8, 10)
N_HALO = 12
CH = 2
NC = K // CH
DV = 3
Z_PART, Z_COL, Z_DIFF = 2 * NC, 2 * NC + 2, 2 * NC + 3
N_Z = 2 * NC + 4


def tile(t):
    return pl.ds(pl.multiple_of(t * 8, 8), 8)


def lroll(x, amount):
    return pltpu.roll(x, amount, 1)


def sroll(x, amount):
    return pltpu.roll(x, amount, 0)


def face(level, limit, speed):
    return jnp.where(level < limit, speed, 0.0)


def coefficients(fe, fw, fn, fs):
    ce = -SUB * jnp.minimum(fe, 0.0)
    cw = SUB * jnp.maximum(fw, 0.0)
    cn = -SUB * jnp.minimum(fn, 0.0)
    cs = SUB * jnp.maximum(fs, 0.0)
    out = (jnp.maximum(fe, 0.0) - jnp.minimum(fw, 0.0)) + (jnp.maximum(fn, 0.0) - jnp.minimum(fs, 0.0))
    return 1.0 - SUB * out, ce, cw, cn, cs


def combine(c, q, qe, qw, qn, qs):
    c0, ce, cw, cn, cs = c
    return (c0 * q + (ce * qe + cw * qw)) + (cn * qn + cs * qs)


def kernel(n_sect, n_lon, n_lat, x_hbm, lev_ref, out,
           x, cols, cols_w, cols_e, rows_out, rows, near, far, corner_s, corner_n,
           zm, flow_rows, flow_rows_out, flow_cols, flow_cols_out, diff, rhs, div, ratio, ring_cols, ring_rows,
           in_sem, send_sem, recv_sem, zsend_sem, zsend2_sem, zrecv_sem):
    sect = lax.axis_index("sect")
    lon = lax.axis_index("lon")
    lat = lax.axis_index("lat")
    east = lax.rem(lon + 1, n_lon)
    west = lax.rem(lon + n_lon - 1, n_lon)
    has_s = lat > 0
    has_n = lat < n_lat - 1

    barrier = pltpu.get_barrier_semaphore()
    for step in range(1, n_sect):
        pl.semaphore_signal(barrier, inc=1, device_id={"sect": lax.rem(sect + step, n_sect)}, device_id_type=MESH)
    for side in (east, west):
        pl.semaphore_signal(barrier, inc=1, device_id={"lon": side}, device_id_type=MESH)

    @pl.when(has_s)
    def _():
        pl.semaphore_signal(barrier, inc=1, device_id={"lat": lat - 1}, device_id_type=MESH)

    @pl.when(has_n)
    def _():
        pl.semaphore_signal(barrier, inc=1, device_id={"lat": lat + 1}, device_id_type=MESH)

    load = pltpu.make_async_copy(x_hbm, x, in_sem)
    load.start()

    lane = lax.broadcasted_iota(jnp.int32, (8, 128), 1)
    row = lax.broadcasted_iota(jnp.int32, (8, 128), 0)
    even = (lane & 1) == 0
    pair = 63 - (lane >> 1)
    pair_b = 63 - (jnp.where(even, (lane + 126) >> 1, (lane + 1) >> 1) & 63)
    first_lane, last_lane = lane == 0, lane == 127
    first_row, last_row = row == 0, row == 7
    lev = lev_ref[...].astype(F32)
    zero = jnp.zeros((8, 128), F32)

    def bcast(value):
        return jnp.broadcast_to(value, (8, 128))

    @pl.when(jnp.logical_not(has_s))
    def _():
        rows[0] = jnp.zeros((N_ROW, 128), F32)
        rows[2] = jnp.zeros((N_ROW, 128), F32)
        corner_s[...] = jnp.zeros((16, 128), F32)
        flow_rows[:, 0:24, :] = jnp.zeros((2, 24, 128), F32)

    @pl.when(jnp.logical_not(has_n))
    def _():
        rows[1] = jnp.zeros((N_ROW, 128), F32)
        rows[3] = jnp.zeros((N_ROW, 128), F32)
        corner_n[...] = jnp.zeros((16, 128), F32)
        flow_rows[:, 24:40, :] = jnp.zeros((2, 16, 128), F32)

    load.wait()

    def pack(acc, value, turn, p):
        a, b = acc
        turned = lroll(value, turn)
        return jnp.where(pair == p, turned, a), jnp.where(pair_b == p, turned, b)

    def pack_level(k, carry):
        a0, a1, b0, b1 = carry
        for f in range(NF):
            p = (f % 4) * K + k
            value = x[tile(f * K + k), :]
            if f < 4:
                a0, b0 = pack((a0, b0), value, 127 - 2 * p, p)
            else:
                a1, b1 = pack((a1, b1), value, 127 - 2 * p, p)
        return a0, a1, b0, b1

    a0, a1, b0, b1 = lax.fori_loop(0, K, pack_level, (zero,) * 4)
    a1, b1 = pack((a1, b1), lev, 63, 32)
    for i, value in enumerate((a0, a1, b0, b1)):
        cols[i * 8:i * 8 + 8, :] = value

    def pack_rows(u, carry):
        for i, r in enumerate((7, 0, 6, 1)):
            rows_out[i, tile(u), :] = x[pl.ds(u * 64 + r, 8, stride=8), :]
        return carry

    lax.fori_loop(0, NT // 8, pack_rows, 0)
    for i, r in enumerate((7, 0, 6, 1)):
        rows_out[i, NT:NT + 8, :] = bcast(lev[r:r + 1, :])

    pl.semaphore_wait(barrier, n_sect + 1 + has_s.astype(jnp.int32) + has_n.astype(jnp.int32))

    def remote(src, dst, send, recv, to):
        return pltpu.make_async_remote_copy(src_ref=src, dst_ref=dst, send_sem=send, recv_sem=recv, device_id=to,
                                            device_id_type=MESH)

    def halo(src, dst, slot, to):
        return remote(src, dst, send_sem.at[slot], recv_sem.at[slot], to)

    south, north = {"lat": lat - 1}, {"lat": lat + 1}
    from_w = halo(cols, cols_w, R_COL_W, {"lon": east})
    from_e = halo(cols, cols_e, R_COL_E, {"lon": west})
    near_s = halo(rows_out.at[0], rows.at[0], R_NEAR_S, north)
    near_n = halo(rows_out.at[1], rows.at[1], R_NEAR_N, south)
    far_s = halo(rows_out.at[2], rows.at[2], R_FAR_S, north)
    far_n = halo(rows_out.at[3], rows.at[3], R_FAR_N, south)
    edge_s = halo(near, corner_s, R_CORNER_S, north)
    edge_n = halo(near, corner_n, R_CORNER_N, south)

    def flow_s(octet):
        return halo(flow_rows_out.at[octet, 0:24], flow_rows.at[octet, 0:24], R_FLOW_S + octet, north)

    def flow_n(octet):
        return halo(flow_rows_out.at[octet, 24:40], flow_rows.at[octet, 24:40], R_FLOW_N + octet, south)

    def across(src, dst, slot, peer):
        return remote(src, dst, zsend_sem.at[slot], zrecv_sem.at[slot], {"sect": peer})

    def rows_of(ref, start, size):
        return ref.at[pl.ds(pl.multiple_of(start * 8, 8), size * 8)]

    def speed(field, c):
        return across(rows_of(x_hbm, field * K + c * CH, CH), rows_of(zm, field * K + c * CH, CH), field * NC + c, field + 1)

    def speed_on(field, c, peer):
        part = rows_of(zm, field * K + c * CH, CH)
        return across(part, part, field * NC + c, peer)

    def part_of(field, peer):
        part = rows_of(diff, field * DV, DV)
        return across(part, part, Z_PART + field, peer)

    def both(slot, src, dst):
        return [remote(src, dst, zsend2_sem.at[peer - 1, slot - Z_COL], zrecv_sem.at[slot], {"sect": peer})
                for peer in range(1, n_sect)]

    send_cols = both(Z_COL, flow_cols_out, flow_cols)
    rest = slice(2 * DV * 8, K * 8)
    send_diff = both(Z_DIFF, diff.at[rest], diff.at[rest])

    from_w.start()
    from_e.start()

    @pl.when(has_n)
    def _():
        near_s.start()

    @pl.when(has_s)
    def _():
        near_n.start()

    @pl.when(sect == 0)
    def _():
        for c in range(NC):
            for field in range(2):
                speed(field, c).start()

    @pl.when(has_n & (sect != 0))
    def _():
        far_s.start()

    @pl.when(has_s & (sect != 0))
    def _():
        far_n.start()

    from_w.wait_recv()
    from_e.wait_recv()
    for v in range(2):
        a, b = slice(v * 8, v * 8 + 8), slice(16 + v * 8, 24 + v * 8)
        near[a, :] = jnp.where(even, lroll(cols_e[a, :], 127), lroll(cols_w[a, :], 1))
        far[a, :] = jnp.where(even, lroll(cols_e[b, :], 126), lroll(cols_w[b, :], 2))

    @pl.when(has_n)
    def _():
        edge_s.start()

    @pl.when(has_s)
    def _():
        edge_n.start()

    @pl.when(has_s)
    def _():
        near_s.wait_recv()

    @pl.when(has_n)
    def _():
        near_n.wait_recv()

    def neighbours(q, f, k, columns, south_ref, north_ref):
        v = (f // 4) * 8
        p = (f % 4) * K + k
        side = lroll(columns[v:v + 8, :], 2 * p + 1)
        return (
            jnp.where(last_lane, side, lroll(q, 127)),
            jnp.where(first_lane, side, lroll(q, 1)),
            jnp.where(last_row, bcast(north_ref[pl.ds(f * K + k, 1), :]), sroll(q, 7)),
            jnp.where(first_row, bcast(south_ref[pl.ds(f * K + k, 1), :]), sroll(q, 1)),
        )

    side = lroll(near[8:16, :], 65)
    lev_e = jnp.where(last_lane, side, lroll(lev, 127))
    lev_w = jnp.where(first_lane, side, lroll(lev, 1))
    lev_n = jnp.where(last_row, rows[1, NT:NT + 8, :], sroll(lev, 7))
    lev_s = jnp.where(first_row, rows[0, NT:NT + 8, :], sroll(lev, 1))
    lim_e, lim_w = jnp.minimum(lev, lev_e), jnp.minimum(lev, lev_w)
    lim_n, lim_s = jnp.minimum(lev, lev_n), jnp.minimum(lev, lev_s)

    @pl.when(sect == 0)
    def _():
        def around(f, k):
            q = x[tile(f * K + k), :]
            return q, neighbours(q, f, k, near, rows.at[0], rows.at[1])

        def conductances(k, level):
            v, (ve, vw, vn, vs) = around(4, k)
            return (face(level, lim_e, 0.5 * (v + ve)), face(level, lim_w, 0.5 * (vw + v)),
                    face(level, lim_n, 0.5 * (v + vn)), face(level, lim_s, 0.5 * (vs + v)))

        def diffuse(c, q, sides):
            ce, cw, cn, cs = c
            qe, qw, qn, qs = sides
            return ce * (qe - q) - cw * (q - qw) + cn * (qn - q) - cs * (q - qs)

        def warm(k, above):
            level = lax.convert_element_type(k, F32)
            c = conductances(k, level)
            t, sides = around(2, k)
            new = t + diffuse(c, t, sides)
            out[tile(2 * K + k), :] = new
            jump = 0.2 * (above - new)
            wet = jnp.where((level < lev) & (k > 0), x[tile(5 * K + k), :], 0.0)
            mixing = wet * (1.0 + 4.0 / (1.0 + jump * jump))
            out[tile(5 * K + k), :] = mixing
            diff[tile(k), :] = mixing
            return new

        lax.fori_loop(0, K, warm, zero)

        for field in range(2):
            part_of(field, field + 1).start()

        @pl.when(has_s)
        def _():
            edge_s.wait_recv()

        @pl.when(has_n)
        def _():
            edge_n.wait_recv()

        flow_cols_out[0:8, :] = jnp.where(
            lane >= 64, near[0:8, :], jnp.where(lane >= 32, lroll(far[0:8, :], 64), lroll(cols[0:8, :], 32)))
        flow_cols_out[8:16, :] = jnp.where(first_row, corner_n[0:8, :], corner_s[0:8, :])
        for copy in send_cols + send_diff:
            copy.start()

        def move(k, sums):
            level = lax.convert_element_type(k, F32)
            c = conductances(k, level)
            z, zs = around(0, k)
            m, ms = around(1, k)
            t, ts = around(2, k)
            s, ss = around(3, k)
            out[tile(3 * K + k), :] = s + diffuse(c, s, ss)
            here, at_e, at_n = sums

            def add(total, limit, sal, tem):
                return total + jnp.where(level < limit, 0.15 * sal - 0.2 * tem, 0.0)

            here = add(here, lev, s, t)
            at_e = add(at_e, lev_e, ss[0], ts[0])
            at_n = add(at_n, lev_n, ss[2], ts[2])
            new_z = z + (diffuse(c, z, zs) + 0.3 * m - 0.05 * (at_e - here))
            new_m = m + (diffuse(c, m, ms) - 0.3 * z - 0.05 * (at_n - here))
            out[tile(k), :] = face(level, lim_e, new_z)
            out[tile(K + k), :] = face(level, lim_n, new_m)
            div[tile(k), :] = (face(level, lim_e, z) - face(level, lim_w, zs[1])) + (
                face(level, lim_n, m) - face(level, lim_s, ms[3]))
            return here, at_e, at_n

        lax.fori_loop(0, K, move, (zero,) * 3)

        def rise(i, total):
            k = K - 1 - i
            total = total + div[tile(k), :]
            out[tile(4 * K + k), :] = jnp.where(k > 0, -total, 0.0)
            return total

        lax.fori_loop(0, K, rise, zero)

    @pl.when(sect != 0)
    def _():
        own, peer = sect - 1, 3 - sect
        for c in range(NC):
            speed_on(own, c, peer).wait_recv()
            speed_on(own, c, peer).start()
        part_of(own, peer).wait_recv()
        part_of(own, peer).start()

        @pl.when(has_s)
        def _():
            far_s.wait_recv()
            edge_s.wait_recv()

        @pl.when(has_n)
        def _():
            far_n.wait_recv()
            edge_n.wait_recv()

        def share_rows(octet):
            for c in range(octet * NC // 2, (octet + 1) * NC // 2):
                speed_on(1 - own, c, peer).wait_recv()
            for i, (field, r) in enumerate(((0, 7), (1, 7), (1, 6), (0, 0), (1, 0))):
                flow_rows_out[octet, i * 8:i * 8 + 8, :] = zm[pl.ds((field * K + octet * 8) * 8 + r, 8, stride=8), :]

            @pl.when(has_n)
            def _():
                flow_s(octet).start()

            @pl.when(has_s)
            def _():
                flow_n(octet).start()

        share_rows(0)
        send_cols[0].wait_recv()

        p1_lev = jnp.where(even, bcast(near[8:16, 62:63]), bcast(near[8:16, 63:64]))
        p2_lev = jnp.where(even, bcast(far[8:16, 62:63]), bcast(far[8:16, 63:64]))
        p0_lev = jnp.where(even, bcast(cols[8:16, 62:63]), bcast(cols[8:16, 63:64]))
        cs_lev = jnp.where(even, bcast(corner_s[8:16, 62:63]), bcast(corner_s[8:16, 63:64]))
        cn_lev = jnp.where(even, bcast(corner_n[8:16, 62:63]), bcast(corner_n[8:16, 63:64]))

        def up_one(value, beyond):
            return jnp.where(last_row, sroll(beyond, 7), sroll(value, 7))

        def down_one(value, beyond):
            return jnp.where(first_row, sroll(beyond, 1), sroll(value, 1))

        def repeat(value, offset):
            if offset:
                value = lroll(value, offset)
            value = jnp.where(lane >= 96, value, 0.0)
            value = value + lroll(value, 32)
            return value + lroll(value, 64)

        p1_z, p1_m, p2_z, p0_z = (repeat(flow_cols[0:8, :], offset) for offset in (0, 32, 64, 96))
        corner_m = repeat(flow_cols[8:16, :], 32)
        k_lane = (pair & (K - 1)).astype(F32)
        lim = functools.partial(jnp.minimum, p1_lev)
        c = coefficients(
            face(k_lane, lim(jnp.where(even, p2_lev, p0_lev)), p1_z),
            face(k_lane, lim(jnp.where(even, p0_lev, p2_lev)), jnp.where(even, p0_z, p2_z)),
            face(k_lane, lim(up_one(p1_lev, cn_lev)), p1_m),
            face(k_lane, lim(down_one(p1_lev, cs_lev)), down_one(p1_m, corner_m)),
        )
        for v in range(2):
            a = slice(v * 8, v * 8 + 8)
            p0, p1, p2 = cols[a, :], near[a, :], far[a, :]
            ring_cols[a, :] = combine(c, p1, jnp.where(even, p2, p0), jnp.where(even, p0, p2),
                                      up_one(p1, corner_n[a, :]), down_one(p1, corner_s[a, :]))

        def corner_of(value, at, p):
            return pltpu.roll(bcast(value[at:at + 1, :]), 2 * p + 1, 1, stride=2, stride_axis=0)

        def turn(value, corner):
            return jnp.where(last_lane, corner, lroll(value, 127)), jnp.where(first_lane, corner, lroll(value, 1))

        def ring_of(north_side, octet):
            at = 0 if north_side else 7
            corner = corner_n if north_side else corner_s
            base = 24 if north_side else 0
            r_lev = rows[north_side, NT:NT + 8, :]
            r_in = rows_out[1 - north_side, NT:NT + 8, :]
            r_out = rows[2 + north_side, NT:NT + 8, :]
            r_e, r_w = turn(r_lev, lroll(bcast(corner[8 + at:9 + at, :]), 65))
            k_row = (row + 8 * octet).astype(F32)
            z = flow_rows[octet, base:base + 8, :]
            m = flow_rows[octet, base + 8:base + 16, :]
            _, zw = turn(z, corner_of(flow_cols[8:16, :], at, octet * 8))
            lim_in, lim_out = jnp.minimum(r_lev, r_in), jnp.minimum(r_lev, r_out)
            if north_side:
                fn, fs = face(k_row, lim_out, m), face(k_row, lim_in, flow_rows_out[octet, 8:16, :])
            else:
                fn, fs = face(k_row, lim_in, m), face(k_row, lim_out, flow_rows[octet, 16:24, :])
            c = coefficients(face(k_row, jnp.minimum(r_lev, r_e), z), face(k_row, jnp.minimum(r_lev, r_w), zw), fn, fs)
            for f in range(NF):
                v, p, u = f // 4, (f % 4) * K + octet * 8, (f * K + octet * 8)
                a = slice(u, u + 8)
                q, inner, outer = rows[north_side, a, :], rows_out[1 - north_side, a, :], rows[2 + north_side, a, :]
                qe, qw = turn(q, corner_of(corner[v * 8:v * 8 + 8, :], at, p))
                qn, qs = (outer, inner) if north_side else (inner, outer)
                ring_rows[north_side, a, :] = combine(c, q, qe, qw, qn, qs)

        def advance(octet, k, carry):
            level = lax.convert_element_type(k, F32)
            z, m = zm[tile(k), :], zm[tile(K + k), :]
            side = lroll(flow_cols[0:8, :], 2 * k + 1)
            zw = jnp.where(first_lane, side, lroll(z, 1))
            ms = jnp.where(first_row, bcast(flow_rows[octet, pl.ds(k + 8 - octet * 8, 1), :]), sroll(m, 1))
            fe, fw, fn, fs = face(level, lim_e, z), face(level, lim_w, zw), face(level, lim_n, m), face(level, lim_s, ms)
            div[tile(k), :] = (fe - fw) + (fn - fs)
            c = coefficients(fe, fw, fn, fs)
            for f in range(NF):
                q = x[tile(f * K + k), :]
                q = combine(c, q, *neighbours(q, f, k, near, rows.at[0], rows.at[1]))
                q = combine(c, q, *neighbours(q, f, k, ring_cols, ring_rows.at[0], ring_rows.at[1]))
                rhs[tile(f * K + k), :] = q
            return carry

        for octet in range(2):
            if octet:
                share_rows(1)

            @pl.when(has_s)
            def _(octet=octet):
                flow_s(octet).wait_recv()

            @pl.when(has_n)
            def _(octet=octet):
                flow_n(octet).wait_recv()

            ring_of(0, octet)
            ring_of(1, octet)
            lax.fori_loop(octet * 8, octet * 8 + 8, functools.partial(advance, octet), 0)
        send_diff[0].wait_recv()
        part_of(1 - own, peer).wait_recv()

        def eliminate(i, carry):
            total, up_below, down_below, ratio_below, below = carry
            k = K - 1 - i
            total = total + div[tile(k), :]
            kappa = diff[tile(k), :]
            vertical = jnp.where(k > 0, -total, 0.0)
            up = jnp.maximum(vertical, 0.0) + kappa
            down = jnp.minimum(vertical, 0.0) - kappa
            inverse = 1.0 / ((1.0 + (up - down_below)) + up_below * ratio_below)
            here = down * inverse
            ratio[tile(k), :] = here
            values = []
            for f in range(NF):
                value = (rhs[tile(f * K + k), :] + up_below * below[f]) * inverse
                rhs[tile(f * K + k), :] = value
                values.append(value)
            return total, up, down, here, tuple(values)

        lax.fori_loop(0, K, eliminate, (zero,) * 4 + ((zero,) * NF,))

        def settle(k, above):
            level = lax.convert_element_type(k, F32)
            here = ratio[tile(k), :]
            values = []
            for f in range(NF):
                value = rhs[tile(f * K + k), :] - here * above[f]
                out[tile(f * K + k), :] = face(level, lev, value)
                values.append(value)
            return tuple(values)

        lax.fori_loop(0, K, settle, (zero,) * NF)

    from_w.wait_send()
    from_e.wait_send()

    @pl.when(has_n)
    def _():
        near_s.wait_send()
        edge_s.wait_send()

    @pl.when(has_s)
    def _():
        near_n.wait_send()
        edge_n.wait_send()

    @pl.when(has_n & (sect != 0))
    def _():
        for copy in (far_s, flow_s(0), flow_s(1)):
            copy.wait_send()

    @pl.when(has_s & (sect != 0))
    def _():
        for copy in (far_n, flow_n(0), flow_n(1)):
            copy.wait_send()

    @pl.when(sect == 0)
    def _():
        for field in range(2):
            for c in range(NC):
                speed(field, c).wait_send()
            part_of(field, field + 1).wait_send()
        for copy in send_cols + send_diff:
            copy.wait_send()

    @pl.when(sect != 0)
    def _():
        for c in range(NC):
            speed_on(sect - 1, c, 3 - sect).wait_send()
        part_of(sect - 1, 3 - sect).wait_send()


def solution(mesh):
    n_sect, n_lon, n_lat = (mesh.shape[a] for a in ("sect", "lon", "lat"))

    def on_device(fields, levels):
        vmem = pltpu.VMEM
        result = pl.pallas_call(
            functools.partial(kernel, n_sect, n_lon, n_lat),
            out_shape=jax.ShapeDtypeStruct((NT * 8, 128), F32),
            in_specs=[pl.BlockSpec(memory_space=pl.ANY), pl.BlockSpec(memory_space=pltpu.VMEM)],
            out_specs=pl.BlockSpec(memory_space=pltpu.VMEM),
            scratch_shapes=[
                vmem((NT * 8, 128), F32),
                vmem((32, 128), F32),
                vmem((32, 128), F32),
                vmem((32, 128), F32),
                vmem((4, N_ROW, 128), F32),
                vmem((4, N_ROW, 128), F32),
                vmem((16, 128), F32),
                vmem((16, 128), F32),
                vmem((16, 128), F32),
                vmem((16, 128), F32),
                vmem((2 * K * 8, 128), F32),
                vmem((2, 40, 128), F32),
                vmem((2, 40, 128), F32),
                vmem((16, 128), F32),
                vmem((16, 128), F32),
                vmem((K * 8, 128), F32),
                vmem((NT * 8, 128), F32),
                vmem((K * 8, 128), F32),
                vmem((K * 8, 128), F32),
                vmem((16, 128), F32),
                vmem((2, NT, 128), F32),
                pltpu.SemaphoreType.DMA,
                pltpu.SemaphoreType.DMA((N_HALO,)),
                pltpu.SemaphoreType.DMA((N_HALO,)),
                pltpu.SemaphoreType.DMA((N_Z,)),
                pltpu.SemaphoreType.DMA((n_sect - 1, 2)),
                pltpu.SemaphoreType.DMA((N_Z,)),
            ],
            compiler_params=pltpu.CompilerParams(collective_id=0, has_side_effects=True),
        )(fields.reshape(NT * 8, 128), levels)
        return result.reshape(1, NF, K, 8, 128)

    return jax.shard_map(
        on_device,
        mesh=mesh,
        in_specs=(P("sect", None, None, "lat", "lon"), P("lat", "lon")),
        out_specs=P("sect", None, None, "lat", "lon"),
        check_vma=False,
    )
```

```python
import functools

import jax
import jax.numpy as jnp
from jax import lax
from jax.experimental import pallas as pl
from jax.experimental.pallas import tpu as pltpu
from jax.sharding import PartitionSpec as P

MESH = pl.DeviceIdType.MESH
F32 = jnp.float32
K = 16
NF = 6
NT = NF * K
SUB = 0.5
N_ROW = NT + 8

(R_COL_W, R_COL_E, R_NEAR_S, R_NEAR_N, R_FAR_S, R_FAR_N, R_CORNER_S, R_CORNER_N, R_FLOW_S, R_FLOW_N) = (*range(8), 8, 10)
N_HALO = 12
CH = 2
NC = K // CH
DV = 3
Z_PART, Z_COL, Z_DIFF = 2 * NC, 2 * NC + 2, 2 * NC + 3
N_Z = 2 * NC + 4


def tile(t):
    return pl.ds(pl.multiple_of(t * 8, 8), 8)


def lroll(x, amount):
    return pltpu.roll(x, amount, 1)


def sroll(x, amount):
    return pltpu.roll(x, amount, 0)


def face(level, limit, speed):
    return jnp.where(level < limit, speed, 0.0)


def coefficients(fe, fw, fn, fs):
    ce = -SUB * jnp.minimum(fe, 0.0)
    cw = SUB * jnp.maximum(fw, 0.0)
    cn = -SUB * jnp.minimum(fn, 0.0)
    cs = SUB * jnp.maximum(fs, 0.0)
    out = (jnp.maximum(fe, 0.0) - jnp.minimum(fw, 0.0)) + (jnp.maximum(fn, 0.0) - jnp.minimum(fs, 0.0))
    return 1.0 - SUB * out, ce, cw, cn, cs


def combine(c, q, qe, qw, qn, qs):
    c0, ce, cw, cn, cs = c
    return (c0 * q + (ce * qe + cw * qw)) + (cn * qn + cs * qs)


def kernel(n_sect, n_lon, n_lat, x_hbm, lev_hbm, out,
           x, lev_ref, cols, cols_w, cols_e, rows_out, rows, near, far, corner_s, corner_n,
           zm, flow_rows, flow_rows_out, flow_cols, flow_cols_out, diff, rhs, div, ratio, ring_cols, ring_rows, shifted, turned,
           in_sem, send_sem, recv_sem, zsend_sem, zsend2_sem, zrecv_sem):
    sect = lax.axis_index("sect")
    lon = lax.axis_index("lon")
    lat = lax.axis_index("lat")
    east = lax.rem(lon + 1, n_lon)
    west = lax.rem(lon + n_lon - 1, n_lon)
    has_s = lat > 0
    has_n = lat < n_lat - 1

    barrier = pltpu.get_barrier_semaphore()
    for step in range(1, n_sect):
        pl.semaphore_signal(barrier, inc=1, device_id={"sect": lax.rem(sect + step, n_sect)}, device_id_type=MESH)
    for side in (east, west):
        pl.semaphore_signal(barrier, inc=1, device_id={"lon": side}, device_id_type=MESH)

    @pl.when(has_s)
    def _():
        pl.semaphore_signal(barrier, inc=1, device_id={"lat": lat - 1}, device_id_type=MESH)

    @pl.when(has_n)
    def _():
        pl.semaphore_signal(barrier, inc=1, device_id={"lat": lat + 1}, device_id_type=MESH)

    load = pltpu.make_async_copy(x_hbm, x, in_sem.at[0])
    load.start()
    load_lev = pltpu.make_async_copy(lev_hbm, lev_ref, in_sem.at[1])
    load_lev.start()

    lane = lax.broadcasted_iota(jnp.int32, (8, 128), 1)
    row = lax.broadcasted_iota(jnp.int32, (8, 128), 0)
    even = (lane & 1) == 0
    pair = 63 - (lane >> 1)
    pair_b = 63 - (jnp.where(even, (lane + 126) >> 1, (lane + 1) >> 1) & 63)
    first_lane, last_lane = lane == 0, lane == 127
    first_row, last_row = row == 0, row == 7
    zero = jnp.zeros((8, 128), F32)

    def bcast(value):
        return jnp.broadcast_to(value, (8, 128))

    @pl.when(jnp.logical_not(has_s))
    def _():
        rows[0] = jnp.zeros((N_ROW, 128), F32)
        rows[2] = jnp.zeros((N_ROW, 128), F32)
        corner_s[...] = jnp.zeros((16, 128), F32)
        flow_rows[:, 0:24, :] = jnp.zeros((2, 24, 128), F32)

    @pl.when(jnp.logical_not(has_n))
    def _():
        rows[1] = jnp.zeros((N_ROW, 128), F32)
        rows[3] = jnp.zeros((N_ROW, 128), F32)
        corner_n[...] = jnp.zeros((16, 128), F32)
        flow_rows[:, 24:40, :] = jnp.zeros((2, 16, 128), F32)

    load_lev.wait()
    load.wait()
    lev = lev_ref[...].astype(F32)

    def pack(acc, value, turn, p):
        a, b = acc
        turned = lroll(value, turn)
        return jnp.where(pair == p, turned, a), jnp.where(pair_b == p, turned, b)

    def pack_level(k, carry):
        a0, a1, b0, b1 = carry
        for f in range(NF):
            p = (f % 4) * K + k
            value = x[tile(f * K + k), :]
            if f < 4:
                a0, b0 = pack((a0, b0), value, 127 - 2 * p, p)
            else:
                a1, b1 = pack((a1, b1), value, 127 - 2 * p, p)
        return a0, a1, b0, b1

    a0, a1, b0, b1 = lax.fori_loop(0, K, pack_level, (zero,) * 4)
    a1, b1 = pack((a1, b1), lev, 63, 32)
    for i, value in enumerate((a0, a1, b0, b1)):
        cols[i * 8:i * 8 + 8, :] = value

    def pack_rows(u, carry):
        for i, r in enumerate((7, 0, 6, 1)):
            rows_out[i, tile(u), :] = x[pl.ds(u * 64 + r, 8, stride=8), :]
        return carry

    lax.fori_loop(0, NT // 8, pack_rows, 0)
    for i, r in enumerate((7, 0, 6, 1)):
        rows_out[i, NT:NT + 8, :] = bcast(lev[r:r + 1, :])

    pl.semaphore_wait(barrier, n_sect + 1 + has_s.astype(jnp.int32) + has_n.astype(jnp.int32))

    def remote(src, dst, send, recv, to):
        return pltpu.make_async_remote_copy(src_ref=src, dst_ref=dst, send_sem=send, recv_sem=recv, device_id=to,
                                            device_id_type=MESH)

    def halo(src, dst, slot, to):
        return remote(src, dst, send_sem.at[slot], recv_sem.at[slot], to)

    south, north = {"lat": lat - 1}, {"lat": lat + 1}
    from_w = halo(cols, cols_w, R_COL_W, {"lon": east})
    from_e = halo(cols, cols_e, R_COL_E, {"lon": west})
    near_s = halo(rows_out.at[0], rows.at[0], R_NEAR_S, north)
    near_n = halo(rows_out.at[1], rows.at[1], R_NEAR_N, south)
    far_s = halo(rows_out.at[2], rows.at[2], R_FAR_S, north)
    far_n = halo(rows_out.at[3], rows.at[3], R_FAR_N, south)
    edge_s = halo(near, corner_s, R_CORNER_S, north)
    edge_n = halo(near, corner_n, R_CORNER_N, south)

    def flow_s(octet):
        return halo(flow_rows_out.at[octet, 0:24], flow_rows.at[octet, 0:24], R_FLOW_S + octet, north)

    def flow_n(octet):
        return halo(flow_rows_out.at[octet, 24:40], flow_rows.at[octet, 24:40], R_FLOW_N + octet, south)

    def across(src, dst, slot, peer):
        return remote(src, dst, zsend_sem.at[slot], zrecv_sem.at[slot], {"sect": peer})

    def rows_of(ref, start, size):
        return ref.at[pl.ds(pl.multiple_of(start * 8, 8), size * 8)]

    def speed(field, c):
        return across(rows_of(x_hbm, field * K + c * CH, CH), rows_of(zm, field * K + c * CH, CH), field * NC + c, field + 1)

    def speed_on(field, c, peer):
        part = rows_of(zm, field * K + c * CH, CH)
        return across(part, part, field * NC + c, peer)

    def part_of(field, peer):
        part = rows_of(diff, field * DV, DV)
        return across(part, part, Z_PART + field, peer)

    def both(slot, src, dst):
        return [remote(src, dst, zsend2_sem.at[peer - 1, slot - Z_COL], zrecv_sem.at[slot], {"sect": peer})
                for peer in range(1, n_sect)]

    send_cols = both(Z_COL, flow_cols_out, flow_cols)
    rest = slice(2 * DV * 8, K * 8)
    send_diff = both(Z_DIFF, diff.at[rest], diff.at[rest])

    from_w.start()
    from_e.start()

    @pl.when(has_n)
    def _():
        near_s.start()

    @pl.when(has_s)
    def _():
        near_n.start()

    @pl.when(sect == 0)
    def _():
        for c in range(NC):
            for field in range(2):
                speed(field, c).start()

    @pl.when(has_n & (sect != 0))
    def _():
        far_s.start()

    @pl.when(has_s & (sect != 0))
    def _():
        far_n.start()

    own, peer = sect - 1, 3 - sect

    @pl.when(sect != 0)
    def _():
        for c in range(NC):
            speed_on(own, c, peer).wait_recv()
            speed_on(own, c, peer).start()

    from_w.wait_recv()
    from_e.wait_recv()
    for v in range(2):
        a, b = slice(v * 8, v * 8 + 8), slice(16 + v * 8, 24 + v * 8)
        near[a, :] = jnp.where(even, lroll(cols_e[a, :], 127), lroll(cols_w[a, :], 1))
        far[a, :] = jnp.where(even, lroll(cols_e[b, :], 126), lroll(cols_w[b, :], 2))

    @pl.when(has_n)
    def _():
        edge_s.start()

    @pl.when(has_s)
    def _():
        edge_n.start()

    @pl.when(has_s)
    def _():
        near_s.wait_recv()

    @pl.when(has_n)
    def _():
        near_n.wait_recv()

    def neighbours(q, f, k, columns, south_ref, north_ref):
        v = (f // 4) * 8
        p = (f % 4) * K + k
        side = lroll(columns[v:v + 8, :], 2 * p + 1)
        return (
            jnp.where(last_lane, side, lroll(q, 127)),
            jnp.where(first_lane, side, lroll(q, 1)),
            jnp.where(last_row, bcast(north_ref[pl.ds(f * K + k, 1), :]), sroll(q, 7)),
            jnp.where(first_row, bcast(south_ref[pl.ds(f * K + k, 1), :]), sroll(q, 1)),
        )

    side = lroll(near[8:16, :], 65)
    lev_e = jnp.where(last_lane, side, lroll(lev, 127))
    lev_w = jnp.where(first_lane, side, lroll(lev, 1))
    lev_n = jnp.where(last_row, rows[1, NT:NT + 8, :], sroll(lev, 7))
    lev_s = jnp.where(first_row, rows[0, NT:NT + 8, :], sroll(lev, 1))
    lim_e, lim_w = jnp.minimum(lev, lev_e), jnp.minimum(lev, lev_w)
    lim_n, lim_s = jnp.minimum(lev, lev_n), jnp.minimum(lev, lev_s)

    @pl.when(sect == 0)
    def _():
        def around(f, k):
            q = x[tile(f * K + k), :]
            return q, neighbours(q, f, k, near, rows.at[0], rows.at[1])

        def conductances(k, level):
            v, (ve, vw, vn, vs) = around(4, k)
            return (face(level, lim_e, 0.5 * (v + ve)), face(level, lim_w, 0.5 * (vw + v)),
                    face(level, lim_n, 0.5 * (v + vn)), face(level, lim_s, 0.5 * (vs + v)))

        def diffuse(c, q, sides):
            ce, cw, cn, cs = c
            qe, qw, qn, qs = sides
            return ce * (qe - q) - cw * (q - qw) + cn * (qn - q) - cs * (q - qs)

        def warm(k, above):
            level = lax.convert_element_type(k, F32)
            c = conductances(k, level)
            t, sides = around(2, k)
            new = t + diffuse(c, t, sides)
            out[tile(2 * K + k), :] = new
            jump = 0.2 * (above - new)
            wet = jnp.where((level < lev) & (k > 0), x[tile(5 * K + k), :], 0.0)
            mixing = wet * (1.0 + 4.0 / (1.0 + jump * jump))
            out[tile(5 * K + k), :] = mixing
            diff[tile(k), :] = mixing
            return new

        lax.fori_loop(0, K, warm, zero)

        for field in range(2):
            part_of(field, field + 1).start()

        @pl.when(has_s)
        def _():
            edge_s.wait_recv()

        @pl.when(has_n)
        def _():
            edge_n.wait_recv()

        flow_cols_out[0:8, :] = jnp.where(
            lane >= 64, near[0:8, :], jnp.where(lane >= 32, lroll(far[0:8, :], 64), lroll(cols[0:8, :], 32)))
        flow_cols_out[8:16, :] = jnp.where(first_row, corner_n[0:8, :], corner_s[0:8, :])
        for copy in send_cols + send_diff:
            copy.start()

        def move(k, sums):
            level = lax.convert_element_type(k, F32)
            c = conductances(k, level)
            z, zs = around(0, k)
            m, ms = around(1, k)
            t, ts = around(2, k)
            s, ss = around(3, k)
            out[tile(3 * K + k), :] = s + diffuse(c, s, ss)
            here, at_e, at_n = sums

            def add(total, limit, sal, tem):
                return total + jnp.where(level < limit, 0.15 * sal - 0.2 * tem, 0.0)

            here = add(here, lev, s, t)
            at_e = add(at_e, lev_e, ss[0], ts[0])
            at_n = add(at_n, lev_n, ss[2], ts[2])
            new_z = z + (diffuse(c, z, zs) + 0.3 * m - 0.05 * (at_e - here))
            new_m = m + (diffuse(c, m, ms) - 0.3 * z - 0.05 * (at_n - here))
            out[tile(k), :] = face(level, lim_e, new_z)
            out[tile(K + k), :] = face(level, lim_n, new_m)
            div[tile(k), :] = (face(level, lim_e, z) - face(level, lim_w, zs[1])) + (
                face(level, lim_n, m) - face(level, lim_s, ms[3]))
            return here, at_e, at_n

        lax.fori_loop(0, K, move, (zero,) * 3)

        def rise(i, total):
            k = K - 1 - i
            total = total + div[tile(k), :]
            out[tile(4 * K + k), :] = jnp.where(k > 0, -total, 0.0)
            return total

        lax.fori_loop(0, K, rise, zero)

    @pl.when(sect != 0)
    def _():
        def corner_of(value, at, p):
            return pltpu.roll(bcast(value[at:at + 1, :]), 2 * p + 1, 1, stride=2, stride_axis=0)

        def turn(value, corner):
            return jnp.where(last_lane, corner, lroll(value, 127)), jnp.where(first_lane, corner, lroll(value, 1))

        def shift(k, carry):
            for f in range(NF):
                q = x[tile(f * K + k), :]
                for i, value in enumerate(neighbours(q, f, k, near, rows.at[0], rows.at[1])):
                    shifted[i, tile(f * K + k), :] = value
            return carry

        lax.fori_loop(0, K, shift, 0)

        @pl.when(has_s)
        def _():
            far_s.wait_recv()
            edge_s.wait_recv()

        @pl.when(has_n)
        def _():
            far_n.wait_recv()
            edge_n.wait_recv()

        for north_side in range(2):
            corner = corner_n if north_side else corner_s
            for u in range(NT // 8):
                v, p, a = u // 8, (u * 8) % 64, slice(u * 8, u * 8 + 8)
                qe, qw = turn(rows[north_side, a, :], corner_of(corner[v * 8:v * 8 + 8, :], 0 if north_side else 7, p))
                turned[north_side, 0, a, :] = qe
                turned[north_side, 1, a, :] = qw

        def share_rows(octet):
            for c in range(octet * NC // 2, (octet + 1) * NC // 2):
                speed_on(1 - own, c, peer).wait_recv()
            for i, (field, r) in enumerate(((0, 7), (1, 7), (1, 6), (0, 0), (1, 0))):
                flow_rows_out[octet, i * 8:i * 8 + 8, :] = zm[pl.ds((field * K + octet * 8) * 8 + r, 8, stride=8), :]

            @pl.when(has_n)
            def _():
                flow_s(octet).start()

            @pl.when(has_s)
            def _():
                flow_n(octet).start()

        share_rows(0)
        part_of(own, peer).wait_recv()
        part_of(own, peer).start()
        share_rows(1)
        send_cols[0].wait_recv()

        p1_lev = jnp.where(even, bcast(near[8:16, 62:63]), bcast(near[8:16, 63:64]))
        p2_lev = jnp.where(even, bcast(far[8:16, 62:63]), bcast(far[8:16, 63:64]))
        p0_lev = jnp.where(even, bcast(cols[8:16, 62:63]), bcast(cols[8:16, 63:64]))
        cs_lev = jnp.where(even, bcast(corner_s[8:16, 62:63]), bcast(corner_s[8:16, 63:64]))
        cn_lev = jnp.where(even, bcast(corner_n[8:16, 62:63]), bcast(corner_n[8:16, 63:64]))

        def up_one(value, beyond):
            return jnp.where(last_row, sroll(beyond, 7), sroll(value, 7))

        def down_one(value, beyond):
            return jnp.where(first_row, sroll(beyond, 1), sroll(value, 1))

        def repeat(value, offset):
            if offset:
                value = lroll(value, offset)
            value = jnp.where(lane >= 96, value, 0.0)
            value = value + lroll(value, 32)
            return value + lroll(value, 64)

        p1_z, p1_m, p2_z, p0_z = (repeat(flow_cols[0:8, :], offset) for offset in (0, 32, 64, 96))
        corner_m = repeat(flow_cols[8:16, :], 32)
        k_lane = (pair & (K - 1)).astype(F32)
        lim = functools.partial(jnp.minimum, p1_lev)
        c = coefficients(
            face(k_lane, lim(jnp.where(even, p2_lev, p0_lev)), p1_z),
            face(k_lane, lim(jnp.where(even, p0_lev, p2_lev)), jnp.where(even, p0_z, p2_z)),
            face(k_lane, lim(up_one(p1_lev, cn_lev)), p1_m),
            face(k_lane, lim(down_one(p1_lev, cs_lev)), down_one(p1_m, corner_m)),
        )
        for v in range(2):
            a = slice(v * 8, v * 8 + 8)
            p0, p1, p2 = cols[a, :], near[a, :], far[a, :]
            ring_cols[a, :] = combine(c, p1, jnp.where(even, p2, p0), jnp.where(even, p0, p2),
                                      up_one(p1, corner_n[a, :]), down_one(p1, corner_s[a, :]))

        def ring_of(north_side, octet):
            at = 0 if north_side else 7
            corner = corner_n if north_side else corner_s
            base = 24 if north_side else 0
            r_lev = rows[north_side, NT:NT + 8, :]
            r_in = rows_out[1 - north_side, NT:NT + 8, :]
            r_out = rows[2 + north_side, NT:NT + 8, :]
            r_e, r_w = turn(r_lev, lroll(bcast(corner[8 + at:9 + at, :]), 65))
            k_row = (row + 8 * octet).astype(F32)
            z = flow_rows[octet, base:base + 8, :]
            m = flow_rows[octet, base + 8:base + 16, :]
            _, zw = turn(z, corner_of(flow_cols[8:16, :], at, octet * 8))
            lim_in, lim_out = jnp.minimum(r_lev, r_in), jnp.minimum(r_lev, r_out)
            if north_side:
                fn, fs = face(k_row, lim_out, m), face(k_row, lim_in, flow_rows_out[octet, 8:16, :])
            else:
                fn, fs = face(k_row, lim_in, m), face(k_row, lim_out, flow_rows[octet, 16:24, :])
            c = coefficients(face(k_row, jnp.minimum(r_lev, r_e), z), face(k_row, jnp.minimum(r_lev, r_w), zw), fn, fs)
            for f in range(NF):
                a = slice(f * K + octet * 8, f * K + octet * 8 + 8)
                q, inner, outer = rows[north_side, a, :], rows_out[1 - north_side, a, :], rows[2 + north_side, a, :]
                qe, qw = turned[north_side, 0, a, :], turned[north_side, 1, a, :]
                qn, qs = (outer, inner) if north_side else (inner, outer)
                ring_rows[north_side, a, :] = combine(c, q, qe, qw, qn, qs)

        def advance(octet, k, carry):
            level = lax.convert_element_type(k, F32)
            z, m = zm[tile(k), :], zm[tile(K + k), :]
            side = lroll(flow_cols[0:8, :], 2 * k + 1)
            zw = jnp.where(first_lane, side, lroll(z, 1))
            ms = jnp.where(first_row, bcast(flow_rows[octet, pl.ds(k + 8 - octet * 8, 1), :]), sroll(m, 1))
            fe, fw, fn, fs = face(level, lim_e, z), face(level, lim_w, zw), face(level, lim_n, m), face(level, lim_s, ms)
            div[tile(k), :] = (fe - fw) + (fn - fs)
            c = coefficients(fe, fw, fn, fs)
            for f in range(NF):
                q = x[tile(f * K + k), :]
                q = combine(c, q, *(shifted[i, tile(f * K + k), :] for i in range(4)))
                q = combine(c, q, *neighbours(q, f, k, ring_cols, ring_rows.at[0], ring_rows.at[1]))
                rhs[tile(f * K + k), :] = q
            return carry

        for octet in range(2):
            @pl.when(has_s)
            def _(octet=octet):
                flow_s(octet).wait_recv()

            @pl.when(has_n)
            def _(octet=octet):
                flow_n(octet).wait_recv()

            ring_of(0, octet)
            ring_of(1, octet)
            lax.fori_loop(octet * 8, octet * 8 + 8, functools.partial(advance, octet), 0)
        send_diff[0].wait_recv()
        part_of(1 - own, peer).wait_recv()

        def eliminate(i, carry):
            total, up_below, down_below, ratio_below, below = carry
            k = K - 1 - i
            total = total + div[tile(k), :]
            kappa = diff[tile(k), :]
            vertical = jnp.where(k > 0, -total, 0.0)
            up = jnp.maximum(vertical, 0.0) + kappa
            down = jnp.minimum(vertical, 0.0) - kappa
            inverse = 1.0 / ((1.0 + (up - down_below)) + up_below * ratio_below)
            here = down * inverse
            ratio[tile(k), :] = here
            values = []
            for f in range(NF):
                value = (rhs[tile(f * K + k), :] + up_below * below[f]) * inverse
                rhs[tile(f * K + k), :] = value
                values.append(value)
            return total, up, down, here, tuple(values)

        lax.fori_loop(0, K, eliminate, (zero,) * 4 + ((zero,) * NF,))

        def settle(k, above):
            level = lax.convert_element_type(k, F32)
            here = ratio[tile(k), :]
            values = []
            for f in range(NF):
                value = rhs[tile(f * K + k), :] - here * above[f]
                out[tile(f * K + k), :] = face(level, lev, value)
                values.append(value)
            return tuple(values)

        lax.fori_loop(0, K, settle, (zero,) * NF)

    from_w.wait_send()
    from_e.wait_send()

    @pl.when(has_n)
    def _():
        near_s.wait_send()
        edge_s.wait_send()

    @pl.when(has_s)
    def _():
        near_n.wait_send()
        edge_n.wait_send()

    @pl.when(has_n & (sect != 0))
    def _():
        for copy in (far_s, flow_s(0), flow_s(1)):
            copy.wait_send()

    @pl.when(has_s & (sect != 0))
    def _():
        for copy in (far_n, flow_n(0), flow_n(1)):
            copy.wait_send()

    @pl.when(sect == 0)
    def _():
        for field in range(2):
            for c in range(NC):
                speed(field, c).wait_send()
            part_of(field, field + 1).wait_send()
        for copy in send_cols + send_diff:
            copy.wait_send()

    @pl.when(sect != 0)
    def _():
        for c in range(NC):
            speed_on(sect - 1, c, 3 - sect).wait_send()
        part_of(sect - 1, 3 - sect).wait_send()


def solution(mesh):
    n_sect, n_lon, n_lat = (mesh.shape[a] for a in ("sect", "lon", "lat"))

    def on_device(fields, levels):
        vmem = pltpu.VMEM
        result = pl.pallas_call(
            functools.partial(kernel, n_sect, n_lon, n_lat),
            out_shape=pltpu.VMEM((NT * 8, 128), F32),
            in_specs=[pl.BlockSpec(memory_space=pl.ANY)] * 2,
            out_specs=pl.BlockSpec(memory_space=pltpu.VMEM),
            scratch_shapes=[
                vmem((NT * 8, 128), F32),
                vmem((8, 128), jnp.int32),
                vmem((32, 128), F32),
                vmem((32, 128), F32),
                vmem((32, 128), F32),
                vmem((4, N_ROW, 128), F32),
                vmem((4, N_ROW, 128), F32),
                vmem((16, 128), F32),
                vmem((16, 128), F32),
                vmem((16, 128), F32),
                vmem((16, 128), F32),
                vmem((2 * K * 8, 128), F32),
                vmem((2, 40, 128), F32),
                vmem((2, 40, 128), F32),
                vmem((16, 128), F32),
                vmem((16, 128), F32),
                vmem((K * 8, 128), F32),
                vmem((NT * 8, 128), F32),
                vmem((K * 8, 128), F32),
                vmem((K * 8, 128), F32),
                vmem((16, 128), F32),
                vmem((2, NT, 128), F32),
                vmem((4, NT * 8, 128), F32),
                vmem((2, 2, NT, 128), F32),
                pltpu.SemaphoreType.DMA((2,)),
                pltpu.SemaphoreType.DMA((N_HALO,)),
                pltpu.SemaphoreType.DMA((N_HALO,)),
                pltpu.SemaphoreType.DMA((N_Z,)),
                pltpu.SemaphoreType.DMA((n_sect - 1, 2)),
                pltpu.SemaphoreType.DMA((N_Z,)),
            ],
            compiler_params=pltpu.CompilerParams(collective_id=0, has_side_effects=True),
        )(fields.reshape(NT * 8, 128), levels)
        return result.reshape(1, NF, K, 8, 128)

    return jax.shard_map(
        on_device,
        mesh=mesh,
        in_specs=(P("sect", None, None, "lat", "lon"), P("lat", "lon")),
        out_specs=P("sect", None, None, "lat", "lon"),
        check_vma=False,
    )
```

```python
import functools

import jax
import jax.numpy as jnp
from jax import lax
from jax.experimental import pallas as pl
from jax.experimental.pallas import tpu as pltpu
from jax.sharding import PartitionSpec as P

MESH = pl.DeviceIdType.MESH
F32 = jnp.float32
K = 16
NF = 6
NT = NF * K
SUB = 0.5
N_ROW = NT + 8

(R_COL_W, R_COL_E, R_NEAR_S, R_NEAR_N, R_FAR_S, R_FAR_N, R_CORNER_S, R_CORNER_N, R_FLOW_S, R_FLOW_N) = (*range(8), 8, 10)
N_HALO = 12
CH = 2
NC = K // CH
Z_COL, Z_DIFF = 2 * NC, 2 * NC + 1
N_Z = 2 * NC + 2
DEPTH = 4
VIA_FIRST = 2
VIA_SECOND = 3
(E, W, N, S, FIRST, SECOND, GO) = range(7)
MID = 2


def tile(t):
    return pl.ds(pl.multiple_of(t * 8, 8), 8)


def lroll(x, amount):
    return pltpu.roll(x, amount, 1)


def sroll(x, amount):
    return pltpu.roll(x, amount, 0)


def face(level, limit, speed):
    return jnp.where(level < limit, speed, 0.0)


def coefficients(fe, fw, fn, fs):
    ce = -SUB * jnp.minimum(fe, 0.0)
    cw = SUB * jnp.maximum(fw, 0.0)
    cn = -SUB * jnp.minimum(fn, 0.0)
    cs = SUB * jnp.maximum(fs, 0.0)
    out = (jnp.maximum(fe, 0.0) - jnp.minimum(fw, 0.0)) + (jnp.maximum(fn, 0.0) - jnp.minimum(fs, 0.0))
    return 1.0 - SUB * out, ce, cw, cn, cs


def combine(c, q, qe, qw, qn, qs):
    c0, ce, cw, cn, cs = c
    return (c0 * q + (ce * qe + cw * qw)) + (cn * qn + cs * qs)


def kernel(n_sect, n_lon, n_lat, x_hbm, lev_hbm, out,
           x, lev_ref, cols, cols_w, cols_e, rows_out, rows, near, far, corner_s, corner_n,
           zm, flow_rows, flow_rows_out, flow_cols, flow_cols_out, diff, rhs, div, ratio, ring_cols, ring_rows, shifted, turned,
           in_sem, send_sem, recv_sem, zsend_sem, zrecv_sem, ready):
    sect = lax.axis_index("sect")
    lon = lax.axis_index("lon")
    lat = lax.axis_index("lat")
    east = lax.rem(lon + 1, n_lon)
    west = lax.rem(lon + n_lon - 1, n_lon)
    has_s = lat > 0
    has_n = lat < n_lat - 1

    place = lax.rem(lon // 2, DEPTH)
    to_first, to_second = place < VIA_SECOND, place >= VIA_FIRST
    onward = (sect == 1) & jnp.logical_not(to_second)
    passes_on = onward | ((sect == 2) & jnp.logical_not(to_first))
    paired = jnp.logical_not(to_first & to_second)

    run, half = 2 * DEPTH, n_lat // 2
    end, head = lax.rem(lon, run) == run - 1, lax.rem(lon, run) == 0
    to = ({"lon": east}, {"lon": west}, {"lat": lat + 1}, {"lat": lat - 1}, {"sect": 1}, {"sect": 2})
    announces = (jnp.logical_not(end), head, has_n & ((lat < half) | (lat == n_lat - 2)), has_s & ((lat > half) | (lat == 1)),
                 (sect == 0) & to_first, ((sect == 0) & to_second) | ((sect == 1) & paired))
    hears = (end, jnp.logical_not(head), has_n & ((lat >= half) | (lat == 0)), has_s & ((lat <= half) | (lat == n_lat - 1)))
    hears_sect = ((sect == 1) & to_first, (sect == 2) & to_second, (sect == 2) & paired)

    def signal(sem, where):
        pl.semaphore_signal(sem, inc=1, device_id=where, device_id_type=MESH)

    mid = (sect == 0) & (place == MID)
    held = (sect == 0) & (place != MID)

    barrier = pltpu.get_barrier_semaphore()

    @pl.when(held)
    def _():
        signal(barrier, {"lon": lon + 2 * (MID - place)})

    for side in range(6):
        @pl.when(announces[side])
        def _(side=side):
            signal(barrier, to[side])

    load = pltpu.make_async_copy(x_hbm, x, in_sem.at[0])
    load.start()
    load_lev = pltpu.make_async_copy(lev_hbm, lev_ref, in_sem.at[1])
    load_lev.start()

    lane = lax.broadcasted_iota(jnp.int32, (8, 128), 1)
    row = lax.broadcasted_iota(jnp.int32, (8, 128), 0)
    even = (lane & 1) == 0
    pair = 63 - (lane >> 1)
    pair_b = 63 - (jnp.where(even, (lane + 126) >> 1, (lane + 1) >> 1) & 63)
    first_lane, last_lane = lane == 0, lane == 127
    first_row, last_row = row == 0, row == 7
    zero = jnp.zeros((8, 128), F32)

    def bcast(value):
        return jnp.broadcast_to(value, (8, 128))

    pl.semaphore_wait(barrier, sum(heard.astype(jnp.int32) for heard in hears + hears_sect) + jnp.where(mid, DEPTH - 1, 0))
    for side, back in ((E, W), (W, E), (N, S), (S, N)):
        @pl.when(hears[side])
        def _(side=side, back=back):
            signal(ready.at[back], to[side])

    for heard, slot, lower in ((hears_sect[0], FIRST, 0), (hears_sect[1], SECOND, 0),
                               ((sect == 2) & jnp.logical_not(to_second), SECOND, 1)):
        @pl.when(heard)
        def _(slot=slot, lower=lower):
            signal(ready.at[slot], {"sect": lower})

    def await_ready(side, only=True):
        @pl.when(announces[side] & only)
        def _():
            pl.semaphore_wait(ready.at[side], 1)

    @pl.when(jnp.logical_not(has_s))
    def _():
        rows[0] = jnp.zeros((N_ROW, 128), F32)
        rows[2] = jnp.zeros((N_ROW, 128), F32)
        corner_s[...] = jnp.zeros((16, 128), F32)
        flow_rows[:, 0:24, :] = jnp.zeros((2, 24, 128), F32)

    @pl.when(jnp.logical_not(has_n))
    def _():
        rows[1] = jnp.zeros((N_ROW, 128), F32)
        rows[3] = jnp.zeros((N_ROW, 128), F32)
        corner_n[...] = jnp.zeros((16, 128), F32)
        flow_rows[:, 24:40, :] = jnp.zeros((2, 16, 128), F32)

    load_lev.wait()
    load.wait()
    lev = lev_ref[...].astype(F32)

    def pack(acc, value, turn, p):
        a, b = acc
        turned = lroll(value, turn)
        return jnp.where(pair == p, turned, a), jnp.where(pair_b == p, turned, b)

    def pack_level(k, carry):
        a0, a1, b0, b1 = carry
        for f in range(NF):
            p = (f % 4) * K + k
            value = x[tile(f * K + k), :]
            if f < 4:
                a0, b0 = pack((a0, b0), value, 127 - 2 * p, p)
            else:
                a1, b1 = pack((a1, b1), value, 127 - 2 * p, p)
        return a0, a1, b0, b1

    a0, a1, b0, b1 = lax.fori_loop(0, K, pack_level, (zero,) * 4, unroll=4)
    a1, b1 = pack((a1, b1), lev, 63, 32)
    for i, value in enumerate((a0, a1, b0, b1)):
        cols[i * 8:i * 8 + 8, :] = value

    def pack_rows(u, carry):
        for i, r in enumerate((7, 0, 6, 1)):
            rows_out[i, tile(u), :] = x[pl.ds(u * 64 + r, 8, stride=8), :]
        return carry

    lax.fori_loop(0, NT // 8, pack_rows, 0, unroll=4)
    for i, r in enumerate((7, 0, 6, 1)):
        rows_out[i, NT:NT + 8, :] = bcast(lev[r:r + 1, :])

    def remote(src, dst, send, recv, to):
        return pltpu.make_async_remote_copy(src_ref=src, dst_ref=dst, send_sem=send, recv_sem=recv, device_id=to,
                                            device_id_type=MESH)

    def halo(src, dst, slot, to):
        return remote(src, dst, send_sem.at[slot], recv_sem.at[slot], to)

    south, north = {"lat": lat - 1}, {"lat": lat + 1}
    from_w = halo(cols, cols_w, R_COL_W, {"lon": east})
    from_e = halo(cols, cols_e, R_COL_E, {"lon": west})
    near_s = halo(rows_out.at[0], rows.at[0], R_NEAR_S, north)
    near_n = halo(rows_out.at[1], rows.at[1], R_NEAR_N, south)
    far_s = halo(rows_out.at[2], rows.at[2], R_FAR_S, north)
    far_n = halo(rows_out.at[3], rows.at[3], R_FAR_N, south)
    edge_s = halo(near, corner_s, R_CORNER_S, north)
    edge_n = halo(near, corner_n, R_CORNER_N, south)

    def flow_s(octet):
        return halo(flow_rows_out.at[octet, 0:24], flow_rows.at[octet, 0:24], R_FLOW_S + octet, north)

    def flow_n(octet):
        return halo(flow_rows_out.at[octet, 24:40], flow_rows.at[octet, 24:40], R_FLOW_N + octet, south)

    def across(src, dst, slot, peer):
        return remote(src, dst, zsend_sem.at[slot], zrecv_sem.at[slot], {"sect": peer})

    def rows_of(ref, start, size):
        return ref.at[pl.ds(pl.multiple_of(start * 8, 8), size * 8)]

    peer = 3 - sect

    def chunk(field, c, target, relayed=False):
        part = field * K + c * CH
        slot = field * NC + c
        src = rows_of(zm if relayed else x_hbm, part, CH)
        return remote(src, rows_of(zm, part, CH), zsend_sem.at[0 if relayed else target - 1, slot], zrecv_sem.at[slot],
                      {"sect": target})

    def send_cols(target, relayed=False):
        return remote(flow_cols if relayed else flow_cols_out, flow_cols, zsend_sem.at[0 if relayed else target - 1, Z_COL],
                      zrecv_sem.at[Z_COL], {"sect": target})

    def send_diff(target, relayed=False):
        return remote(diff, diff, zsend_sem.at[0 if relayed else target - 1, Z_DIFF], zrecv_sem.at[Z_DIFF], {"sect": target})

    def to_tracers(act, targets, *copies):
        for target in targets:
            @pl.when((to_first, to_second)[target - 1])
            def _(target=target):
                for make in copies:
                    act(make(target))

    def start(copy):
        copy.start()

    def wait_send(copy):
        copy.wait_send()

    chunks = [functools.partial(chunk, field, c) for c in range(NC) for field in range(2)]

    await_ready(E)
    from_w.start()
    await_ready(W)
    from_e.start()
    await_ready(N)
    await_ready(S)

    @pl.when(has_n)
    def _():
        near_s.start()

    @pl.when(has_s)
    def _():
        near_n.start()

    @pl.when(sect == 0)
    def _():
        await_ready(FIRST)
        to_tracers(start, (1,), *chunks)

    @pl.when(has_n & (sect != 0))
    def _():
        far_s.start()

    @pl.when(has_s & (sect != 0))
    def _():
        far_n.start()

    await_ready(SECOND, onward)

    @pl.when(passes_on)
    def _():
        for make in chunks:
            make(peer, True).wait_recv()
            make(peer, True).start()

    from_w.wait_recv()
    from_e.wait_recv()
    for v in range(2):
        a, b = slice(v * 8, v * 8 + 8), slice(16 + v * 8, 24 + v * 8)
        near[a, :] = jnp.where(even, lroll(cols_e[a, :], 127), lroll(cols_w[a, :], 1))
        far[a, :] = jnp.where(even, lroll(cols_e[b, :], 126), lroll(cols_w[b, :], 2))

    @pl.when(has_n)
    def _():
        edge_s.start()

    @pl.when(has_s)
    def _():
        edge_n.start()

    @pl.when(has_s)
    def _():
        near_s.wait_recv()

    @pl.when(has_n)
    def _():
        near_n.wait_recv()

    def neighbours(q, f, k, columns, south_ref, north_ref):
        v = (f // 4) * 8
        p = (f % 4) * K + k
        side = lroll(columns[v:v + 8, :], 2 * p + 1)
        return (
            jnp.where(last_lane, side, lroll(q, 127)),
            jnp.where(first_lane, side, lroll(q, 1)),
            jnp.where(last_row, bcast(north_ref[pl.ds(f * K + k, 1), :]), sroll(q, 7)),
            jnp.where(first_row, bcast(south_ref[pl.ds(f * K + k, 1), :]), sroll(q, 1)),
        )

    side = lroll(near[8:16, :], 65)
    lev_e = jnp.where(last_lane, side, lroll(lev, 127))
    lev_w = jnp.where(first_lane, side, lroll(lev, 1))
    lev_n = jnp.where(last_row, rows[1, NT:NT + 8, :], sroll(lev, 7))
    lev_s = jnp.where(first_row, rows[0, NT:NT + 8, :], sroll(lev, 1))
    lim_e, lim_w = jnp.minimum(lev, lev_e), jnp.minimum(lev, lev_w)
    lim_n, lim_s = jnp.minimum(lev, lev_n), jnp.minimum(lev, lev_s)

    @pl.when(sect == 0)
    def _():
        def around(f, k):
            q = x[tile(f * K + k), :]
            return q, neighbours(q, f, k, near, rows.at[0], rows.at[1])

        def conductances(k, level):
            v, (ve, vw, vn, vs) = around(4, k)
            return (face(level, lim_e, 0.5 * (v + ve)), face(level, lim_w, 0.5 * (vw + v)),
                    face(level, lim_n, 0.5 * (v + vn)), face(level, lim_s, 0.5 * (vs + v)))

        def diffuse(c, q, sides):
            ce, cw, cn, cs = c
            qe, qw, qn, qs = sides
            return ce * (qe - q) - cw * (q - qw) + cn * (qn - q) - cs * (q - qs)

        def warm(k, above):
            level = lax.convert_element_type(k, F32)
            c = conductances(k, level)
            t, sides = around(2, k)
            new = t + diffuse(c, t, sides)
            out[tile(2 * K + k), :] = new
            jump = 0.2 * (above - new)
            wet = jnp.where((level < lev) & (k > 0), x[tile(5 * K + k), :], 0.0)
            mixing = wet * (1.0 + 4.0 / (1.0 + jump * jump))
            out[tile(5 * K + k), :] = mixing
            diff[tile(k), :] = mixing
            return new

        lax.fori_loop(0, K, warm, zero, unroll=4)

        @pl.when(has_s)
        def _():
            edge_s.wait_recv()

        @pl.when(has_n)
        def _():
            edge_n.wait_recv()

        flow_cols_out[0:8, :] = jnp.where(
            lane >= 64, near[0:8, :], jnp.where(lane >= 32, lroll(far[0:8, :], 64), lroll(cols[0:8, :], 32)))
        flow_cols_out[8:16, :] = jnp.where(first_row, corner_n[0:8, :], corner_s[0:8, :])
        to_tracers(start, (1,), send_cols)

        @pl.when(mid)
        def _():
            send_diff(1).start()

        await_ready(SECOND)
        to_tracers(start, (2,), *chunks, send_cols)

        @pl.when(mid)
        def _():
            send_diff(2).start()

        def move(k, sums):
            level = lax.convert_element_type(k, F32)
            c = conductances(k, level)
            z, zs = around(0, k)
            m, ms = around(1, k)
            t, ts = around(2, k)
            s, ss = around(3, k)
            out[tile(3 * K + k), :] = s + diffuse(c, s, ss)
            here, at_e, at_n = sums

            def add(total, limit, sal, tem):
                return total + jnp.where(level < limit, 0.15 * sal - 0.2 * tem, 0.0)

            here = add(here, lev, s, t)
            at_e = add(at_e, lev_e, ss[0], ts[0])
            at_n = add(at_n, lev_n, ss[2], ts[2])
            new_z = z + (diffuse(c, z, zs) + 0.3 * m - 0.05 * (at_e - here))
            new_m = m + (diffuse(c, m, ms) - 0.3 * z - 0.05 * (at_n - here))
            out[tile(k), :] = face(level, lim_e, new_z)
            out[tile(K + k), :] = face(level, lim_n, new_m)
            div[tile(k), :] = (face(level, lim_e, z) - face(level, lim_w, zs[1])) + (
                face(level, lim_n, m) - face(level, lim_s, ms[3]))
            return here, at_e, at_n

        lax.fori_loop(0, K, move, (zero,) * 3, unroll=2)

        def rise(i, total):
            k = K - 1 - i
            total = total + div[tile(k), :]
            out[tile(4 * K + k), :] = jnp.where(k > 0, -total, 0.0)
            return total

        lax.fori_loop(0, K, rise, zero, unroll=4)

        @pl.when(mid)
        def _():
            for target, others in ((1, range(MID)), (2, range(MID + 1, DEPTH))):
                for make in chunks:
                    make(target).wait_send()
                for other in others:
                    signal(ready.at[GO], {"lon": lon + 2 * (other - MID)})

        @pl.when(held)
        def _():
            pl.semaphore_wait(ready.at[GO], 1)
            to_tracers(start, (1, 2), send_diff)

    @pl.when(sect != 0)
    def _():
        def corner_of(value, at, p):
            return pltpu.roll(bcast(value[at:at + 1, :]), 2 * p + 1, 1, stride=2, stride_axis=0)

        def turn(value, corner):
            return jnp.where(last_lane, corner, lroll(value, 127)), jnp.where(first_lane, corner, lroll(value, 1))

        def shift(k, carry):
            for f in range(NF):
                q = x[tile(f * K + k), :]
                for i, value in enumerate(neighbours(q, f, k, near, rows.at[0], rows.at[1])):
                    shifted[i, tile(f * K + k), :] = value
            return carry

        lax.fori_loop(0, K, shift, 0, unroll=2)

        def share_rows(octet):
            @pl.when(jnp.logical_not(passes_on))
            def _():
                for make in chunks[octet * NC:(octet + 1) * NC]:
                    make(1).wait_recv()

            for i, (field, r) in enumerate(((0, 7), (1, 7), (1, 6), (0, 0), (1, 0))):
                flow_rows_out[octet, i * 8:i * 8 + 8, :] = zm[pl.ds((field * K + octet * 8) * 8 + r, 8, stride=8), :]

            @pl.when(has_n)
            def _():
                flow_s(octet).start()

            @pl.when(has_s)
            def _():
                flow_n(octet).start()

        share_rows(0)
        share_rows(1)
        @pl.when(has_s)
        def _():
            far_s.wait_recv()
            edge_s.wait_recv()

        @pl.when(has_n)
        def _():
            far_n.wait_recv()
            edge_n.wait_recv()

        for north_side in range(2):
            corner = corner_n if north_side else corner_s
            for u in range(NT // 8):
                v, p, a = u // 8, (u * 8) % 64, slice(u * 8, u * 8 + 8)
                qe, qw = turn(rows[north_side, a, :], corner_of(corner[v * 8:v * 8 + 8, :], 0 if north_side else 7, p))
                turned[north_side, 0, a, :] = qe
                turned[north_side, 1, a, :] = qw

        send_cols(1).wait_recv()

        @pl.when(passes_on)
        def _():
            send_cols(peer, True).start()


        p1_lev = jnp.where(even, bcast(near[8:16, 62:63]), bcast(near[8:16, 63:64]))
        p2_lev = jnp.where(even, bcast(far[8:16, 62:63]), bcast(far[8:16, 63:64]))
        p0_lev = jnp.where(even, bcast(cols[8:16, 62:63]), bcast(cols[8:16, 63:64]))
        cs_lev = jnp.where(even, bcast(corner_s[8:16, 62:63]), bcast(corner_s[8:16, 63:64]))
        cn_lev = jnp.where(even, bcast(corner_n[8:16, 62:63]), bcast(corner_n[8:16, 63:64]))

        def up_one(value, beyond):
            return jnp.where(last_row, sroll(beyond, 7), sroll(value, 7))

        def down_one(value, beyond):
            return jnp.where(first_row, sroll(beyond, 1), sroll(value, 1))

        def repeat(value, offset):
            if offset:
                value = lroll(value, offset)
            value = jnp.where(lane >= 96, value, 0.0)
            value = value + lroll(value, 32)
            return value + lroll(value, 64)

        p1_z, p1_m, p2_z, p0_z = (repeat(flow_cols[0:8, :], offset) for offset in (0, 32, 64, 96))
        corner_m = repeat(flow_cols[8:16, :], 32)
        k_lane = (pair & (K - 1)).astype(F32)
        lim = functools.partial(jnp.minimum, p1_lev)
        c = coefficients(
            face(k_lane, lim(jnp.where(even, p2_lev, p0_lev)), p1_z),
            face(k_lane, lim(jnp.where(even, p0_lev, p2_lev)), jnp.where(even, p0_z, p2_z)),
            face(k_lane, lim(up_one(p1_lev, cn_lev)), p1_m),
            face(k_lane, lim(down_one(p1_lev, cs_lev)), down_one(p1_m, corner_m)),
        )
        for v in range(2):
            a = slice(v * 8, v * 8 + 8)
            p0, p1, p2 = cols[a, :], near[a, :], far[a, :]
            ring_cols[a, :] = combine(c, p1, jnp.where(even, p2, p0), jnp.where(even, p0, p2),
                                      up_one(p1, corner_n[a, :]), down_one(p1, corner_s[a, :]))

        def ring_of(north_side, octet):
            at = 0 if north_side else 7
            corner = corner_n if north_side else corner_s
            base = 24 if north_side else 0
            r_lev = rows[north_side, NT:NT + 8, :]
            r_in = rows_out[1 - north_side, NT:NT + 8, :]
            r_out = rows[2 + north_side, NT:NT + 8, :]
            r_e, r_w = turn(r_lev, lroll(bcast(corner[8 + at:9 + at, :]), 65))
            k_row = (row + 8 * octet).astype(F32)
            z = flow_rows[octet, base:base + 8, :]
            m = flow_rows[octet, base + 8:base + 16, :]
            _, zw = turn(z, corner_of(flow_cols[8:16, :], at, octet * 8))
            lim_in, lim_out = jnp.minimum(r_lev, r_in), jnp.minimum(r_lev, r_out)
            if north_side:
                fn, fs = face(k_row, lim_out, m), face(k_row, lim_in, flow_rows_out[octet, 8:16, :])
            else:
                fn, fs = face(k_row, lim_in, m), face(k_row, lim_out, flow_rows[octet, 16:24, :])
            c = coefficients(face(k_row, jnp.minimum(r_lev, r_e), z), face(k_row, jnp.minimum(r_lev, r_w), zw), fn, fs)
            for f in range(NF):
                a = slice(f * K + octet * 8, f * K + octet * 8 + 8)
                q, inner, outer = rows[north_side, a, :], rows_out[1 - north_side, a, :], rows[2 + north_side, a, :]
                qe, qw = turned[north_side, 0, a, :], turned[north_side, 1, a, :]
                qn, qs = (outer, inner) if north_side else (inner, outer)
                ring_rows[north_side, a, :] = combine(c, q, qe, qw, qn, qs)

        def advance(octet, k, carry):
            level = lax.convert_element_type(k, F32)
            z, m = zm[tile(k), :], zm[tile(K + k), :]
            side = lroll(flow_cols[0:8, :], 2 * k + 1)
            zw = jnp.where(first_lane, side, lroll(z, 1))
            ms = jnp.where(first_row, bcast(flow_rows[octet, pl.ds(k + 8 - octet * 8, 1), :]), sroll(m, 1))
            fe, fw, fn, fs = face(level, lim_e, z), face(level, lim_w, zw), face(level, lim_n, m), face(level, lim_s, ms)
            div[tile(k), :] = (fe - fw) + (fn - fs)
            c = coefficients(fe, fw, fn, fs)
            for f in range(NF):
                q = x[tile(f * K + k), :]
                q = combine(c, q, *(shifted[i, tile(f * K + k), :] for i in range(4)))
                q = combine(c, q, *neighbours(q, f, k, ring_cols, ring_rows.at[0], ring_rows.at[1]))
                rhs[tile(f * K + k), :] = q
            return carry

        for octet in range(2):
            @pl.when(has_s)
            def _(octet=octet):
                flow_s(octet).wait_recv()

            @pl.when(has_n)
            def _(octet=octet):
                flow_n(octet).wait_recv()

            ring_of(0, octet)
            ring_of(1, octet)
            lax.fori_loop(octet * 8, octet * 8 + 8, functools.partial(advance, octet), 0, unroll=4)

        send_diff(1).wait_recv()

        @pl.when(passes_on)
        def _():
            send_diff(peer, True).start()


        def eliminate(i, carry):
            total, up_below, down_below, ratio_below, below = carry
            k = K - 1 - i
            total = total + div[tile(k), :]
            kappa = diff[tile(k), :]
            vertical = jnp.where(k > 0, -total, 0.0)
            up = jnp.maximum(vertical, 0.0) + kappa
            down = jnp.minimum(vertical, 0.0) - kappa
            inverse = 1.0 / ((1.0 + (up - down_below)) + up_below * ratio_below)
            here = down * inverse
            ratio[tile(k), :] = here
            values = []
            for f in range(NF):
                value = (rhs[tile(f * K + k), :] + up_below * below[f]) * inverse
                rhs[tile(f * K + k), :] = value
                values.append(value)
            return total, up, down, here, tuple(values)

        lax.fori_loop(0, K, eliminate, (zero,) * 4 + ((zero,) * NF,), unroll=4)

        def settle(k, above):
            level = lax.convert_element_type(k, F32)
            here = ratio[tile(k), :]
            values = []
            for f in range(NF):
                value = rhs[tile(f * K + k), :] - here * above[f]
                out[tile(f * K + k), :] = face(level, lev, value)
                values.append(value)
            return tuple(values)

        lax.fori_loop(0, K, settle, (zero,) * NF, unroll=4)

    from_w.wait_send()
    from_e.wait_send()

    @pl.when(has_n)
    def _():
        near_s.wait_send()
        edge_s.wait_send()

    @pl.when(has_s)
    def _():
        near_n.wait_send()
        edge_n.wait_send()

    @pl.when(has_n & (sect != 0))
    def _():
        for copy in (far_s, flow_s(0), flow_s(1)):
            copy.wait_send()

    @pl.when(has_s & (sect != 0))
    def _():
        for copy in (far_n, flow_n(0), flow_n(1)):
            copy.wait_send()

    @pl.when(sect == 0)
    def _():
        @pl.when(held)
        def _():
            to_tracers(wait_send, (1, 2), *chunks)

        to_tracers(wait_send, (1, 2), send_cols, send_diff)

    @pl.when(passes_on)
    def _():
        for make in (*chunks, send_cols, send_diff):
            make(peer, True).wait_send()


def solution(mesh):
    n_sect, n_lon, n_lat = (mesh.shape[a] for a in ("sect", "lon", "lat"))

    def on_device(fields, levels):
        vmem = pltpu.VMEM
        result = pl.pallas_call(
            functools.partial(kernel, n_sect, n_lon, n_lat),
            out_shape=pltpu.VMEM((NT * 8, 128), F32),
            in_specs=[pl.BlockSpec(memory_space=pl.ANY)] * 2,
            out_specs=pl.BlockSpec(memory_space=pltpu.VMEM),
            scratch_shapes=[
                vmem((NT * 8, 128), F32),
                vmem((8, 128), jnp.int32),
                vmem((32, 128), F32),
                vmem((32, 128), F32),
                vmem((32, 128), F32),
                vmem((4, N_ROW, 128), F32),
                vmem((4, N_ROW, 128), F32),
                vmem((16, 128), F32),
                vmem((16, 128), F32),
                vmem((16, 128), F32),
                vmem((16, 128), F32),
                vmem((2 * K * 8, 128), F32),
                vmem((2, 40, 128), F32),
                vmem((2, 40, 128), F32),
                vmem((16, 128), F32),
                vmem((16, 128), F32),
                vmem((K * 8, 128), F32),
                vmem((NT * 8, 128), F32),
                vmem((K * 8, 128), F32),
                vmem((K * 8, 128), F32),
                vmem((16, 128), F32),
                vmem((2, NT, 128), F32),
                vmem((4, NT * 8, 128), F32),
                vmem((2, 2, NT, 128), F32),
                pltpu.SemaphoreType.DMA((2,)),
                pltpu.SemaphoreType.DMA((N_HALO,)),
                pltpu.SemaphoreType.DMA((N_HALO,)),
                pltpu.SemaphoreType.DMA((n_sect - 1, N_Z)),
                pltpu.SemaphoreType.DMA((N_Z,)),
                pltpu.SemaphoreType.REGULAR((7,)),
            ],
            compiler_params=pltpu.CompilerParams(collective_id=0, has_side_effects=True),
        )(fields.reshape(NT * 8, 128), levels)
        return result.reshape(1, NF, K, 8, 128)

    return jax.shard_map(
        on_device,
        mesh=mesh,
        in_specs=(P("sect", None, None, "lat", "lon"), P("lat", "lon")),
        out_specs=P("sect", None, None, "lat", "lon"),
        check_vma=False,
    )
```

```python
import functools

import jax
import jax.numpy as jnp
from jax import lax
from jax.experimental import pallas as pl
from jax.experimental.pallas import tpu as pltpu
from jax.sharding import PartitionSpec as P

MESH = pl.DeviceIdType.MESH
F32 = jnp.float32
K = 16
NF = 6
NT = NF * K
SUB = 0.5
N_ROW = NT + 8

(R_COL_W, R_COL_E, R_NEAR_S, R_NEAR_N, R_FAR_S, R_FAR_N, R_CORNER_S, R_CORNER_N, R_FLOW_S, R_FLOW_N) = (*range(8), 8, 10)
N_HALO = 12
CH = 2
NC = K // CH
Z_COL, Z_DIFF = 2 * NC, 2 * NC + 1
N_Z = 2 * NC + 2
DEPTH = 4
VIA_FIRST = 2
VIA_SECOND = 3
(E, W, N, S, FIRST, SECOND, GO) = range(7)
MID = 2


def tile(t):
    return pl.ds(pl.multiple_of(t * 8, 8), 8)


def lroll(x, amount):
    return pltpu.roll(x, amount, 1)


def sroll(x, amount):
    return pltpu.roll(x, amount, 0)


def face(level, limit, speed):
    return jnp.where(level < limit, speed, 0.0)


def coefficients(fe, fw, fn, fs):
    ce = -SUB * jnp.minimum(fe, 0.0)
    cw = SUB * jnp.maximum(fw, 0.0)
    cn = -SUB * jnp.minimum(fn, 0.0)
    cs = SUB * jnp.maximum(fs, 0.0)
    out = (jnp.maximum(fe, 0.0) - jnp.minimum(fw, 0.0)) + (jnp.maximum(fn, 0.0) - jnp.minimum(fs, 0.0))
    return 1.0 - SUB * out, ce, cw, cn, cs


def combine(c, q, qe, qw, qn, qs):
    c0, ce, cw, cn, cs = c
    return (c0 * q + (ce * qe + cw * qw)) + (cn * qn + cs * qs)


def kernel(n_sect, n_lon, n_lat, x_hbm, lev_hbm, out,
           x, lev_ref, cols, cols_w, cols_e, rows_out, rows, near, far, corner_s, corner_n,
           zm, flow_rows, flow_rows_out, flow_cols, flow_cols_out, diff, rhs, div, ratio, ring_cols, ring_rows, shifted, turned,
           in_sem, send_sem, recv_sem, zsend_sem, zrecv_sem, ready):
    sect = lax.axis_index("sect")
    lon = lax.axis_index("lon")
    lat = lax.axis_index("lat")
    east = lax.rem(lon + 1, n_lon)
    west = lax.rem(lon + n_lon - 1, n_lon)
    has_s = lat > 0
    has_n = lat < n_lat - 1

    place = lax.rem(lon // 2, DEPTH)
    to_first, to_second = place < VIA_SECOND, place >= VIA_FIRST
    onward = (sect == 1) & jnp.logical_not(to_second)
    passes_on = onward | ((sect == 2) & jnp.logical_not(to_first))
    paired = jnp.logical_not(to_first & to_second)

    run, half = 2 * DEPTH, n_lat // 2
    end, head = lax.rem(lon, run) == run - 1, lax.rem(lon, run) == 0
    to = ({"lon": east}, {"lon": west}, {"lat": lat + 1}, {"lat": lat - 1}, {"sect": 1}, {"sect": 2})
    announces = (jnp.logical_not(end), head, has_n & ((lat < half) | (lat == n_lat - 2)), has_s & ((lat > half) | (lat == 1)),
                 (sect == 0) & to_first, ((sect == 0) & to_second) | ((sect == 1) & paired))
    hears = (end, jnp.logical_not(head), has_n & ((lat >= half) | (lat == 0)), has_s & ((lat <= half) | (lat == n_lat - 1)))
    hears_sect = ((sect == 1) & to_first, (sect == 2) & to_second, (sect == 2) & paired)

    def signal(sem, where):
        pl.semaphore_signal(sem, inc=1, device_id=where, device_id_type=MESH)

    mid = (sect == 0) & (place == MID)
    held = (sect == 0) & (place != MID)

    barrier = pltpu.get_barrier_semaphore()

    @pl.when(held)
    def _():
        signal(barrier, {"lon": lon + 2 * (MID - place)})

    for side in range(6):
        @pl.when(announces[side])
        def _(side=side):
            signal(barrier, to[side])

    load = pltpu.make_async_copy(x_hbm, x, in_sem.at[0])
    load.start()
    load_lev = pltpu.make_async_copy(lev_hbm, lev_ref, in_sem.at[1])
    load_lev.start()

    lane = lax.broadcasted_iota(jnp.int32, (8, 128), 1)
    row = lax.broadcasted_iota(jnp.int32, (8, 128), 0)
    even = (lane & 1) == 0
    pair = 63 - (lane >> 1)
    pair_b = 63 - (jnp.where(even, (lane + 126) >> 1, (lane + 1) >> 1) & 63)
    first_lane, last_lane = lane == 0, lane == 127
    first_row, last_row = row == 0, row == 7
    zero = jnp.zeros((8, 128), F32)

    def bcast(value):
        return jnp.broadcast_to(value, (8, 128))

    pl.semaphore_wait(barrier, sum(heard.astype(jnp.int32) for heard in hears + hears_sect) + jnp.where(mid, DEPTH - 1, 0))
    for side, back in ((E, W), (W, E), (N, S), (S, N)):
        @pl.when(hears[side])
        def _(side=side, back=back):
            signal(ready.at[back], to[side])

    for heard, slot, lower in ((hears_sect[0], FIRST, 0), (hears_sect[1], SECOND, 0),
                               ((sect == 2) & jnp.logical_not(to_second), SECOND, 1)):
        @pl.when(heard)
        def _(slot=slot, lower=lower):
            signal(ready.at[slot], {"sect": lower})

    def await_ready(side, only=True):
        @pl.when(announces[side] & only)
        def _():
            pl.semaphore_wait(ready.at[side], 1)

    @pl.when(jnp.logical_not(has_s))
    def _():
        rows[0] = jnp.zeros((N_ROW, 128), F32)
        rows[2] = jnp.zeros((N_ROW, 128), F32)
        corner_s[...] = jnp.zeros((16, 128), F32)
        flow_rows[:, 0:24, :] = jnp.zeros((2, 24, 128), F32)

    @pl.when(jnp.logical_not(has_n))
    def _():
        rows[1] = jnp.zeros((N_ROW, 128), F32)
        rows[3] = jnp.zeros((N_ROW, 128), F32)
        corner_n[...] = jnp.zeros((16, 128), F32)
        flow_rows[:, 24:40, :] = jnp.zeros((2, 16, 128), F32)

    load_lev.wait()
    load.wait()
    lev = lev_ref[...].astype(F32)

    def pack(acc, value, turn, p):
        a, b = acc
        turned = lroll(value, turn)
        return jnp.where(pair == p, turned, a), jnp.where(pair_b == p, turned, b)

    def pack_level(k, carry):
        a0, a1, b0, b1 = carry
        for f in range(NF):
            p = (f % 4) * K + k
            value = x[tile(f * K + k), :]
            if f < 4:
                a0, b0 = pack((a0, b0), value, 127 - 2 * p, p)
            else:
                a1, b1 = pack((a1, b1), value, 127 - 2 * p, p)
        return a0, a1, b0, b1

    a0, a1, b0, b1 = lax.fori_loop(0, K, pack_level, (zero,) * 4, unroll=4)
    a1, b1 = pack((a1, b1), lev, 63, 32)
    for i, value in enumerate((a0, a1, b0, b1)):
        cols[i * 8:i * 8 + 8, :] = value

    def pack_rows(u, carry):
        for i, r in enumerate((7, 0, 6, 1)):
            rows_out[i, tile(u), :] = x[pl.ds(u * 64 + r, 8, stride=8), :]
        return carry

    lax.fori_loop(0, NT // 8, pack_rows, 0, unroll=4)
    for i, r in enumerate((7, 0, 6, 1)):
        rows_out[i, NT:NT + 8, :] = bcast(lev[r:r + 1, :])

    def remote(src, dst, send, recv, to):
        return pltpu.make_async_remote_copy(src_ref=src, dst_ref=dst, send_sem=send, recv_sem=recv, device_id=to,
                                            device_id_type=MESH)

    def halo(src, dst, slot, to):
        return remote(src, dst, send_sem.at[slot], recv_sem.at[slot], to)

    south, north = {"lat": lat - 1}, {"lat": lat + 1}
    from_w = halo(cols, cols_w, R_COL_W, {"lon": east})
    from_e = halo(cols, cols_e, R_COL_E, {"lon": west})
    near_s = halo(rows_out.at[0], rows.at[0], R_NEAR_S, north)
    near_n = halo(rows_out.at[1], rows.at[1], R_NEAR_N, south)
    far_s = halo(rows_out.at[2], rows.at[2], R_FAR_S, north)
    far_n = halo(rows_out.at[3], rows.at[3], R_FAR_N, south)
    edge_s = halo(near, corner_s, R_CORNER_S, north)
    edge_n = halo(near, corner_n, R_CORNER_N, south)

    def flow_s(octet):
        return halo(flow_rows_out.at[octet, 0:24], flow_rows.at[octet, 0:24], R_FLOW_S + octet, north)

    def flow_n(octet):
        return halo(flow_rows_out.at[octet, 24:40], flow_rows.at[octet, 24:40], R_FLOW_N + octet, south)

    def across(src, dst, slot, peer):
        return remote(src, dst, zsend_sem.at[slot], zrecv_sem.at[slot], {"sect": peer})

    def rows_of(ref, start, size):
        return ref.at[pl.ds(pl.multiple_of(start * 8, 8), size * 8)]

    peer = 3 - sect

    def chunk(field, c, target, relayed=False):
        part = field * K + c * CH
        slot = field * NC + c
        src = rows_of(zm if relayed else x_hbm, part, CH)
        return remote(src, rows_of(zm, part, CH), zsend_sem.at[0 if relayed else target - 1, slot], zrecv_sem.at[slot],
                      {"sect": target})

    def send_cols(target, relayed=False):
        return remote(flow_cols if relayed else flow_cols_out, flow_cols, zsend_sem.at[0 if relayed else target - 1, Z_COL],
                      zrecv_sem.at[Z_COL], {"sect": target})

    def send_diff(target, relayed=False):
        return remote(diff, diff, zsend_sem.at[0 if relayed else target - 1, Z_DIFF], zrecv_sem.at[Z_DIFF], {"sect": target})

    def to_tracers(act, targets, *copies):
        for target in targets:
            @pl.when((to_first, to_second)[target - 1])
            def _(target=target):
                for make in copies:
                    act(make(target))

    def start(copy):
        copy.start()

    def wait_send(copy):
        copy.wait_send()

    chunks = [functools.partial(chunk, field, c) for c in range(NC) for field in range(2)]

    await_ready(E)
    from_w.start()
    await_ready(W)
    from_e.start()
    await_ready(N)
    await_ready(S)

    @pl.when(has_n)
    def _():
        near_s.start()

    @pl.when(has_s)
    def _():
        near_n.start()

    @pl.when(sect == 0)
    def _():
        await_ready(FIRST)
        to_tracers(start, (1,), *chunks)

    @pl.when(has_n & (sect != 0))
    def _():
        far_s.start()

    @pl.when(has_s & (sect != 0))
    def _():
        far_n.start()

    await_ready(SECOND, onward)

    @pl.when(passes_on)
    def _():
        for make in chunks:
            make(peer, True).wait_recv()
            make(peer, True).start()

    from_w.wait_recv()
    from_e.wait_recv()
    for v in range(2):
        a, b = slice(v * 8, v * 8 + 8), slice(16 + v * 8, 24 + v * 8)
        near[a, :] = jnp.where(even, lroll(cols_e[a, :], 127), lroll(cols_w[a, :], 1))
        far[a, :] = jnp.where(even, lroll(cols_e[b, :], 126), lroll(cols_w[b, :], 2))

    @pl.when(has_n)
    def _():
        edge_s.start()

    @pl.when(has_s)
    def _():
        edge_n.start()

    @pl.when(has_s)
    def _():
        near_s.wait_recv()

    @pl.when(has_n)
    def _():
        near_n.wait_recv()

    def neighbours(q, f, k, columns, south_ref, north_ref):
        v = (f // 4) * 8
        p = (f % 4) * K + k
        side = lroll(columns[v:v + 8, :], 2 * p + 1)
        return (
            jnp.where(last_lane, side, lroll(q, 127)),
            jnp.where(first_lane, side, lroll(q, 1)),
            jnp.where(last_row, bcast(north_ref[pl.ds(f * K + k, 1), :]), sroll(q, 7)),
            jnp.where(first_row, bcast(south_ref[pl.ds(f * K + k, 1), :]), sroll(q, 1)),
        )

    side = lroll(near[8:16, :], 65)
    lev_e = jnp.where(last_lane, side, lroll(lev, 127))
    lev_w = jnp.where(first_lane, side, lroll(lev, 1))
    lev_n = jnp.where(last_row, rows[1, NT:NT + 8, :], sroll(lev, 7))
    lev_s = jnp.where(first_row, rows[0, NT:NT + 8, :], sroll(lev, 1))
    lim_e, lim_w = jnp.minimum(lev, lev_e), jnp.minimum(lev, lev_w)
    lim_n, lim_s = jnp.minimum(lev, lev_n), jnp.minimum(lev, lev_s)

    @pl.when(sect == 0)
    def _():
        def around(f, k):
            q = x[tile(f * K + k), :]
            return q, neighbours(q, f, k, near, rows.at[0], rows.at[1])

        def conductances(k, level):
            v, (ve, vw, vn, vs) = around(4, k)
            return (face(level, lim_e, 0.5 * (v + ve)), face(level, lim_w, 0.5 * (vw + v)),
                    face(level, lim_n, 0.5 * (v + vn)), face(level, lim_s, 0.5 * (vs + v)))

        def diffuse(c, q, sides):
            ce, cw, cn, cs = c
            qe, qw, qn, qs = sides
            return ce * (qe - q) - cw * (q - qw) + cn * (qn - q) - cs * (q - qs)

        def warm(k, above):
            level = lax.convert_element_type(k, F32)
            c = conductances(k, level)
            t, sides = around(2, k)
            new = t + diffuse(c, t, sides)
            out[tile(2 * K + k), :] = new
            jump = 0.2 * (above - new)
            wet = jnp.where((level < lev) & (k > 0), x[tile(5 * K + k), :], 0.0)
            mixing = wet * (1.0 + 4.0 / (1.0 + jump * jump))
            out[tile(5 * K + k), :] = mixing
            diff[tile(k), :] = mixing
            return new

        lax.fori_loop(0, K, warm, zero, unroll=4)

        @pl.when(has_s)
        def _():
            edge_s.wait_recv()

        @pl.when(has_n)
        def _():
            edge_n.wait_recv()

        flow_cols_out[0:8, :] = jnp.where(
            lane >= 64, near[0:8, :], jnp.where(lane >= 32, lroll(far[0:8, :], 64), lroll(cols[0:8, :], 32)))
        flow_cols_out[8:16, :] = jnp.where(first_row, corner_n[0:8, :], corner_s[0:8, :])
        to_tracers(start, (1,), send_cols)
        await_ready(SECOND)
        to_tracers(start, (2,), *chunks, send_cols)

        def move(k, sums):
            level = lax.convert_element_type(k, F32)
            c = conductances(k, level)
            z, zs = around(0, k)
            m, ms = around(1, k)
            t, ts = around(2, k)
            s, ss = around(3, k)
            out[tile(3 * K + k), :] = s + diffuse(c, s, ss)
            here, at_e, at_n = sums

            def add(total, limit, sal, tem):
                return total + jnp.where(level < limit, 0.15 * sal - 0.2 * tem, 0.0)

            here = add(here, lev, s, t)
            at_e = add(at_e, lev_e, ss[0], ts[0])
            at_n = add(at_n, lev_n, ss[2], ts[2])
            new_z = z + (diffuse(c, z, zs) + 0.3 * m - 0.05 * (at_e - here))
            new_m = m + (diffuse(c, m, ms) - 0.3 * z - 0.05 * (at_n - here))
            out[tile(k), :] = face(level, lim_e, new_z)
            out[tile(K + k), :] = face(level, lim_n, new_m)
            div[tile(k), :] = (face(level, lim_e, z) - face(level, lim_w, zs[1])) + (
                face(level, lim_n, m) - face(level, lim_s, ms[3]))
            return here, at_e, at_n

        lax.fori_loop(0, K, move, (zero,) * 3, unroll=2)

        def rise(i, total):
            k = K - 1 - i
            total = total + div[tile(k), :]
            out[tile(4 * K + k), :] = jnp.where(k > 0, -total, 0.0)
            return total

        lax.fori_loop(0, K, rise, zero, unroll=4)

        @pl.when(mid)
        def _():
            for target, others in ((1, range(MID)), (2, range(MID + 1, DEPTH))):
                for make in chunks:
                    make(target).wait_send()
                for other in others:
                    signal(ready.at[GO], {"lon": lon + 2 * (other - MID)})

        pl.semaphore_wait(ready.at[GO], 1)
        to_tracers(start, (1, 2), send_diff)

        @pl.when(place == 0)
        def _():
            send_diff(1).wait_send()
            signal(ready.at[GO], {"lon": lon + 2 * MID})

    @pl.when(sect != 0)
    def _():
        def corner_of(value, at, p):
            return pltpu.roll(bcast(value[at:at + 1, :]), 2 * p + 1, 1, stride=2, stride_axis=0)

        def turn(value, corner):
            return jnp.where(last_lane, corner, lroll(value, 127)), jnp.where(first_lane, corner, lroll(value, 1))

        def shift(k, carry):
            for f in range(NF):
                q = x[tile(f * K + k), :]
                for i, value in enumerate(neighbours(q, f, k, near, rows.at[0], rows.at[1])):
                    shifted[i, tile(f * K + k), :] = value
            return carry

        lax.fori_loop(0, K, shift, 0, unroll=2)

        def share_rows(octet):
            @pl.when(jnp.logical_not(passes_on))
            def _():
                for make in chunks[octet * NC:(octet + 1) * NC]:
                    make(1).wait_recv()

            for i, (field, r) in enumerate(((0, 7), (1, 7), (1, 6), (0, 0), (1, 0))):
                flow_rows_out[octet, i * 8:i * 8 + 8, :] = zm[pl.ds((field * K + octet * 8) * 8 + r, 8, stride=8), :]

            @pl.when(has_n)
            def _():
                flow_s(octet).start()

            @pl.when(has_s)
            def _():
                flow_n(octet).start()

        share_rows(0)
        share_rows(1)
        @pl.when(has_s)
        def _():
            far_s.wait_recv()
            edge_s.wait_recv()

        @pl.when(has_n)
        def _():
            far_n.wait_recv()
            edge_n.wait_recv()

        for north_side in range(2):
            corner = corner_n if north_side else corner_s
            for u in range(NT // 8):
                v, p, a = u // 8, (u * 8) % 64, slice(u * 8, u * 8 + 8)
                qe, qw = turn(rows[north_side, a, :], corner_of(corner[v * 8:v * 8 + 8, :], 0 if north_side else 7, p))
                turned[north_side, 0, a, :] = qe
                turned[north_side, 1, a, :] = qw

        send_cols(1).wait_recv()

        @pl.when(passes_on)
        def _():
            send_cols(peer, True).start()


        p1_lev = jnp.where(even, bcast(near[8:16, 62:63]), bcast(near[8:16, 63:64]))
        p2_lev = jnp.where(even, bcast(far[8:16, 62:63]), bcast(far[8:16, 63:64]))
        p0_lev = jnp.where(even, bcast(cols[8:16, 62:63]), bcast(cols[8:16, 63:64]))
        cs_lev = jnp.where(even, bcast(corner_s[8:16, 62:63]), bcast(corner_s[8:16, 63:64]))
        cn_lev = jnp.where(even, bcast(corner_n[8:16, 62:63]), bcast(corner_n[8:16, 63:64]))

        def up_one(value, beyond):
            return jnp.where(last_row, sroll(beyond, 7), sroll(value, 7))

        def down_one(value, beyond):
            return jnp.where(first_row, sroll(beyond, 1), sroll(value, 1))

        def repeat(value, offset):
            if offset:
                value = lroll(value, offset)
            value = jnp.where(lane >= 96, value, 0.0)
            value = value + lroll(value, 32)
            return value + lroll(value, 64)

        p1_z, p1_m, p2_z, p0_z = (repeat(flow_cols[0:8, :], offset) for offset in (0, 32, 64, 96))
        corner_m = repeat(flow_cols[8:16, :], 32)
        k_lane = (pair & (K - 1)).astype(F32)
        lim = functools.partial(jnp.minimum, p1_lev)
        c = coefficients(
            face(k_lane, lim(jnp.where(even, p2_lev, p0_lev)), p1_z),
            face(k_lane, lim(jnp.where(even, p0_lev, p2_lev)), jnp.where(even, p0_z, p2_z)),
            face(k_lane, lim(up_one(p1_lev, cn_lev)), p1_m),
            face(k_lane, lim(down_one(p1_lev, cs_lev)), down_one(p1_m, corner_m)),
        )
        for v in range(2):
            a = slice(v * 8, v * 8 + 8)
            p0, p1, p2 = cols[a, :], near[a, :], far[a, :]
            ring_cols[a, :] = combine(c, p1, jnp.where(even, p2, p0), jnp.where(even, p0, p2),
                                      up_one(p1, corner_n[a, :]), down_one(p1, corner_s[a, :]))

        def ring_of(north_side, octet):
            at = 0 if north_side else 7
            corner = corner_n if north_side else corner_s
            base = 24 if north_side else 0
            r_lev = rows[north_side, NT:NT + 8, :]
            r_in = rows_out[1 - north_side, NT:NT + 8, :]
            r_out = rows[2 + north_side, NT:NT + 8, :]
            r_e, r_w = turn(r_lev, lroll(bcast(corner[8 + at:9 + at, :]), 65))
            k_row = (row + 8 * octet).astype(F32)
            z = flow_rows[octet, base:base + 8, :]
            m = flow_rows[octet, base + 8:base + 16, :]
            _, zw = turn(z, corner_of(flow_cols[8:16, :], at, octet * 8))
            lim_in, lim_out = jnp.minimum(r_lev, r_in), jnp.minimum(r_lev, r_out)
            if north_side:
                fn, fs = face(k_row, lim_out, m), face(k_row, lim_in, flow_rows_out[octet, 8:16, :])
            else:
                fn, fs = face(k_row, lim_in, m), face(k_row, lim_out, flow_rows[octet, 16:24, :])
            c = coefficients(face(k_row, jnp.minimum(r_lev, r_e), z), face(k_row, jnp.minimum(r_lev, r_w), zw), fn, fs)
            for f in range(NF):
                a = slice(f * K + octet * 8, f * K + octet * 8 + 8)
                q, inner, outer = rows[north_side, a, :], rows_out[1 - north_side, a, :], rows[2 + north_side, a, :]
                qe, qw = turned[north_side, 0, a, :], turned[north_side, 1, a, :]
                qn, qs = (outer, inner) if north_side else (inner, outer)
                ring_rows[north_side, a, :] = combine(c, q, qe, qw, qn, qs)

        def advance(octet, k, carry):
            level = lax.convert_element_type(k, F32)
            z, m = zm[tile(k), :], zm[tile(K + k), :]
            side = lroll(flow_cols[0:8, :], 2 * k + 1)
            zw = jnp.where(first_lane, side, lroll(z, 1))
            ms = jnp.where(first_row, bcast(flow_rows[octet, pl.ds(k + 8 - octet * 8, 1), :]), sroll(m, 1))
            fe, fw, fn, fs = face(level, lim_e, z), face(level, lim_w, zw), face(level, lim_n, m), face(level, lim_s, ms)
            div[tile(k), :] = (fe - fw) + (fn - fs)
            c = coefficients(fe, fw, fn, fs)
            for f in range(NF):
                q = x[tile(f * K + k), :]
                q = combine(c, q, *(shifted[i, tile(f * K + k), :] for i in range(4)))
                q = combine(c, q, *neighbours(q, f, k, ring_cols, ring_rows.at[0], ring_rows.at[1]))
                rhs[tile(f * K + k), :] = q
            return carry

        for octet in range(2):
            @pl.when(has_s)
            def _(octet=octet):
                flow_s(octet).wait_recv()

            @pl.when(has_n)
            def _(octet=octet):
                flow_n(octet).wait_recv()

            ring_of(0, octet)
            ring_of(1, octet)
            lax.fori_loop(octet * 8, octet * 8 + 8, functools.partial(advance, octet), 0, unroll=4)

        send_diff(1).wait_recv()

        @pl.when(passes_on)
        def _():
            send_diff(peer, True).start()


        def eliminate(i, carry):
            total, up_below, down_below, ratio_below, below = carry
            k = K - 1 - i
            total = total + div[tile(k), :]
            kappa = diff[tile(k), :]
            vertical = jnp.where(k > 0, -total, 0.0)
            up = jnp.maximum(vertical, 0.0) + kappa
            down = jnp.minimum(vertical, 0.0) - kappa
            inverse = 1.0 / ((1.0 + (up - down_below)) + up_below * ratio_below)
            here = down * inverse
            ratio[tile(k), :] = here
            values = []
            for f in range(NF):
                value = (rhs[tile(f * K + k), :] + up_below * below[f]) * inverse
                rhs[tile(f * K + k), :] = value
                values.append(value)
            return total, up, down, here, tuple(values)

        lax.fori_loop(0, K, eliminate, (zero,) * 4 + ((zero,) * NF,), unroll=4)

        def settle(k, above):
            level = lax.convert_element_type(k, F32)
            here = ratio[tile(k), :]
            values = []
            for f in range(NF):
                value = rhs[tile(f * K + k), :] - here * above[f]
                out[tile(f * K + k), :] = face(level, lev, value)
                values.append(value)
            return tuple(values)

        lax.fori_loop(0, K, settle, (zero,) * NF, unroll=4)

    from_w.wait_send()
    from_e.wait_send()

    @pl.when(has_n)
    def _():
        near_s.wait_send()
        edge_s.wait_send()

    @pl.when(has_s)
    def _():
        near_n.wait_send()
        edge_n.wait_send()

    @pl.when(has_n & (sect != 0))
    def _():
        for copy in (far_s, flow_s(0), flow_s(1)):
            copy.wait_send()

    @pl.when(has_s & (sect != 0))
    def _():
        for copy in (far_n, flow_n(0), flow_n(1)):
            copy.wait_send()

    @pl.when(sect == 0)
    def _():
        @pl.when(held)
        def _():
            to_tracers(wait_send, (1, 2), *chunks)

        to_tracers(wait_send, (1, 2), send_cols)

        @pl.when(place != 0)
        def _():
            to_tracers(wait_send, (1, 2), send_diff)

    @pl.when(passes_on)
    def _():
        for make in (*chunks, send_cols, send_diff):
            make(peer, True).wait_send()


def solution(mesh):
    n_sect, n_lon, n_lat = (mesh.shape[a] for a in ("sect", "lon", "lat"))

    def on_device(fields, levels):
        vmem = pltpu.VMEM
        result = pl.pallas_call(
            functools.partial(kernel, n_sect, n_lon, n_lat),
            out_shape=pltpu.VMEM((NT * 8, 128), F32),
            in_specs=[pl.BlockSpec(memory_space=pl.ANY)] * 2,
            out_specs=pl.BlockSpec(memory_space=pltpu.VMEM),
            scratch_shapes=[
                vmem((NT * 8, 128), F32),
                vmem((8, 128), jnp.int32),
                vmem((32, 128), F32),
                vmem((32, 128), F32),
                vmem((32, 128), F32),
                vmem((4, N_ROW, 128), F32),
                vmem((4, N_ROW, 128), F32),
                vmem((16, 128), F32),
                vmem((16, 128), F32),
                vmem((16, 128), F32),
                vmem((16, 128), F32),
                vmem((2 * K * 8, 128), F32),
                vmem((2, 40, 128), F32),
                vmem((2, 40, 128), F32),
                vmem((16, 128), F32),
                vmem((16, 128), F32),
                vmem((K * 8, 128), F32),
                vmem((NT * 8, 128), F32),
                vmem((K * 8, 128), F32),
                vmem((K * 8, 128), F32),
                vmem((16, 128), F32),
                vmem((2, NT, 128), F32),
                vmem((4, NT * 8, 128), F32),
                vmem((2, 2, NT, 128), F32),
                pltpu.SemaphoreType.DMA((2,)),
                pltpu.SemaphoreType.DMA((N_HALO,)),
                pltpu.SemaphoreType.DMA((N_HALO,)),
                pltpu.SemaphoreType.DMA((n_sect - 1, N_Z)),
                pltpu.SemaphoreType.DMA((N_Z,)),
                pltpu.SemaphoreType.REGULAR((7,)),
            ],
            compiler_params=pltpu.CompilerParams(collective_id=0, has_side_effects=True),
        )(fields.reshape(NT * 8, 128), levels)
        return result.reshape(1, NF, K, 8, 128)

    return jax.shard_map(
        on_device,
        mesh=mesh,
        in_specs=(P("sect", None, None, "lat", "lon"), P("lat", "lon")),
        out_specs=P("sect", None, None, "lat", "lon"),
        check_vma=False,
    )
```

```python
import functools

import jax
import jax.numpy as jnp
from jax import lax
from jax.experimental import pallas as pl
from jax.experimental.pallas import tpu as pltpu
from jax.sharding import PartitionSpec as P

MESH = pl.DeviceIdType.MESH
F32 = jnp.float32
K = 16
NF = 6
NT = NF * K
SUB = 0.5
N_ROW = NT + 8

(R_COL_W, R_COL_E, R_NEAR_S, R_NEAR_N, R_FAR_S, R_FAR_N, R_CORNER_S, R_CORNER_N, R_FLOW_S, R_FLOW_N) = (*range(8), 8, 10)
N_HALO = 12
CH = 4
NC = K // CH
Z_COL, Z_DIFF = 2 * NC, 2 * NC + 1
N_Z = 2 * NC + 2
DEPTH = 4
VIA_FIRST = 2
VIA_SECOND = 3
(E, W, N, S, FIRST, SECOND, GO) = range(7)
MID = 2


def tile(t):
    return pl.ds(pl.multiple_of(t * 8, 8), 8)


def lroll(x, amount):
    return pltpu.roll(x, amount, 1)


def sroll(x, amount):
    return pltpu.roll(x, amount, 0)


def face(level, limit, speed):
    return jnp.where(level < limit, speed, 0.0)


def coefficients(fe, fw, fn, fs):
    ce = -SUB * jnp.minimum(fe, 0.0)
    cw = SUB * jnp.maximum(fw, 0.0)
    cn = -SUB * jnp.minimum(fn, 0.0)
    cs = SUB * jnp.maximum(fs, 0.0)
    out = (jnp.maximum(fe, 0.0) - jnp.minimum(fw, 0.0)) + (jnp.maximum(fn, 0.0) - jnp.minimum(fs, 0.0))
    return 1.0 - SUB * out, ce, cw, cn, cs


def combine(c, q, qe, qw, qn, qs):
    c0, ce, cw, cn, cs = c
    return (c0 * q + (ce * qe + cw * qw)) + (cn * qn + cs * qs)


def kernel(n_sect, n_lon, n_lat, x_hbm, lev_hbm, out,
           x, lev_ref, cols, cols_w, cols_e, rows_out, rows, near, far, corner_s, corner_n,
           zm, flow_rows, flow_rows_out, flow_cols, flow_cols_out, diff, rhs, div, ratio, ring_cols, ring_rows, shifted, turned,
           in_sem, send_sem, recv_sem, zsend_sem, zrecv_sem, ready):
    sect = lax.axis_index("sect")
    lon = lax.axis_index("lon")
    lat = lax.axis_index("lat")
    east = lax.rem(lon + 1, n_lon)
    west = lax.rem(lon + n_lon - 1, n_lon)
    has_s = lat > 0
    has_n = lat < n_lat - 1

    place = lax.rem(lon // 2, DEPTH)
    to_first, to_second = place < VIA_SECOND, place >= VIA_FIRST
    onward = (sect == 1) & jnp.logical_not(to_second)
    back = (sect == 2) & jnp.logical_not(to_first)
    passes_on = onward | back
    paired = jnp.logical_not(to_first & to_second)

    run, half = 2 * DEPTH, n_lat // 2
    end, head = lax.rem(lon, run) == run - 1, lax.rem(lon, run) == 0
    to = ({"lon": east}, {"lon": west}, {"lat": lat + 1}, {"lat": lat - 1}, {"sect": 1}, {"sect": 2})
    announces = (jnp.logical_not(end), head, has_n & ((lat < half) | (lat == n_lat - 2)), has_s & ((lat > half) | (lat == 1)),
                 (sect == 0) & to_first, ((sect == 0) & to_second) | ((sect == 1) & paired))
    hears = (end, jnp.logical_not(head), has_n & ((lat >= half) | (lat == 0)), has_s & ((lat <= half) | (lat == n_lat - 1)))
    hears_sect = ((sect == 1) & to_first, (sect == 2) & to_second, (sect == 2) & paired)

    def signal(sem, where):
        pl.semaphore_signal(sem, inc=1, device_id=where, device_id_type=MESH)

    mid = (sect == 0) & (place == MID)
    held = (sect == 0) & (place != MID)

    barrier = pltpu.get_barrier_semaphore()

    @pl.when(held)
    def _():
        signal(barrier, {"lon": lon + 2 * (MID - place)})

    for side in range(6):
        @pl.when(announces[side])
        def _(side=side):
            signal(barrier, to[side])

    load = pltpu.make_async_copy(x_hbm, x, in_sem.at[0])
    load.start()
    load_lev = pltpu.make_async_copy(lev_hbm, lev_ref, in_sem.at[1])
    load_lev.start()

    lane = lax.broadcasted_iota(jnp.int32, (8, 128), 1)
    row = lax.broadcasted_iota(jnp.int32, (8, 128), 0)
    even = (lane & 1) == 0
    pair = 63 - (lane >> 1)
    pair_b = 63 - (jnp.where(even, (lane + 126) >> 1, (lane + 1) >> 1) & 63)
    first_lane, last_lane = lane == 0, lane == 127
    first_row, last_row = row == 0, row == 7
    zero = jnp.zeros((8, 128), F32)

    def bcast(value):
        return jnp.broadcast_to(value, (8, 128))

    pl.semaphore_wait(barrier, sum(heard.astype(jnp.int32) for heard in hears + hears_sect) + jnp.where(mid, DEPTH - 1, 0))
    for heard, slot, lower in ((hears_sect[0], FIRST, 0), (hears_sect[1], SECOND, 0),
                               ((sect == 2) & jnp.logical_not(to_second), SECOND, 1)):
        @pl.when(heard)
        def _(slot=slot, lower=lower):
            signal(ready.at[slot], {"sect": lower})

    for side, slot in ((E, W), (W, E), (N, S), (S, N)):
        @pl.when(hears[side])
        def _(side=side, slot=slot):
            signal(ready.at[slot], to[side])

    def await_ready(side, only=True):
        @pl.when(announces[side] & only)
        def _():
            pl.semaphore_wait(ready.at[side], 1)

    @pl.when(jnp.logical_not(has_s))
    def _():
        rows[0] = jnp.zeros((N_ROW, 128), F32)
        rows[2] = jnp.zeros((N_ROW, 128), F32)
        corner_s[...] = jnp.zeros((16, 128), F32)
        flow_rows[:, 0:24, :] = jnp.zeros((2, 24, 128), F32)

    @pl.when(jnp.logical_not(has_n))
    def _():
        rows[1] = jnp.zeros((N_ROW, 128), F32)
        rows[3] = jnp.zeros((N_ROW, 128), F32)
        corner_n[...] = jnp.zeros((16, 128), F32)
        flow_rows[:, 24:40, :] = jnp.zeros((2, 16, 128), F32)

    load_lev.wait()
    load.wait()
    lev = lev_ref[...].astype(F32)

    def pack(acc, value, turn, p):
        a, b = acc
        turned = lroll(value, turn)
        return jnp.where(pair == p, turned, a), jnp.where(pair_b == p, turned, b)

    def pack_level(k, carry):
        a0, a1, b0, b1 = carry
        for f in range(NF):
            p = (f % 4) * K + k
            value = x[tile(f * K + k), :]
            if f < 4:
                a0, b0 = pack((a0, b0), value, 127 - 2 * p, p)
            else:
                a1, b1 = pack((a1, b1), value, 127 - 2 * p, p)
        return a0, a1, b0, b1

    a0, a1, b0, b1 = lax.fori_loop(0, K, pack_level, (zero,) * 4, unroll=4)
    a1, b1 = pack((a1, b1), lev, 63, 32)
    for i, value in enumerate((a0, a1, b0, b1)):
        cols[i * 8:i * 8 + 8, :] = value

    def pack_rows(u, carry):
        for i, r in enumerate((7, 0, 6, 1)):
            rows_out[i, tile(u), :] = x[pl.ds(u * 64 + r, 8, stride=8), :]
        return carry

    lax.fori_loop(0, NT // 8, pack_rows, 0, unroll=4)
    for i, r in enumerate((7, 0, 6, 1)):
        rows_out[i, NT:NT + 8, :] = bcast(lev[r:r + 1, :])

    def remote(src, dst, send, recv, to):
        return pltpu.make_async_remote_copy(src_ref=src, dst_ref=dst, send_sem=send, recv_sem=recv, device_id=to,
                                            device_id_type=MESH)

    def halo(src, dst, slot, to):
        return remote(src, dst, send_sem.at[slot], recv_sem.at[slot], to)

    south, north = {"lat": lat - 1}, {"lat": lat + 1}
    from_w = halo(cols, cols_w, R_COL_W, {"lon": east})
    from_e = halo(cols, cols_e, R_COL_E, {"lon": west})
    near_s = halo(rows_out.at[0], rows.at[0], R_NEAR_S, north)
    near_n = halo(rows_out.at[1], rows.at[1], R_NEAR_N, south)
    far_s = halo(rows_out.at[2], rows.at[2], R_FAR_S, north)
    far_n = halo(rows_out.at[3], rows.at[3], R_FAR_N, south)
    edge_s = halo(near, corner_s, R_CORNER_S, north)
    edge_n = halo(near, corner_n, R_CORNER_N, south)

    def flow_s(octet):
        return halo(flow_rows_out.at[octet, 0:24], flow_rows.at[octet, 0:24], R_FLOW_S + octet, north)

    def flow_n(octet):
        return halo(flow_rows_out.at[octet, 24:40], flow_rows.at[octet, 24:40], R_FLOW_N + octet, south)

    def across(src, dst, slot, peer):
        return remote(src, dst, zsend_sem.at[slot], zrecv_sem.at[slot], {"sect": peer})

    def rows_of(ref, start, size):
        return ref.at[pl.ds(pl.multiple_of(start * 8, 8), size * 8)]

    peer = 3 - sect

    def chunk(field, c, target, relayed=False):
        part = field * K + c * CH
        slot = field * NC + c
        src = rows_of(zm if relayed else x_hbm, part, CH)
        return remote(src, rows_of(zm, part, CH), zsend_sem.at[0 if relayed else target - 1, slot], zrecv_sem.at[slot],
                      {"sect": target})

    def send_cols(target, relayed=False):
        return remote(flow_cols if relayed else flow_cols_out, flow_cols, zsend_sem.at[0 if relayed else target - 1, Z_COL],
                      zrecv_sem.at[Z_COL], {"sect": target})

    def send_diff(target, relayed=False):
        part = diff.at[8:K * 8]
        return remote(part, part, zsend_sem.at[0 if relayed else target - 1, Z_DIFF], zrecv_sem.at[Z_DIFF], {"sect": target})

    def to_tracers(act, targets, *copies):
        for target in targets:
            @pl.when((to_first, to_second)[target - 1])
            def _(target=target):
                for make in copies:
                    act(make(target))

    def start(copy):
        copy.start()

    def wait_send(copy):
        copy.wait_send()

    chunks = [functools.partial(chunk, field, c) for c in range(NC) for field in range(2)]

    await_ready(E)
    from_w.start()
    await_ready(W)
    from_e.start()
    await_ready(N)
    await_ready(S)

    @pl.when(has_n)
    def _():
        near_s.start()

    @pl.when(has_s)
    def _():
        near_n.start()

    @pl.when(sect == 0)
    def _():
        await_ready(FIRST)
        to_tracers(start, (1,), *chunks)

    @pl.when(has_n & (sect != 0))
    def _():
        far_s.start()

    @pl.when(has_s & (sect != 0))
    def _():
        far_n.start()

    @pl.when(sect != 0)
    def _():
        diff[0:8, :] = zero

    await_ready(SECOND, onward)

    @pl.when(passes_on)
    def _():
        for make in chunks:
            make(peer, True).wait_recv()
            make(peer, True).start()

    from_w.wait_recv()
    from_e.wait_recv()
    for v in range(2):
        a, b = slice(v * 8, v * 8 + 8), slice(16 + v * 8, 24 + v * 8)
        near[a, :] = jnp.where(even, lroll(cols_e[a, :], 127), lroll(cols_w[a, :], 1))
        far[a, :] = jnp.where(even, lroll(cols_e[b, :], 126), lroll(cols_w[b, :], 2))

    @pl.when(has_n)
    def _():
        edge_s.start()

    @pl.when(has_s)
    def _():
        edge_n.start()

    @pl.when(has_s)
    def _():
        near_s.wait_recv()

    @pl.when(has_n)
    def _():
        near_n.wait_recv()

    def neighbours(q, f, k, columns, south_ref, north_ref):
        v = (f // 4) * 8
        p = (f % 4) * K + k
        side = lroll(columns[v:v + 8, :], 2 * p + 1)
        return (
            jnp.where(last_lane, side, lroll(q, 127)),
            jnp.where(first_lane, side, lroll(q, 1)),
            jnp.where(last_row, bcast(north_ref[pl.ds(f * K + k, 1), :]), sroll(q, 7)),
            jnp.where(first_row, bcast(south_ref[pl.ds(f * K + k, 1), :]), sroll(q, 1)),
        )

    side = lroll(near[8:16, :], 65)
    lev_e = jnp.where(last_lane, side, lroll(lev, 127))
    lev_w = jnp.where(first_lane, side, lroll(lev, 1))
    lev_n = jnp.where(last_row, rows[1, NT:NT + 8, :], sroll(lev, 7))
    lev_s = jnp.where(first_row, rows[0, NT:NT + 8, :], sroll(lev, 1))
    lim_e, lim_w = jnp.minimum(lev, lev_e), jnp.minimum(lev, lev_w)
    lim_n, lim_s = jnp.minimum(lev, lev_n), jnp.minimum(lev, lev_s)

    @pl.when(sect == 0)
    def _():
        def around(f, k):
            q = x[tile(f * K + k), :]
            return q, neighbours(q, f, k, near, rows.at[0], rows.at[1])

        def conductances(k, level):
            v, (ve, vw, vn, vs) = around(4, k)
            return (face(level, lim_e, 0.5 * (v + ve)), face(level, lim_w, 0.5 * (vw + v)),
                    face(level, lim_n, 0.5 * (v + vn)), face(level, lim_s, 0.5 * (vs + v)))

        def diffuse(c, q, sides):
            ce, cw, cn, cs = c
            qe, qw, qn, qs = sides
            return ce * (qe - q) - cw * (q - qw) + cn * (qn - q) - cs * (q - qs)

        def warm(k, above):
            level = lax.convert_element_type(k, F32)
            c = conductances(k, level)
            t, sides = around(2, k)
            new = t + diffuse(c, t, sides)
            out[tile(2 * K + k), :] = new
            jump = 0.2 * (above - new)
            wet = jnp.where((level < lev) & (k > 0), x[tile(5 * K + k), :], 0.0)
            mixing = wet * (1.0 + 4.0 / (1.0 + jump * jump))
            out[tile(5 * K + k), :] = mixing
            diff[tile(k), :] = mixing
            return new

        lax.fori_loop(0, K, warm, zero, unroll=4)

        @pl.when(has_s)
        def _():
            edge_s.wait_recv()

        @pl.when(has_n)
        def _():
            edge_n.wait_recv()

        flow_cols_out[0:8, :] = jnp.where(
            lane >= 64, near[0:8, :], jnp.where(lane >= 32, lroll(far[0:8, :], 64), lroll(cols[0:8, :], 32)))
        flow_cols_out[8:16, :] = jnp.where(first_row, corner_n[0:8, :], corner_s[0:8, :])
        to_tracers(start, (1,), send_cols)
        await_ready(SECOND)
        to_tracers(start, (2,), send_cols, *chunks)

        def move(k, sums):
            level = lax.convert_element_type(k, F32)
            c = conductances(k, level)
            z, zs = around(0, k)
            m, ms = around(1, k)
            t, ts = around(2, k)
            s, ss = around(3, k)
            out[tile(3 * K + k), :] = s + diffuse(c, s, ss)
            here, at_e, at_n = sums

            def add(total, limit, sal, tem):
                return total + jnp.where(level < limit, 0.15 * sal - 0.2 * tem, 0.0)

            here = add(here, lev, s, t)
            at_e = add(at_e, lev_e, ss[0], ts[0])
            at_n = add(at_n, lev_n, ss[2], ts[2])
            new_z = z + (diffuse(c, z, zs) + 0.3 * m - 0.05 * (at_e - here))
            new_m = m + (diffuse(c, m, ms) - 0.3 * z - 0.05 * (at_n - here))
            out[tile(k), :] = face(level, lim_e, new_z)
            out[tile(K + k), :] = face(level, lim_n, new_m)
            div[tile(k), :] = (face(level, lim_e, z) - face(level, lim_w, zs[1])) + (
                face(level, lim_n, m) - face(level, lim_s, ms[3]))
            return here, at_e, at_n

        lax.fori_loop(0, K, move, (zero,) * 3, unroll=2)

        def rise(i, total):
            k = K - 1 - i
            total = total + div[tile(k), :]
            out[tile(4 * K + k), :] = jnp.where(k > 0, -total, 0.0)
            return total

        lax.fori_loop(0, K, rise, zero, unroll=4)

        @pl.when(mid)
        def _():
            for target, others in ((1, range(MID)), (2, range(MID + 1, DEPTH))):
                for make in chunks:
                    make(target).wait_send()
                for other in others:
                    signal(ready.at[GO], {"lon": lon + 2 * (other - MID)})

        pl.semaphore_wait(ready.at[GO], 1)
        to_tracers(start, (1, 2), send_diff)

        @pl.when(place == 0)
        def _():
            send_diff(1).wait_send()
            signal(ready.at[GO], {"lon": lon + 2 * MID})

    @pl.when(sect != 0)
    def _():
        def corner_of(value, at, p):
            return pltpu.roll(bcast(value[at:at + 1, :]), 2 * p + 1, 1, stride=2, stride_axis=0)

        def turn(value, corner):
            return jnp.where(last_lane, corner, lroll(value, 127)), jnp.where(first_lane, corner, lroll(value, 1))

        def shift(k, carry):
            for f in range(NF):
                q = x[tile(f * K + k), :]
                for i, value in enumerate(neighbours(q, f, k, near, rows.at[0], rows.at[1])):
                    shifted[i, tile(f * K + k), :] = value
            return carry

        lax.fori_loop(0, K, shift, 0, unroll=2)

        def turn_rows():
            @pl.when(has_s)
            def _():
                far_s.wait_recv()
                edge_s.wait_recv()

            @pl.when(has_n)
            def _():
                far_n.wait_recv()
                edge_n.wait_recv()

            for north_side in range(2):
                corner = corner_n if north_side else corner_s
                for u in range(NT // 8):
                    v, p, a = u // 8, (u * 8) % 64, slice(u * 8, u * 8 + 8)
                    qe, qw = turn(rows[north_side, a, :], corner_of(corner[v * 8:v * 8 + 8, :], 0 if north_side else 7, p))
                    turned[north_side, 0, a, :] = qe
                    turned[north_side, 1, a, :] = qw

        @pl.when(jnp.logical_not(passes_on))
        def _():
            turn_rows()

        def share_rows(octet):
            @pl.when(jnp.logical_not(passes_on))
            def _():
                for make in chunks[octet * NC:(octet + 1) * NC]:
                    make(1).wait_recv()

            for i, (field, r) in enumerate(((0, 7), (1, 7), (1, 6), (0, 0), (1, 0))):
                flow_rows_out[octet, i * 8:i * 8 + 8, :] = zm[pl.ds((field * K + octet * 8) * 8 + r, 8, stride=8), :]

            @pl.when(has_n)
            def _():
                flow_s(octet).start()

            @pl.when(has_s)
            def _():
                flow_n(octet).start()

        share_rows(0)
        share_rows(1)
        @pl.when(passes_on)
        def _():
            turn_rows()

        send_cols(1).wait_recv()

        @pl.when(passes_on)
        def _():
            send_cols(peer, True).start()

        @pl.when(back)
        def _():
            send_diff(peer, True).wait_recv()
            send_diff(peer, True).start()


        p1_lev = jnp.where(even, bcast(near[8:16, 62:63]), bcast(near[8:16, 63:64]))
        p2_lev = jnp.where(even, bcast(far[8:16, 62:63]), bcast(far[8:16, 63:64]))
        p0_lev = jnp.where(even, bcast(cols[8:16, 62:63]), bcast(cols[8:16, 63:64]))
        cs_lev = jnp.where(even, bcast(corner_s[8:16, 62:63]), bcast(corner_s[8:16, 63:64]))
        cn_lev = jnp.where(even, bcast(corner_n[8:16, 62:63]), bcast(corner_n[8:16, 63:64]))

        def up_one(value, beyond):
            return jnp.where(last_row, sroll(beyond, 7), sroll(value, 7))

        def down_one(value, beyond):
            return jnp.where(first_row, sroll(beyond, 1), sroll(value, 1))

        def repeat(value, offset):
            if offset:
                value = lroll(value, offset)
            value = jnp.where(lane >= 96, value, 0.0)
            value = value + lroll(value, 32)
            return value + lroll(value, 64)

        p1_z, p1_m, p2_z, p0_z = (repeat(flow_cols[0:8, :], offset) for offset in (0, 32, 64, 96))
        corner_m = repeat(flow_cols[8:16, :], 32)
        k_lane = (pair & (K - 1)).astype(F32)
        lim = functools.partial(jnp.minimum, p1_lev)
        c = coefficients(
            face(k_lane, lim(jnp.where(even, p2_lev, p0_lev)), p1_z),
            face(k_lane, lim(jnp.where(even, p0_lev, p2_lev)), jnp.where(even, p0_z, p2_z)),
            face(k_lane, lim(up_one(p1_lev, cn_lev)), p1_m),
            face(k_lane, lim(down_one(p1_lev, cs_lev)), down_one(p1_m, corner_m)),
        )
        for v in range(2):
            a = slice(v * 8, v * 8 + 8)
            p0, p1, p2 = cols[a, :], near[a, :], far[a, :]
            ring_cols[a, :] = combine(c, p1, jnp.where(even, p2, p0), jnp.where(even, p0, p2),
                                      up_one(p1, corner_n[a, :]), down_one(p1, corner_s[a, :]))

        def ring_of(north_side, octet):
            at = 0 if north_side else 7
            corner = corner_n if north_side else corner_s
            base = 24 if north_side else 0
            r_lev = rows[north_side, NT:NT + 8, :]
            r_in = rows_out[1 - north_side, NT:NT + 8, :]
            r_out = rows[2 + north_side, NT:NT + 8, :]
            r_e, r_w = turn(r_lev, lroll(bcast(corner[8 + at:9 + at, :]), 65))
            k_row = (row + 8 * octet).astype(F32)
            z = flow_rows[octet, base:base + 8, :]
            m = flow_rows[octet, base + 8:base + 16, :]
            _, zw = turn(z, corner_of(flow_cols[8:16, :], at, octet * 8))
            lim_in, lim_out = jnp.minimum(r_lev, r_in), jnp.minimum(r_lev, r_out)
            if north_side:
                fn, fs = face(k_row, lim_out, m), face(k_row, lim_in, flow_rows_out[octet, 8:16, :])
            else:
                fn, fs = face(k_row, lim_in, m), face(k_row, lim_out, flow_rows[octet, 16:24, :])
            c = coefficients(face(k_row, jnp.minimum(r_lev, r_e), z), face(k_row, jnp.minimum(r_lev, r_w), zw), fn, fs)
            for f in range(NF):
                a = slice(f * K + octet * 8, f * K + octet * 8 + 8)
                q, inner, outer = rows[north_side, a, :], rows_out[1 - north_side, a, :], rows[2 + north_side, a, :]
                qe, qw = turned[north_side, 0, a, :], turned[north_side, 1, a, :]
                qn, qs = (outer, inner) if north_side else (inner, outer)
                ring_rows[north_side, a, :] = combine(c, q, qe, qw, qn, qs)

        def advance(octet, k, carry):
            level = lax.convert_element_type(k, F32)
            z, m = zm[tile(k), :], zm[tile(K + k), :]
            side = lroll(flow_cols[0:8, :], 2 * k + 1)
            zw = jnp.where(first_lane, side, lroll(z, 1))
            ms = jnp.where(first_row, bcast(flow_rows[octet, pl.ds(k + 8 - octet * 8, 1), :]), sroll(m, 1))
            fe, fw, fn, fs = face(level, lim_e, z), face(level, lim_w, zw), face(level, lim_n, m), face(level, lim_s, ms)
            div[tile(k), :] = (fe - fw) + (fn - fs)
            c = coefficients(fe, fw, fn, fs)
            for f in range(NF):
                q = x[tile(f * K + k), :]
                q = combine(c, q, *(shifted[i, tile(f * K + k), :] for i in range(4)))
                q = combine(c, q, *neighbours(q, f, k, ring_cols, ring_rows.at[0], ring_rows.at[1]))
                rhs[tile(f * K + k), :] = q
            return carry

        for octet in range(2):
            @pl.when(has_s)
            def _(octet=octet):
                flow_s(octet).wait_recv()

            @pl.when(has_n)
            def _(octet=octet):
                flow_n(octet).wait_recv()

            ring_of(0, octet)
            ring_of(1, octet)
            lax.fori_loop(octet * 8, octet * 8 + 8, functools.partial(advance, octet), 0, unroll=4)

        @pl.when(jnp.logical_not(back))
        def _():
            send_diff(1).wait_recv()

        @pl.when(onward)
        def _():
            send_diff(peer, True).start()


        def eliminate(i, carry):
            total, up_below, down_below, ratio_below, below = carry
            k = K - 1 - i
            total = total + div[tile(k), :]
            kappa = diff[tile(k), :]
            vertical = jnp.where(k > 0, -total, 0.0)
            up = jnp.maximum(vertical, 0.0) + kappa
            down = jnp.minimum(vertical, 0.0) - kappa
            inverse = 1.0 / ((1.0 + (up - down_below)) + up_below * ratio_below)
            here = down * inverse
            ratio[tile(k), :] = here
            values = []
            for f in range(NF):
                value = (rhs[tile(f * K + k), :] + up_below * below[f]) * inverse
                rhs[tile(f * K + k), :] = value
                values.append(value)
            return total, up, down, here, tuple(values)

        lax.fori_loop(0, K, eliminate, (zero,) * 4 + ((zero,) * NF,), unroll=4)

        def settle(k, above):
            level = lax.convert_element_type(k, F32)
            here = ratio[tile(k), :]
            values = []
            for f in range(NF):
                value = rhs[tile(f * K + k), :] - here * above[f]
                out[tile(f * K + k), :] = face(level, lev, value)
                values.append(value)
            return tuple(values)

        lax.fori_loop(0, K, settle, (zero,) * NF, unroll=4)

    from_w.wait_send()
    from_e.wait_send()

    @pl.when(has_n)
    def _():
        near_s.wait_send()
        edge_s.wait_send()

    @pl.when(has_s)
    def _():
        near_n.wait_send()
        edge_n.wait_send()

    @pl.when(has_n & (sect != 0))
    def _():
        for copy in (far_s, flow_s(0), flow_s(1)):
            copy.wait_send()

    @pl.when(has_s & (sect != 0))
    def _():
        for copy in (far_n, flow_n(0), flow_n(1)):
            copy.wait_send()

    @pl.when(sect == 0)
    def _():
        @pl.when(held)
        def _():
            to_tracers(wait_send, (1, 2), *chunks)

        to_tracers(wait_send, (1, 2), send_cols)

        @pl.when(place != 0)
        def _():
            to_tracers(wait_send, (1, 2), send_diff)

    @pl.when(passes_on)
    def _():
        for make in (*chunks, send_cols, send_diff):
            make(peer, True).wait_send()


def solution(mesh):
    n_sect, n_lon, n_lat = (mesh.shape[a] for a in ("sect", "lon", "lat"))

    def on_device(fields, levels):
        vmem = pltpu.VMEM
        result = pl.pallas_call(
            functools.partial(kernel, n_sect, n_lon, n_lat),
            out_shape=pltpu.VMEM((NT * 8, 128), F32),
            in_specs=[pl.BlockSpec(memory_space=pl.ANY)] * 2,
            out_specs=pl.BlockSpec(memory_space=pltpu.VMEM),
            scratch_shapes=[
                vmem((NT * 8, 128), F32),
                vmem((8, 128), jnp.int32),
                vmem((32, 128), F32),
                vmem((32, 128), F32),
                vmem((32, 128), F32),
                vmem((4, N_ROW, 128), F32),
                vmem((4, N_ROW, 128), F32),
                vmem((16, 128), F32),
                vmem((16, 128), F32),
                vmem((16, 128), F32),
                vmem((16, 128), F32),
                vmem((2 * K * 8, 128), F32),
                vmem((2, 40, 128), F32),
                vmem((2, 40, 128), F32),
                vmem((16, 128), F32),
                vmem((16, 128), F32),
                vmem((K * 8, 128), F32),
                vmem((NT * 8, 128), F32),
                vmem((K * 8, 128), F32),
                vmem((K * 8, 128), F32),
                vmem((16, 128), F32),
                vmem((2, NT, 128), F32),
                vmem((4, NT * 8, 128), F32),
                vmem((2, 2, NT, 128), F32),
                pltpu.SemaphoreType.DMA((2,)),
                pltpu.SemaphoreType.DMA((N_HALO,)),
                pltpu.SemaphoreType.DMA((N_HALO,)),
                pltpu.SemaphoreType.DMA((n_sect - 1, N_Z)),
                pltpu.SemaphoreType.DMA((N_Z,)),
                pltpu.SemaphoreType.REGULAR((7,)),
            ],
            compiler_params=pltpu.CompilerParams(collective_id=0, has_side_effects=True),
        )(fields.reshape(NT * 8, 128), levels)
        return result.reshape(1, NF, K, 8, 128)

    return jax.shard_map(
        on_device,
        mesh=mesh,
        in_specs=(P("sect", None, None, "lat", "lon"), P("lat", "lon")),
        out_specs=P("sect", None, None, "lat", "lon"),
        check_vma=False,
    )
```

```python
import functools

import jax
import jax.numpy as jnp
from jax import lax
from jax.experimental import pallas as pl
from jax.experimental.pallas import tpu as pltpu
from jax.sharding import PartitionSpec as P

MESH = pl.DeviceIdType.MESH
F32 = jnp.float32
K = 16
NF = 6
NT = NF * K
SUB = 0.5
N_ROW = NT + 8

(R_COL_W, R_COL_E, R_NEAR_S, R_NEAR_N, R_FAR_S, R_FAR_N, R_CORNER_S, R_CORNER_N, R_FLOW_S, R_FLOW_N) = (*range(8), 8, 10)
N_HALO = 12
CH = 4
NC = K // CH
Z_COL, Z_DIFF = 2 * NC, 2 * NC + 1
N_Z = 2 * NC + 3
DEPTH = 4
VIA_FIRST = 2
VIA_SECOND = 3
(E, W, N, S, FIRST, SECOND, GO) = range(7)
MID = 2


def tile(t):
    return pl.ds(pl.multiple_of(t * 8, 8), 8)


def lroll(x, amount):
    return pltpu.roll(x, amount, 1)


def sroll(x, amount):
    return pltpu.roll(x, amount, 0)


def face(level, limit, speed):
    return jnp.where(level < limit, speed, 0.0)


def coefficients(fe, fw, fn, fs):
    ce = -SUB * jnp.minimum(fe, 0.0)
    cw = SUB * jnp.maximum(fw, 0.0)
    cn = -SUB * jnp.minimum(fn, 0.0)
    cs = SUB * jnp.maximum(fs, 0.0)
    out = (jnp.maximum(fe, 0.0) - jnp.minimum(fw, 0.0)) + (jnp.maximum(fn, 0.0) - jnp.minimum(fs, 0.0))
    return 1.0 - SUB * out, ce, cw, cn, cs


def combine(c, q, qe, qw, qn, qs):
    c0, ce, cw, cn, cs = c
    return (c0 * q + (ce * qe + cw * qw)) + (cn * qn + cs * qs)


def kernel(n_sect, n_lon, n_lat, x_hbm, lev_hbm, out,
           x, lev_ref, cols, cols_w, cols_e, rows_out, rows, near, far, corner_s, corner_n,
           zm, flow_rows, flow_rows_out, flow_cols, flow_cols_out, diff, rhs, div, ratio, ring_cols, ring_rows, shifted, turned,
           in_sem, send_sem, recv_sem, zsend_sem, zrecv_sem, ready):
    sect = lax.axis_index("sect")
    lon = lax.axis_index("lon")
    lat = lax.axis_index("lat")
    east = lax.rem(lon + 1, n_lon)
    west = lax.rem(lon + n_lon - 1, n_lon)
    has_s = lat > 0
    has_n = lat < n_lat - 1

    place = lax.rem(lon // 2, DEPTH)
    to_first, to_second = place < VIA_SECOND, place >= VIA_FIRST
    onward = (sect == 1) & jnp.logical_not(to_second)
    back = (sect == 2) & jnp.logical_not(to_first)
    passes_on = onward | back
    paired = jnp.logical_not(to_first & to_second)

    run, half = 2 * DEPTH, n_lat // 2
    end, head = lax.rem(lon, run) == run - 1, lax.rem(lon, run) == 0
    to = ({"lon": east}, {"lon": west}, {"lat": lat + 1}, {"lat": lat - 1}, {"sect": 1}, {"sect": 2})
    announces = (jnp.logical_not(end), head, has_n & ((lat < half) | (lat == n_lat - 2)), has_s & ((lat > half) | (lat == 1)),
                 (sect == 0) & to_first, ((sect == 0) & to_second) | ((sect == 1) & paired))
    hears = (end, jnp.logical_not(head), has_n & ((lat >= half) | (lat == 0)), has_s & ((lat <= half) | (lat == n_lat - 1)))
    hears_sect = ((sect == 1) & to_first, (sect == 2) & to_second, (sect == 2) & paired)

    def signal(sem, where):
        pl.semaphore_signal(sem, inc=1, device_id=where, device_id_type=MESH)

    mid = (sect == 0) & (place == MID)
    held = (sect == 0) & (place != MID)

    barrier = pltpu.get_barrier_semaphore()

    @pl.when(held)
    def _():
        signal(barrier, {"lon": lon + 2 * (MID - place)})

    for side in range(6):
        @pl.when(announces[side])
        def _(side=side):
            signal(barrier, to[side])

    load = pltpu.make_async_copy(x_hbm, x, in_sem.at[0])
    load.start()
    load_lev = pltpu.make_async_copy(lev_hbm, lev_ref, in_sem.at[1])
    load_lev.start()

    lane = lax.broadcasted_iota(jnp.int32, (8, 128), 1)
    row = lax.broadcasted_iota(jnp.int32, (8, 128), 0)
    even = (lane & 1) == 0
    pair = 63 - (lane >> 1)
    pair_b = 63 - (jnp.where(even, (lane + 126) >> 1, (lane + 1) >> 1) & 63)
    first_lane, last_lane = lane == 0, lane == 127
    first_row, last_row = row == 0, row == 7
    zero = jnp.zeros((8, 128), F32)

    def bcast(value):
        return jnp.broadcast_to(value, (8, 128))

    pl.semaphore_wait(barrier, sum(heard.astype(jnp.int32) for heard in hears + hears_sect) + jnp.where(mid, DEPTH - 1, 0))
    for heard, slot, lower in ((hears_sect[0], FIRST, 0), (hears_sect[1], SECOND, 0),
                               ((sect == 2) & jnp.logical_not(to_second), SECOND, 1)):
        @pl.when(heard)
        def _(slot=slot, lower=lower):
            signal(ready.at[slot], {"sect": lower})

    for side, slot in ((E, W), (W, E), (N, S), (S, N)):
        @pl.when(hears[side])
        def _(side=side, slot=slot):
            signal(ready.at[slot], to[side])

    def await_ready(side, only=True):
        @pl.when(announces[side] & only)
        def _():
            pl.semaphore_wait(ready.at[side], 1)

    @pl.when(jnp.logical_not(has_s))
    def _():
        rows[0] = jnp.zeros((N_ROW, 128), F32)
        rows[2] = jnp.zeros((N_ROW, 128), F32)
        corner_s[...] = jnp.zeros((16, 128), F32)
        flow_rows[:, 0:24, :] = jnp.zeros((2, 24, 128), F32)

    @pl.when(jnp.logical_not(has_n))
    def _():
        rows[1] = jnp.zeros((N_ROW, 128), F32)
        rows[3] = jnp.zeros((N_ROW, 128), F32)
        corner_n[...] = jnp.zeros((16, 128), F32)
        flow_rows[:, 24:40, :] = jnp.zeros((2, 16, 128), F32)

    load_lev.wait()
    load.wait()
    lev = lev_ref[...].astype(F32)

    def pack(acc, value, turn, p):
        a, b = acc
        turned = lroll(value, turn)
        return jnp.where(pair == p, turned, a), jnp.where(pair_b == p, turned, b)

    def pack_level(k, carry):
        a0, a1, b0, b1 = carry
        for f in range(NF):
            p = (f % 4) * K + k
            value = x[tile(f * K + k), :]
            if f < 4:
                a0, b0 = pack((a0, b0), value, 127 - 2 * p, p)
            else:
                a1, b1 = pack((a1, b1), value, 127 - 2 * p, p)
        return a0, a1, b0, b1

    a0, a1, b0, b1 = lax.fori_loop(0, K, pack_level, (zero,) * 4, unroll=4)
    a1, b1 = pack((a1, b1), lev, 63, 32)
    for i, value in enumerate((a0, a1, b0, b1)):
        cols[i * 8:i * 8 + 8, :] = value

    def pack_rows(u, carry):
        for i, r in enumerate((7, 0, 6, 1)):
            rows_out[i, tile(u), :] = x[pl.ds(u * 64 + r, 8, stride=8), :]
        return carry

    lax.fori_loop(0, NT // 8, pack_rows, 0, unroll=4)
    for i, r in enumerate((7, 0, 6, 1)):
        rows_out[i, NT:NT + 8, :] = bcast(lev[r:r + 1, :])

    def remote(src, dst, send, recv, to):
        return pltpu.make_async_remote_copy(src_ref=src, dst_ref=dst, send_sem=send, recv_sem=recv, device_id=to,
                                            device_id_type=MESH)

    def halo(src, dst, slot, to):
        return remote(src, dst, send_sem.at[slot], recv_sem.at[slot], to)

    south, north = {"lat": lat - 1}, {"lat": lat + 1}
    from_w = halo(cols, cols_w, R_COL_W, {"lon": east})
    from_e = halo(cols, cols_e, R_COL_E, {"lon": west})
    near_s = halo(rows_out.at[0], rows.at[0], R_NEAR_S, north)
    near_n = halo(rows_out.at[1], rows.at[1], R_NEAR_N, south)
    far_s = halo(rows_out.at[2], rows.at[2], R_FAR_S, north)
    far_n = halo(rows_out.at[3], rows.at[3], R_FAR_N, south)
    edge_s = halo(near, corner_s, R_CORNER_S, north)
    edge_n = halo(near, corner_n, R_CORNER_N, south)

    def flow_s(octet):
        return halo(flow_rows_out.at[octet, 0:24], flow_rows.at[octet, 0:24], R_FLOW_S + octet, north)

    def flow_n(octet):
        return halo(flow_rows_out.at[octet, 24:40], flow_rows.at[octet, 24:40], R_FLOW_N + octet, south)

    def across(src, dst, slot, peer):
        return remote(src, dst, zsend_sem.at[slot], zrecv_sem.at[slot], {"sect": peer})

    def rows_of(ref, start, size):
        return ref.at[pl.ds(pl.multiple_of(start * 8, 8), size * 8)]

    peer = 3 - sect

    def chunk(field, c, target, relayed=False):
        part = field * K + c * CH
        slot = field * NC + c
        src = rows_of(zm if relayed else x, part, CH)
        return remote(src, rows_of(zm, part, CH), zsend_sem.at[0 if relayed else target - 1, slot], zrecv_sem.at[slot],
                      {"sect": target})

    def send_cols(target, relayed=False):
        return remote(flow_cols if relayed else flow_cols_out, flow_cols, zsend_sem.at[0 if relayed else target - 1, Z_COL],
                      zrecv_sem.at[Z_COL], {"sect": target})

    def send_half(half, target, relayed=False):
        part = diff.at[8:K * 4] if half else diff.at[K * 4:K * 8]
        return remote(part, part, zsend_sem.at[0 if relayed else target - 1, Z_DIFF + half], zrecv_sem.at[Z_DIFF + half], {"sect": target})

    def to_tracers(act, targets, *copies):
        for target in targets:
            @pl.when((to_first, to_second)[target - 1])
            def _(target=target):
                for make in copies:
                    act(make(target))

    def start(copy):
        copy.start()

    def wait_send(copy):
        copy.wait_send()

    halves = [functools.partial(send_half, half) for half in range(2)]
    chunks = [functools.partial(chunk, field, c) for c in range(NC) for field in range(2)]

    await_ready(E)
    from_w.start()
    await_ready(W)
    from_e.start()
    await_ready(N)
    await_ready(S)

    @pl.when(has_n)
    def _():
        near_s.start()

    @pl.when(has_s)
    def _():
        near_n.start()

    @pl.when(sect == 0)
    def _():
        await_ready(FIRST)
        to_tracers(start, (1,), *chunks)

    @pl.when(has_n & (sect != 0))
    def _():
        far_s.start()

    @pl.when(has_s & (sect != 0))
    def _():
        far_n.start()

    @pl.when(sect != 0)
    def _():
        diff[0:8, :] = zero

    await_ready(SECOND, onward)

    @pl.when(back)
    def _():
        send_cols(peer, True).wait_recv()
        send_cols(peer, True).start()

    @pl.when(passes_on)
    def _():
        for make in chunks:
            make(peer, True).wait_recv()
            make(peer, True).start()

    from_w.wait_recv()
    from_e.wait_recv()
    for v in range(2):
        a, b = slice(v * 8, v * 8 + 8), slice(16 + v * 8, 24 + v * 8)
        near[a, :] = jnp.where(even, lroll(cols_e[a, :], 127), lroll(cols_w[a, :], 1))
        far[a, :] = jnp.where(even, lroll(cols_e[b, :], 126), lroll(cols_w[b, :], 2))

    @pl.when(has_n)
    def _():
        edge_s.start()

    @pl.when(has_s)
    def _():
        edge_n.start()

    @pl.when(has_s)
    def _():
        near_s.wait_recv()

    @pl.when(has_n)
    def _():
        near_n.wait_recv()

    def neighbours(q, f, k, columns, south_ref, north_ref):
        v = (f // 4) * 8
        p = (f % 4) * K + k
        side = lroll(columns[v:v + 8, :], 2 * p + 1)
        return (
            jnp.where(last_lane, side, lroll(q, 127)),
            jnp.where(first_lane, side, lroll(q, 1)),
            jnp.where(last_row, bcast(north_ref[pl.ds(f * K + k, 1), :]), sroll(q, 7)),
            jnp.where(first_row, bcast(south_ref[pl.ds(f * K + k, 1), :]), sroll(q, 1)),
        )

    side = lroll(near[8:16, :], 65)
    lev_e = jnp.where(last_lane, side, lroll(lev, 127))
    lev_w = jnp.where(first_lane, side, lroll(lev, 1))
    lev_n = jnp.where(last_row, rows[1, NT:NT + 8, :], sroll(lev, 7))
    lev_s = jnp.where(first_row, rows[0, NT:NT + 8, :], sroll(lev, 1))
    lim_e, lim_w = jnp.minimum(lev, lev_e), jnp.minimum(lev, lev_w)
    lim_n, lim_s = jnp.minimum(lev, lev_n), jnp.minimum(lev, lev_s)

    @pl.when(sect == 0)
    def _():
        def around(f, k):
            q = x[tile(f * K + k), :]
            return q, neighbours(q, f, k, near, rows.at[0], rows.at[1])

        def conductances(k, level):
            v, (ve, vw, vn, vs) = around(4, k)
            return (face(level, lim_e, 0.5 * (v + ve)), face(level, lim_w, 0.5 * (vw + v)),
                    face(level, lim_n, 0.5 * (v + vn)), face(level, lim_s, 0.5 * (vs + v)))

        def diffuse(c, q, sides):
            ce, cw, cn, cs = c
            qe, qw, qn, qs = sides
            return ce * (qe - q) - cw * (q - qw) + cn * (qn - q) - cs * (q - qs)

        def warm(k, above):
            level = lax.convert_element_type(k, F32)
            c = conductances(k, level)
            t, sides = around(2, k)
            new = t + diffuse(c, t, sides)
            out[tile(2 * K + k), :] = new
            jump = 0.2 * (above - new)
            wet = jnp.where((level < lev) & (k > 0), x[tile(5 * K + k), :], 0.0)
            mixing = wet * (1.0 + 4.0 / (1.0 + jump * jump))
            out[tile(5 * K + k), :] = mixing
            diff[tile(k), :] = mixing
            return new

        lax.fori_loop(0, K, warm, zero, unroll=4)

        @pl.when(has_s)
        def _():
            edge_s.wait_recv()

        @pl.when(has_n)
        def _():
            edge_n.wait_recv()

        flow_cols_out[0:8, :] = jnp.where(
            lane >= 64, near[0:8, :], jnp.where(lane >= 32, lroll(far[0:8, :], 64), lroll(cols[0:8, :], 32)))
        flow_cols_out[8:16, :] = jnp.where(first_row, corner_n[0:8, :], corner_s[0:8, :])
        to_tracers(start, (1,), send_cols)
        await_ready(SECOND)
        to_tracers(start, (2,), send_cols, *chunks)

        def move(k, sums):
            level = lax.convert_element_type(k, F32)
            c = conductances(k, level)
            z, zs = around(0, k)
            m, ms = around(1, k)
            t, ts = around(2, k)
            s, ss = around(3, k)
            out[tile(3 * K + k), :] = s + diffuse(c, s, ss)
            here, at_e, at_n = sums

            def add(total, limit, sal, tem):
                return total + jnp.where(level < limit, 0.15 * sal - 0.2 * tem, 0.0)

            here = add(here, lev, s, t)
            at_e = add(at_e, lev_e, ss[0], ts[0])
            at_n = add(at_n, lev_n, ss[2], ts[2])
            new_z = z + (diffuse(c, z, zs) + 0.3 * m - 0.05 * (at_e - here))
            new_m = m + (diffuse(c, m, ms) - 0.3 * z - 0.05 * (at_n - here))
            out[tile(k), :] = face(level, lim_e, new_z)
            out[tile(K + k), :] = face(level, lim_n, new_m)
            div[tile(k), :] = (face(level, lim_e, z) - face(level, lim_w, zs[1])) + (
                face(level, lim_n, m) - face(level, lim_s, ms[3]))
            return here, at_e, at_n

        lax.fori_loop(0, K, move, (zero,) * 3, unroll=2)

        def rise(i, total):
            k = K - 1 - i
            total = total + div[tile(k), :]
            out[tile(4 * K + k), :] = jnp.where(k > 0, -total, 0.0)
            return total

        lax.fori_loop(0, K, rise, zero, unroll=4)

        @pl.when(mid)
        def _():
            for target, others in ((1, range(MID)), (2, range(MID + 1, DEPTH))):
                for make in chunks:
                    make(target).wait_send()
                for other in others:
                    signal(ready.at[GO], {"lon": lon + 2 * (other - MID)})

        pl.semaphore_wait(ready.at[GO], 1)
        to_tracers(start, (1, 2), *halves)

        @pl.when(place == 0)
        def _():
            halves[0](1).wait_send()
            signal(ready.at[GO], {"lon": lon + 2 * MID})
            halves[1](1).wait_send()

    @pl.when(sect != 0)
    def _():
        def corner_of(value, at, p):
            return pltpu.roll(bcast(value[at:at + 1, :]), 2 * p + 1, 1, stride=2, stride_axis=0)

        def turn(value, corner):
            return jnp.where(last_lane, corner, lroll(value, 127)), jnp.where(first_lane, corner, lroll(value, 1))

        def shift(k, carry):
            for f in range(NF):
                q = x[tile(f * K + k), :]
                for i, value in enumerate(neighbours(q, f, k, near, rows.at[0], rows.at[1])):
                    shifted[i, tile(f * K + k), :] = value
            return carry

        lax.fori_loop(0, K, shift, 0, unroll=2)

        def turn_rows():
            @pl.when(has_s)
            def _():
                far_s.wait_recv()
                edge_s.wait_recv()

            @pl.when(has_n)
            def _():
                far_n.wait_recv()
                edge_n.wait_recv()

            for north_side in range(2):
                corner = corner_n if north_side else corner_s
                for u in range(NT // 8):
                    v, p, a = u // 8, (u * 8) % 64, slice(u * 8, u * 8 + 8)
                    qe, qw = turn(rows[north_side, a, :], corner_of(corner[v * 8:v * 8 + 8, :], 0 if north_side else 7, p))
                    turned[north_side, 0, a, :] = qe
                    turned[north_side, 1, a, :] = qw

        @pl.when(jnp.logical_not(passes_on))
        def _():
            turn_rows()

        def share_rows(octet):
            @pl.when(jnp.logical_not(passes_on))
            def _():
                for make in chunks[octet * NC:(octet + 1) * NC]:
                    make(1).wait_recv()

            for i, (field, r) in enumerate(((0, 7), (1, 7), (1, 6), (0, 0), (1, 0))):
                flow_rows_out[octet, i * 8:i * 8 + 8, :] = zm[pl.ds((field * K + octet * 8) * 8 + r, 8, stride=8), :]

            @pl.when(has_n)
            def _():
                flow_s(octet).start()

            @pl.when(has_s)
            def _():
                flow_n(octet).start()

        share_rows(0)
        share_rows(1)
        @pl.when(passes_on)
        def _():
            turn_rows()

        @pl.when(jnp.logical_not(back))
        def _():
            send_cols(1).wait_recv()

        @pl.when(onward)
        def _():
            send_cols(peer, True).start()

        @pl.when(back)
        def _():
            for make in halves:
                make(peer, True).wait_recv()
                make(peer, True).start()


        p1_lev = jnp.where(even, bcast(near[8:16, 62:63]), bcast(near[8:16, 63:64]))
        p2_lev = jnp.where(even, bcast(far[8:16, 62:63]), bcast(far[8:16, 63:64]))
        p0_lev = jnp.where(even, bcast(cols[8:16, 62:63]), bcast(cols[8:16, 63:64]))
        cs_lev = jnp.where(even, bcast(corner_s[8:16, 62:63]), bcast(corner_s[8:16, 63:64]))
        cn_lev = jnp.where(even, bcast(corner_n[8:16, 62:63]), bcast(corner_n[8:16, 63:64]))

        def up_one(value, beyond):
            return jnp.where(last_row, sroll(beyond, 7), sroll(value, 7))

        def down_one(value, beyond):
            return jnp.where(first_row, sroll(beyond, 1), sroll(value, 1))

        def repeat(value, offset):
            if offset:
                value = lroll(value, offset)
            value = jnp.where(lane >= 96, value, 0.0)
            value = value + lroll(value, 32)
            return value + lroll(value, 64)

        p1_z, p1_m, p2_z, p0_z = (repeat(flow_cols[0:8, :], offset) for offset in (0, 32, 64, 96))
        corner_m = repeat(flow_cols[8:16, :], 32)
        k_lane = (pair & (K - 1)).astype(F32)
        lim = functools.partial(jnp.minimum, p1_lev)
        c = coefficients(
            face(k_lane, lim(jnp.where(even, p2_lev, p0_lev)), p1_z),
            face(k_lane, lim(jnp.where(even, p0_lev, p2_lev)), jnp.where(even, p0_z, p2_z)),
            face(k_lane, lim(up_one(p1_lev, cn_lev)), p1_m),
            face(k_lane, lim(down_one(p1_lev, cs_lev)), down_one(p1_m, corner_m)),
        )
        for v in range(2):
            a = slice(v * 8, v * 8 + 8)
            p0, p1, p2 = cols[a, :], near[a, :], far[a, :]
            ring_cols[a, :] = combine(c, p1, jnp.where(even, p2, p0), jnp.where(even, p0, p2),
                                      up_one(p1, corner_n[a, :]), down_one(p1, corner_s[a, :]))

        def ring_of(north_side, octet):
            at = 0 if north_side else 7
            corner = corner_n if north_side else corner_s
            base = 24 if north_side else 0
            r_lev = rows[north_side, NT:NT + 8, :]
            r_in = rows_out[1 - north_side, NT:NT + 8, :]
            r_out = rows[2 + north_side, NT:NT + 8, :]
            r_e, r_w = turn(r_lev, lroll(bcast(corner[8 + at:9 + at, :]), 65))
            k_row = (row + 8 * octet).astype(F32)
            z = flow_rows[octet, base:base + 8, :]
            m = flow_rows[octet, base + 8:base + 16, :]
            _, zw = turn(z, corner_of(flow_cols[8:16, :], at, octet * 8))
            lim_in, lim_out = jnp.minimum(r_lev, r_in), jnp.minimum(r_lev, r_out)
            if north_side:
                fn, fs = face(k_row, lim_out, m), face(k_row, lim_in, flow_rows_out[octet, 8:16, :])
            else:
                fn, fs = face(k_row, lim_in, m), face(k_row, lim_out, flow_rows[octet, 16:24, :])
            c = coefficients(face(k_row, jnp.minimum(r_lev, r_e), z), face(k_row, jnp.minimum(r_lev, r_w), zw), fn, fs)
            for f in range(NF):
                a = slice(f * K + octet * 8, f * K + octet * 8 + 8)
                q, inner, outer = rows[north_side, a, :], rows_out[1 - north_side, a, :], rows[2 + north_side, a, :]
                qe, qw = turned[north_side, 0, a, :], turned[north_side, 1, a, :]
                qn, qs = (outer, inner) if north_side else (inner, outer)
                ring_rows[north_side, a, :] = combine(c, q, qe, qw, qn, qs)

        def advance(octet, k, carry):
            level = lax.convert_element_type(k, F32)
            z, m = zm[tile(k), :], zm[tile(K + k), :]
            side = lroll(flow_cols[0:8, :], 2 * k + 1)
            zw = jnp.where(first_lane, side, lroll(z, 1))
            ms = jnp.where(first_row, bcast(flow_rows[octet, pl.ds(k + 8 - octet * 8, 1), :]), sroll(m, 1))
            fe, fw, fn, fs = face(level, lim_e, z), face(level, lim_w, zw), face(level, lim_n, m), face(level, lim_s, ms)
            div[tile(k), :] = (fe - fw) + (fn - fs)
            c = coefficients(fe, fw, fn, fs)
            for f in range(NF):
                q = x[tile(f * K + k), :]
                q = combine(c, q, *(shifted[i, tile(f * K + k), :] for i in range(4)))
                q = combine(c, q, *neighbours(q, f, k, ring_cols, ring_rows.at[0], ring_rows.at[1]))
                rhs[tile(f * K + k), :] = q
            return carry

        for octet in range(2):
            @pl.when(has_s)
            def _(octet=octet):
                flow_s(octet).wait_recv()

            @pl.when(has_n)
            def _(octet=octet):
                flow_n(octet).wait_recv()

            ring_of(0, octet)
            ring_of(1, octet)
            lax.fori_loop(octet * 8, octet * 8 + 8, functools.partial(advance, octet), 0, unroll=4)

        @pl.when(jnp.logical_not(back))
        def _():
            for make in halves:
                make(1).wait_recv()

        @pl.when(onward)
        def _():
            for make in halves:
                make(peer, True).start()


        def eliminate(i, carry):
            total, up_below, down_below, ratio_below, below = carry
            k = K - 1 - i
            total = total + div[tile(k), :]
            kappa = diff[tile(k), :]
            vertical = jnp.where(k > 0, -total, 0.0)
            up = jnp.maximum(vertical, 0.0) + kappa
            down = jnp.minimum(vertical, 0.0) - kappa
            inverse = 1.0 / ((1.0 + (up - down_below)) + up_below * ratio_below)
            here = down * inverse
            ratio[tile(k), :] = here
            values = []
            for f in range(NF):
                value = (rhs[tile(f * K + k), :] + up_below * below[f]) * inverse
                rhs[tile(f * K + k), :] = value
                values.append(value)
            return total, up, down, here, tuple(values)

        lax.fori_loop(0, K, eliminate, (zero,) * 4 + ((zero,) * NF,), unroll=4)

        def settle(k, above):
            level = lax.convert_element_type(k, F32)
            here = ratio[tile(k), :]
            values = []
            for f in range(NF):
                value = rhs[tile(f * K + k), :] - here * above[f]
                out[tile(f * K + k), :] = face(level, lev, value)
                values.append(value)
            return tuple(values)

        lax.fori_loop(0, K, settle, (zero,) * NF, unroll=4)

    from_w.wait_send()
    from_e.wait_send()

    @pl.when(has_n)
    def _():
        near_s.wait_send()
        edge_s.wait_send()

    @pl.when(has_s)
    def _():
        near_n.wait_send()
        edge_n.wait_send()

    @pl.when(has_n & (sect != 0))
    def _():
        for copy in (far_s, flow_s(0), flow_s(1)):
            copy.wait_send()

    @pl.when(has_s & (sect != 0))
    def _():
        for copy in (far_n, flow_n(0), flow_n(1)):
            copy.wait_send()

    @pl.when(sect == 0)
    def _():
        @pl.when(held)
        def _():
            to_tracers(wait_send, (1, 2), *chunks)

        to_tracers(wait_send, (1, 2), send_cols)

        @pl.when(place != 0)
        def _():
            to_tracers(wait_send, (1, 2), *halves)

    @pl.when(passes_on)
    def _():
        for make in (*chunks, send_cols, *halves):
            make(peer, True).wait_send()


def solution(mesh):
    n_sect, n_lon, n_lat = (mesh.shape[a] for a in ("sect", "lon", "lat"))

    def on_device(fields, levels):
        vmem = pltpu.VMEM
        result = pl.pallas_call(
            functools.partial(kernel, n_sect, n_lon, n_lat),
            out_shape=pltpu.VMEM((NT * 8, 128), F32),
            in_specs=[pl.BlockSpec(memory_space=pl.ANY)] * 2,
            out_specs=pl.BlockSpec(memory_space=pltpu.VMEM),
            scratch_shapes=[
                vmem((NT * 8, 128), F32),
                vmem((8, 128), jnp.int32),
                vmem((32, 128), F32),
                vmem((32, 128), F32),
                vmem((32, 128), F32),
                vmem((4, N_ROW, 128), F32),
                vmem((4, N_ROW, 128), F32),
                vmem((16, 128), F32),
                vmem((16, 128), F32),
                vmem((16, 128), F32),
                vmem((16, 128), F32),
                vmem((2 * K * 8, 128), F32),
                vmem((2, 40, 128), F32),
                vmem((2, 40, 128), F32),
                vmem((16, 128), F32),
                vmem((16, 128), F32),
                vmem((K * 8, 128), F32),
                vmem((NT * 8, 128), F32),
                vmem((K * 8, 128), F32),
                vmem((K * 8, 128), F32),
                vmem((16, 128), F32),
                vmem((2, NT, 128), F32),
                vmem((4, NT * 8, 128), F32),
                vmem((2, 2, NT, 128), F32),
                pltpu.SemaphoreType.DMA((2,)),
                pltpu.SemaphoreType.DMA((N_HALO,)),
                pltpu.SemaphoreType.DMA((N_HALO,)),
                pltpu.SemaphoreType.DMA((n_sect - 1, N_Z)),
                pltpu.SemaphoreType.DMA((N_Z,)),
                pltpu.SemaphoreType.REGULAR((7,)),
            ],
            compiler_params=pltpu.CompilerParams(collective_id=0, has_side_effects=True),
        )(fields.reshape(NT * 8, 128), levels)
        return result.reshape(1, NF, K, 8, 128)

    return jax.shard_map(
        on_device,
        mesh=mesh,
        in_specs=(P("sect", None, None, "lat", "lon"), P("lat", "lon")),
        out_specs=P("sect", None, None, "lat", "lon"),
        check_vma=False,
    )
```
